32 devices in a mesh: dp: 8 (over z, x), tensor: 4 (over y, core).
Axes of the slice: x: 2, y: 2, z: 4, core: 2. Of those that a mesh axis runs over, the one named last changes fastest.
Arguments:
- block_input: bfloat16 [8, 512, 2048], P('dp'), may hold values from -6 to 6
- out_grad: bfloat16 [8, 512, 2048], P('dp'), may hold values from -6 to 6
- seg_ids: int32 [8, 512], P('dp'), may hold values from 0 to 5, never falling along the last dimension, each value on 1 to 400 neighbouring positions
- slot_live: int32 [8], P('dp'), may hold values 0 or 1
- norm_gain: float32 [2048], replicated, may hold values from 0.5 to 1.5
- z_weight: float32 [2048, 4096], P('dp', 'tensor'), may hold values from -0.125 to 0.125
- x_weight: float32 [2048, 4096], P('dp', 'tensor'), may hold values from -0.125 to 0.125
- bc_weight: float32 [2048, 256], P('dp'), may hold values from -0.125 to 0.125
- dt_weight: float32 [2048, 64], P('dp', 'tensor'), may hold values from -0.125 to 0.125
- conv_x: float32 [4, 4096], P(None, 'tensor'), may hold values from -3 to 3
- conv_bc: float32 [4, 256], replicated, may hold values from -3 to 3
- head_params: float32 [3, 64], P(None, 'tensor'), may hold values from -5 to 3, as said below
- gated_gain: float32 [4096], P('tensor'), may hold values from 0.5 to 1.5
- out_weight: float32 [2048, 4096], P('dp', 'tensor'), may hold values from -0.09375 to 0.09375
- norm_gain_sq: float32 [2048], replicated, may hold values from 64 to 1024
- z_rows: float32 [2048], P('dp'), may hold values from 32 to 8192, as said below
- z_cols: float32 [4096], P('tensor'), may hold values from 64 to 1024
- x_rows: float32 [2048], P('dp'), may hold values from 32 to 8192, as said below
- x_cols: float32 [4096], P('tensor'), may hold values from 64 to 1024
- bc_rows: float32 [2048], P('dp'), may hold values from 32 to 8192, as said below
- bc_cols: float32 [256], replicated, may hold values from 64 to 1024
- dt_rows: float32 [2048], P('dp'), may hold values from 32 to 8192, as said below
- dt_cols: float32 [64], P('tensor'), may hold values from 64 to 1024
- conv_x_sq: float32 [4, 4096], P(None, 'tensor'), may hold values from 64 to 1024
- conv_bc_sq: float32 [4, 256], replicated, may hold values from 64 to 1024
- head_sq: float32 [3, 64], P(None, 'tensor'), may hold values from 64 to 1024
- gated_gain_sq: float32 [4096], P('tensor'), may hold values from 64 to 1024
- out_rows: float32 [2048], P('dp'), may hold values from 32 to 8192, as said below
- out_cols: float32 [4096], P('tensor'), may hold values from 64 to 1024
Outputs:
- output: bfloat16 [8, 512, 2048], P('dp')
- input_grad: bfloat16 [8, 512, 2048], P('dp')
- norm_gain_grad: float32 [2048], replicated
- norm_gain_update: float32 [2048], replicated
- norm_gain_sq_new: float32 [2048], replicated
- z_grad: float32 [2048, 4096], P('dp', 'tensor')
- z_update: float32 [2048, 4096], P('dp', 'tensor')
- z_rows_new: float32 [2048], P('dp')
- z_cols_new: float32 [4096], P('tensor')
- x_grad: float32 [2048, 4096], P('dp', 'tensor')
- x_update: float32 [2048, 4096], P('dp', 'tensor')
- x_rows_new: float32 [2048], P('dp')
- x_cols_new: float32 [4096], P('tensor')
- bc_grad: float32 [2048, 256], P('dp')
- bc_update: float32 [2048, 256], P('dp')
- bc_rows_new: float32 [2048], P('dp')
- bc_cols_new: float32 [256], replicated
- dt_grad: float32 [2048, 64], P('dp', 'tensor')
- dt_update: float32 [2048, 64], P('dp', 'tensor')
- dt_rows_new: float32 [2048], P('dp')
- dt_cols_new: float32 [64], P('tensor')
- conv_x_grad: float32 [4, 4096], P(None, 'tensor')
- conv_x_update: float32 [4, 4096], P(None, 'tensor')
- conv_x_sq_new: float32 [4, 4096], P(None, 'tensor')
- conv_bc_grad: float32 [4, 256], replicated
- conv_bc_update: float32 [4, 256], replicated
- conv_bc_sq_new: float32 [4, 256], replicated
- head_grad: float32 [3, 64], P(None, 'tensor')
- head_update: float32 [3, 64], P(None, 'tensor')
- head_sq_new: float32 [3, 64], P(None, 'tensor')
- gated_gain_grad: float32 [4096], P('tensor')
- gated_gain_update: float32 [4096], P('tensor')
- gated_gain_sq_new: float32 [4096], P('tensor')
- out_grad_w: float32 [2048, 4096], P('dp', 'tensor')
- out_update: float32 [2048, 4096], P('dp', 'tensor')
- out_rows_new: float32 [2048], P('dp')
- out_cols_new: float32 [4096], P('tensor')
The draws below stay inside these ranges and needn't reach their ends.
Inputs may be any that keep to these rules, and one draw needn't show every extreme that they name: `seg_ids`: in each slot the document numbers never fall and take all 6 values; each document has 1 to 400 tokens, one exactly 400. `head_params`: row 0 holds step size offsets, row 1 logarithms of decay rates, row 2 skip gains. `z_rows`: positive. `x_rows`: positive. `bc_rows`: positive. `dt_rows`: positive. `out_rows`: positive.
All inputs are finite; a program needn't handle non-finite values. No bound on the sum of `slot_live` on one device may be relied on, other than what follows from the above.
Results may differ from the reference program's by a relative error of at most 0.0044.
The reference program's roundings to bfloat16 on the way count: a program that leaves them out, or rounds other values in their place, can miss the bound.
Values may be sent and summed in bfloat16 or wider, within the bound.
No kernel may reach another device: no remote copies, remote signals or barrier semaphores. Data moves between devices by JAX's collectives and lax.ppermute only.
A program may use at most 192 MiB of HBM per device.

```python
import math
import jax
import jax.numpy as jnp
import numpy as np
from jax import lax

D = 2048
HEADS = 64
STATE = 128
INNER = 4096
KCONV = 4
STRETCH = 256
SLOT = 512
DOCS = 6
DOC_MOST = 400
SLOTS = 8
TOKENS = 4096


def draw_head_params(key, part):
    offset_key = jax.random.fold_in(key, 11)
    decay_key = jax.random.fold_in(key, 12)
    skip_key = jax.random.fold_in(key, 13)
    offsets = jax.random.uniform(offset_key, (HEADS,), jnp.float32, -5.0, -1.0)
    log_rates = jax.random.uniform(decay_key, (HEADS,), jnp.float32, 0.0, 2.75)
    skips = jax.random.uniform(skip_key, (HEADS,), jnp.float32, 0.5, 1.5)
    return jnp.stack([offsets, log_rates, skips])


def rising_rows(key, salt):
    places = jnp.arange(D).astype(jnp.float32) / (D - 1)
    rough = jax.random.uniform(jax.random.fold_in(key, salt), (D,), jnp.float32, 0.7, 1.4)
    span = 16.0
    return TOKENS / 64.0 * jnp.exp(places * jnp.log(span)) * rough


def draw_z_rows(key, part):
    return rising_rows(key, 21)


def draw_x_rows(key, part):
    return rising_rows(key, 22)


def draw_bc_rows(key, part):
    return rising_rows(key, 23)


def draw_dt_rows(key, part):
    return rising_rows(key, 24)


def draw_out_rows(key, part):
    return rising_rows(key, 25)


def set_ends(values, own_key, low, top_value):
    dims = values.shape
    place = [jax.random.randint(jax.random.fold_in(own_key, axis), (), 0, dims[axis]) for axis in range(len(dims))]
    values = values.at[tuple(place)].set(low)
    longest = dims.index(max(dims))
    place[longest] = (place[longest] + 1) % dims[longest]
    return values.at[tuple(place)].set(top_value)


def level_of(rng, dims, split, low, top_value):
    level, own = 1.0, jax.random.fold_in(rng, 6)
    for axis_at, parts in split:
        steps = jnp.exp(jax.random.uniform(jax.random.fold_in(own, axis_at), (parts,), jnp.float32, low / len(split), top_value / len(split)))
        level = level * jnp.repeat(steps, dims[axis_at] // parts).reshape([-1 if axis == axis_at else 1 for axis in range(len(dims))])
    return level


def length_profile(number_of, total, reach, lean):
    portions = [(1 << 20) // math.isqrt(rank ** lean) + 1 for rank in range(2, number_of + 1)]
    surplus, holding = total - reach - (number_of - 1), [1] * (number_of - 1)
    while surplus > 0:
        free = [i for i in range(number_of - 1) if holding[i] < reach]
        pool, left = sum([portions[i] for i in free]), surplus
        for i in free:
            extra = min(reach - holding[i], max(1, left * portions[i] // pool), surplus)
            holding[i] = holding[i] + extra
            surplus = surplus - extra
    return np.array([reach] + holding)


def ragged_sizes(stream_key, number_of, total, limit, skew):
    if number_of == 2:
        one = jax.random.randint(stream_key, (), max(1, total - limit), min(limit, total - 1) + 1)
        return jnp.stack([one, total - one])
    tallies = jnp.asarray(length_profile(number_of, total, limit, skew), jnp.int32)
    couples = (number_of - 1) // 2
    source_of, receiver = tallies[1:1 + 2 * couples:2], tallies[2:2 + 2 * couples:2]
    margin = jnp.minimum(source_of - 1, limit - receiver)
    shifted = jax.random.randint(jax.random.fold_in(stream_key, 1), (couples,), 0, 1 << 20) % (margin + 1)
    tallies = tallies.at[1:1 + 2 * couples:2].set(source_of - shifted).at[2:2 + 2 * couples:2].set(receiver + shifted)
    return tallies[jax.random.permutation(jax.random.fold_in(stream_key, 2), number_of)]


def bell_draw(rng, extent, scale, limit, split=(), kind=jnp.bfloat16):
    entries = jax.random.normal(rng, extent, jnp.float32) * scale
    if len(split) > 0:
        entries = level_of(rng, extent, split, -0.22, 0.18) * entries
    return jnp.clip(entries, min=-limit, max=limit).astype(kind)


def setup_inputs(seed: int = 0) -> dict:
    seeds = jax.random.split(jax.random.key(seed), 30)
    return {
        "block_input": bell_draw(seeds[0], (SLOTS, SLOT, D), 1.0, 6.0, ((0, 8),)),
        "out_grad": bell_draw(seeds[1], (SLOTS, SLOT, D), 1.0, 6.0, ((0, 8),)),
        "seg_ids": jax.vmap(lambda own: jnp.searchsorted(jnp.cumsum(ragged_sizes(own, DOCS, SLOT, DOC_MOST, 1)), jnp.arange(SLOT), side="right"))(jax.random.split(seeds[2], SLOTS)).reshape((SLOTS, SLOT)).astype(jnp.int32),
        "slot_live": set_ends((jax.random.randint(seeds[3], (SLOTS,), 0, 32) < 29).astype(jnp.int32), jax.random.fold_in(seeds[3], 1), 0, 1),
        "norm_gain": jnp.clip(1.0 + 0.1 * jax.random.normal(seeds[4], (D,), jnp.float32), 0.5, 1.5),
        "z_weight": bell_draw(seeds[5], (D, INNER), D ** -0.5, 0.125, ((0, 8), (1, 4)), jnp.float32),
        "x_weight": bell_draw(seeds[6], (D, INNER), D ** -0.5, 0.125, ((0, 8), (1, 4)), jnp.float32),
        "bc_weight": bell_draw(seeds[7], (D, 2 * STATE), D ** -0.5, 0.125, ((0, 8),), jnp.float32),
        "dt_weight": bell_draw(seeds[8], (D, HEADS), D ** -0.5, 0.125, ((0, 8), (1, 4)), jnp.float32),
        "conv_x": bell_draw(seeds[9], (KCONV, INNER), KCONV ** -0.5, 3.0, ((1, 4),), jnp.float32),
        "conv_bc": bell_draw(seeds[10], (KCONV, 2 * STATE), KCONV ** -0.5, 3.0, (), jnp.float32),
        "head_params": draw_head_params(jax.random.fold_in(seeds[29], 71), 0),
        "gated_gain": jnp.clip(1.0 + 0.1 * jax.random.normal(seeds[12], (INNER,), jnp.float32), 0.5, 1.5),
        "out_weight": bell_draw(seeds[13], (D, INNER), INNER ** -0.5, 0.09375, ((0, 8), (1, 4)), jnp.float32),
        "norm_gain_sq": jnp.clip(jnp.exp(jax.random.uniform(seeds[14], (D,), jnp.float32, math.log(64.0), math.log(1024.0))), 64.0, 1024.0),
        "z_rows": draw_z_rows(jax.random.fold_in(seeds[29], 71), 0),
        "z_cols": jnp.clip(jnp.exp(math.log(1024.0) - 2.7725887 * jax.random.uniform(seeds[16], (INNER,), jnp.float32) ** level_of(seeds[16], (INNER,), ((0, 4),), -0.2, 0.2)), 64.0, 1024.0),
        "x_rows": draw_x_rows(jax.random.fold_in(seeds[29], 71), 0),
        "x_cols": jnp.clip(jnp.exp(math.log(1024.0) - 2.7725887 * jax.random.uniform(seeds[18], (INNER,), jnp.float32) ** level_of(seeds[18], (INNER,), ((0, 4),), -0.2, 0.2)), 64.0, 1024.0),
        "bc_rows": draw_bc_rows(jax.random.fold_in(seeds[29], 71), 0),
        "bc_cols": jnp.clip(jnp.exp(jax.random.uniform(seeds[20], (2 * STATE,), jnp.float32, math.log(64.0), math.log(1024.0))), 64.0, 1024.0),
        "dt_rows": draw_dt_rows(jax.random.fold_in(seeds[29], 71), 0),
        "dt_cols": jnp.clip(jnp.exp(math.log(1024.0) - 2.7725887 * jax.random.uniform(seeds[22], (HEADS,), jnp.float32) ** level_of(seeds[22], (HEADS,), ((0, 4),), -0.2, 0.2)), 64.0, 1024.0),
        "conv_x_sq": jnp.clip(jnp.exp(math.log(1024.0) - 2.7725887 * jax.random.uniform(seeds[23], (KCONV, INNER), jnp.float32) ** level_of(seeds[23], (KCONV, INNER), ((1, 4),), -0.2, 0.2)), 64.0, 1024.0),
        "conv_bc_sq": jnp.clip(jnp.exp(jax.random.uniform(seeds[24], (KCONV, 2 * STATE), jnp.float32, math.log(64.0), math.log(1024.0))), 64.0, 1024.0),
        "head_sq": jnp.clip(jnp.exp(math.log(1024.0) - 2.7725887 * jax.random.uniform(seeds[25], (3, HEADS), jnp.float32) ** level_of(seeds[25], (3, HEADS), ((1, 4),), -0.2, 0.2)), 64.0, 1024.0),
        "gated_gain_sq": jnp.clip(jnp.exp(math.log(1024.0) - 2.7725887 * jax.random.uniform(seeds[26], (INNER,), jnp.float32) ** level_of(seeds[26], (INNER,), ((0, 4),), -0.2, 0.2)), 64.0, 1024.0),
        "out_rows": draw_out_rows(jax.random.fold_in(seeds[29], 71), 0),
        "out_cols": jnp.clip(jnp.exp(math.log(1024.0) - 2.7725887 * jax.random.uniform(seeds[28], (INNER,), jnp.float32) ** level_of(seeds[28], (INNER,), ((0, 4),), -0.2, 0.2)), 64.0, 1024.0),
    }


HIGHEST = lax.Precision.HIGHEST
norm_eps = 1e-05
decay_rate = 0.5
tiny_eps = 1e-30
unit_eps = 1e-06
vector_rate = 0.05

@jax.custom_vjp
def low(v):
    return lax.optimization_barrier(v.astype(jnp.bfloat16)).astype(jnp.float32)

@jax.custom_vjp
def low_back(v):
    return v

def low_keep(v):
    return (low(v), None)

def low_pass(kept, grad):
    return (grad,)

def back_keep(v):
    return (v, None)

def back_low(kept, grad):
    return (low(grad),)
low.defvjp(low_keep, low_pass)
low_back.defvjp(back_keep, back_low)

def shift_down(values, offset):
    padding = jnp.zeros((offset,) + values.shape[1:], values.dtype)
    return jnp.concatenate([padding, values[:-offset]], axis=0)

def causal_conv(values, taps, segment):
    result = taps[0] * values
    for offset in range(1, taps.shape[0]):
        same_doc = jnp.concatenate([jnp.zeros((offset,), jnp.bool_), segment[offset:] == segment[:-offset]])
        result = result + taps[offset] * shift_down(values, offset) * same_doc[:, None].astype(values.dtype)
    return result

def state_scan(heads_x, step_size, decay_coef, b_mat, c_mat, segment):
    length, head_count, head_width = heads_x.shape
    blocks = length // STRETCH

    def by_blocks(values):
        return values.reshape((blocks, STRETCH) + values.shape[1:])

    def advance(carried, block_data):
        memory, prev_doc = carried
        block_x, block_dt, block_b, block_c, block_doc = block_data
        log_decay = jnp.cumsum(block_dt * decay_coef[None, :], axis=0)
        places = jnp.arange(STRETCH)
        visible = (places[:, None] >= places[None, :]) & (block_doc[:, None] == block_doc[None, :])
        visible = visible[:, :, None]
        log_gaps = log_decay[:, None, :] - log_decay[None, :, :]
        kernel = jnp.where(visible, jnp.exp(jnp.where(visible, log_gaps, 0.0)), 0.0)
        intersection = jnp.dot(block_c, block_b.T, precision=HIGHEST)
        mixing = intersection[:, :, None] * kernel * block_dt[None, :, :]
        inside = jnp.einsum('tsh,shp->thp', mixing, block_x, precision=HIGHEST)
        keep_prev = (block_doc == prev_doc).astype(block_x.dtype)
        carry_in = jnp.einsum('tn,hpn->thp', block_c, memory, precision=HIGHEST)
        carry_in = carry_in * (jnp.exp(log_decay) * keep_prev[:, None])[:, :, None]
        last_doc = block_doc[-1]
        tail_weight = jnp.exp(log_decay[-1][None, :] - log_decay) * block_dt
        tail_weight = tail_weight * (block_doc == last_doc).astype(block_x.dtype)[:, None]
        fresh_state = jnp.einsum('sh,shp,sn->hpn', tail_weight, block_x, block_b, precision=HIGHEST)
        kept_share = (jnp.exp(log_decay[-1]) * (last_doc == prev_doc).astype(block_x.dtype))[:, None, None]
        return ((fresh_state + memory * kept_share, last_doc), inside + carry_in)
    initial = (jnp.zeros((head_count, head_width, b_mat.shape[1]), heads_x.dtype), jnp.array(-1, jnp.int32))
    _, outputs = lax.scan(jax.checkpoint(advance), initial, (by_blocks(heads_x), by_blocks(step_size), by_blocks(b_mat), by_blocks(c_mat), by_blocks(segment)))
    return outputs.reshape(heads_x.shape)

def mixer(gate_z, x_raw, bc_raw, dt_raw, conv_x, conv_bc, head_params, gated_gain, segment):
    head_count = dt_raw.shape[1]
    x_conv = jax.nn.silu(causal_conv(x_raw, conv_x, segment))
    bc_conv = jax.nn.silu(causal_conv(bc_raw, conv_bc, segment))
    half_width = bc_conv.shape[1] // 2
    step_size = jax.nn.softplus(dt_raw + head_params[0])
    decay_coef = -jnp.exp(head_params[1])
    heads_x = x_conv.reshape(x_conv.shape[0], head_count, -1)
    scanned = state_scan(heads_x, step_size, decay_coef, bc_conv[:, :half_width], bc_conv[:, half_width:], segment)
    scanned = scanned + head_params[2][None, :, None] * heads_x
    gated_values = scanned.reshape(x_conv.shape) * jax.nn.silu(gate_z)
    return (gated_values * gated_gain, lax.optimization_barrier(jnp.sum(gated_values * gated_values, axis=1)))

def slot_forward(params, block_in, segment):
    norm_gain, z_weight, x_weight, bc_weight, dt_weight, conv_x, conv_bc, head_params, gated_gain, out_weight = params
    mean_square = lax.optimization_barrier(jnp.mean(block_in * block_in, axis=1, keepdims=True))
    normed = low(block_in * lax.rsqrt(mean_square + norm_eps) * norm_gain)
    gate_z = low_back(jnp.dot(normed, low(z_weight), precision=HIGHEST))
    x_raw = low_back(jnp.dot(normed, low(x_weight), precision=HIGHEST))
    bc_raw = low_back(jnp.dot(normed, low(bc_weight), precision=HIGHEST))
    dt_raw = low_back(jnp.dot(normed, low(dt_weight), precision=HIGHEST))
    scaled, squares = mixer(gate_z, x_raw, bc_raw, dt_raw, conv_x, conv_bc, head_params, gated_gain, segment)
    projected = low_back(jnp.dot(low(scaled), low(out_weight).T, precision=HIGHEST))
    return block_in + lax.rsqrt(squares / INNER + norm_eps)[:, None] * projected

def normalized(unit):
    return unit * lax.rsqrt(jnp.mean(unit * unit) + unit_eps)

def factored(grad, rows_old, cols_old, rate):
    squared = grad * grad + tiny_eps
    rows_new = decay_rate * rows_old + (1.0 - decay_rate) * lax.optimization_barrier(jnp.mean(squared, axis=1))
    cols_new = decay_rate * cols_old + (1.0 - decay_rate) * lax.optimization_barrier(jnp.mean(squared, axis=0))
    unit = grad * lax.rsqrt(rows_new[:, None] * cols_new[None, :])
    return (-rate * normalized(unit), rows_new, cols_new)

def unfactored(grad, second_old):
    second = decay_rate * second_old + (1.0 - decay_rate) * (grad * grad + tiny_eps)
    return (-vector_rate * normalized(grad * lax.rsqrt(second)), second)

def reference(block_input, out_grad, seg_ids, slot_live, norm_gain, z_weight, x_weight, bc_weight, dt_weight, conv_x, conv_bc, head_params, gated_gain, out_weight, norm_gain_sq, z_rows, z_cols, x_rows, x_cols, bc_rows, bc_cols, dt_rows, dt_cols, conv_x_sq, conv_bc_sq, head_sq, gated_gain_sq, out_rows, out_cols):
    params = (norm_gain, z_weight, x_weight, bc_weight, dt_weight, conv_x, conv_bc, head_params, gated_gain, out_weight)

    def per_slot(totals, item):
        slot_in, slot_cot, segment, live_flag = item

        def forward(weights, values):
            return slot_forward(weights, values, segment)
        result, pull = jax.vjp(forward, params, slot_in.astype(jnp.float32))
        grads, in_grad = pull(slot_cot.astype(jnp.float32) * live_flag.astype(jnp.float32))
        totals = jax.tree.map(jnp.add, totals, grads)
        return (totals, (result.astype(jnp.bfloat16), in_grad.astype(jnp.bfloat16)))
    zeros = jax.tree.map(jnp.zeros_like, params)
    grads, (output, input_grad) = lax.scan(per_slot, zeros, (block_input, out_grad, seg_ids, slot_live))
    g_norm, g_z, g_x, g_bc, g_dt, g_convx, g_convbc, g_head, g_gated, g_out = grads
    in_rate = D ** (-0.5)
    out_rate = INNER ** (-0.5)
    norm_upd, norm_sq_new = unfactored(g_norm, norm_gain_sq)
    z_upd, z_rows_new, z_cols_new = factored(g_z, z_rows, z_cols, in_rate)
    x_upd, x_rows_new, x_cols_new = factored(g_x, x_rows, x_cols, in_rate)
    bc_upd, bc_rows_new, bc_cols_new = factored(g_bc, bc_rows, bc_cols, in_rate)
    dt_upd, dt_rows_new, dt_cols_new = factored(g_dt, dt_rows, dt_cols, in_rate)
    convx_upd, convx_sq_new = unfactored(g_convx, conv_x_sq)
    convbc_upd, convbc_sq_new = unfactored(g_convbc, conv_bc_sq)
    head_upd, head_sq_new = unfactored(g_head, head_sq)
    gated_upd, gated_sq_new = unfactored(g_gated, gated_gain_sq)
    out_upd, out_rows_new, out_cols_new = factored(g_out, out_rows, out_cols, out_rate)
    return (output, input_grad, g_norm, norm_upd, norm_sq_new, g_z, z_upd, z_rows_new, z_cols_new, g_x, x_upd, x_rows_new, x_cols_new, g_bc, bc_upd, bc_rows_new, bc_cols_new, g_dt, dt_upd, dt_rows_new, dt_cols_new, g_convx, convx_upd, convx_sq_new, g_convbc, convbc_upd, convbc_sq_new, g_head, head_upd, head_sq_new, g_gated, gated_upd, gated_sq_new, g_out, out_upd, out_rows_new, out_cols_new)
```

```python
import jax
import jax.numpy as jnp
from jax import lax
from jax.sharding import PartitionSpec as P

D = 2048
HEADS = 64
STATE = 128
INNER = 4096
KCONV = 4
STRETCH = 256


norm_eps = 1e-05
decay_rate = 0.5
tiny_eps = 1e-30
unit_eps = 1e-06
vector_rate = 0.05


def shift_down(values, offset):
    padding = jnp.zeros((offset,) + values.shape[1:], values.dtype)
    return jnp.concatenate([padding, values[:-offset]], axis=0)


def causal_conv(values, taps, segment):
    result = taps[0] * values
    for offset in range(1, taps.shape[0]):
        same_doc = jnp.concatenate(
            [jnp.zeros((offset,), jnp.bool_), segment[offset:] == segment[:-offset]]
        )
        result = result + taps[offset] * shift_down(values, offset) * same_doc[:, None].astype(
            values.dtype
        )
    return result


def state_scan(heads_x, step_size, decay_coef, b_mat, c_mat, segment):
    length, head_count, head_width = heads_x.shape
    blocks = length // STRETCH
    highest = lax.Precision.HIGHEST
    x_blocks = heads_x.reshape(blocks, STRETCH, head_count, head_width).transpose(0, 2, 3, 1)
    dt_blocks = step_size.reshape(blocks, STRETCH, head_count).transpose(0, 2, 1)
    b_blocks = b_mat.reshape(blocks, STRETCH, -1).transpose(0, 2, 1)
    c_blocks = c_mat.reshape(blocks, STRETCH, -1).transpose(0, 2, 1)
    doc_blocks = segment.reshape(blocks, STRETCH)

    def advance(carried, block_data):
        memory, prev_doc = carried
        block_x, block_dt, block_b, block_c, block_doc = block_data
        log_decay = jnp.cumsum(block_dt * decay_coef[:, None], axis=1)
        places = jnp.arange(STRETCH)
        visible = (places[:, None] >= places[None, :]) & (block_doc[:, None] == block_doc[None, :])
        visible = visible[None, :, :]
        log_gaps = log_decay[:, :, None] - log_decay[:, None, :]
        kernel = jnp.where(visible, jnp.exp(jnp.where(visible, log_gaps, 0.0)), 0.0)
        intersection = jnp.dot(block_c.T, block_b, precision=highest)
        mixing = intersection[None, :, :] * kernel * block_dt[:, None, :]
        inside = jnp.einsum("hts,hps->hpt", mixing, block_x, precision=highest)
        keep_prev = (block_doc == prev_doc).astype(block_x.dtype)
        carry_in = jnp.einsum("nt,hpn->hpt", block_c, memory, precision=highest)
        carry_in = carry_in * (jnp.exp(log_decay) * keep_prev[None, :])[:, None, :]
        last_doc = block_doc[-1]
        tail_weight = jnp.exp(log_decay[:, -1:] - log_decay) * block_dt
        tail_weight = tail_weight * (block_doc == last_doc).astype(block_x.dtype)[None, :]
        fresh_state = jnp.einsum("hs,hps,ns->hpn", tail_weight, block_x, block_b, precision=highest)
        kept_share = (jnp.exp(log_decay[:, -1]) * (last_doc == prev_doc).astype(block_x.dtype))[
            :, None, None
        ]
        return ((fresh_state + memory * kept_share, last_doc), inside + carry_in)

    initial = (
        jnp.zeros((head_count, head_width, b_mat.shape[1]), heads_x.dtype),
        jnp.array(-1, jnp.int32),
    )
    _, outputs = lax.scan(
        jax.checkpoint(advance), initial, (x_blocks, dt_blocks, b_blocks, c_blocks, doc_blocks)
    )
    return outputs.transpose(0, 3, 1, 2).reshape(heads_x.shape)


def mixer(gate_z, x_raw, bc_raw, dt_raw, conv_x, conv_bc, head_params, gated_gain, segment):
    head_count = dt_raw.shape[1]
    x_conv = jax.nn.silu(causal_conv(x_raw, conv_x, segment))
    bc_conv = jax.nn.silu(causal_conv(bc_raw, conv_bc, segment))
    half_width = bc_conv.shape[1] // 2
    step_size = jax.nn.softplus(dt_raw + head_params[0])
    decay_coef = -jnp.exp(head_params[1])
    heads_x = x_conv.reshape(x_conv.shape[0], head_count, -1)
    scanned = state_scan(
        heads_x, step_size, decay_coef, bc_conv[:, :half_width], bc_conv[:, half_width:], segment
    )
    scanned = scanned + head_params[2][None, :, None] * heads_x
    gated_values = scanned.reshape(x_conv.shape) * jax.nn.silu(gate_z)
    return (gated_values * gated_gain, jnp.sum(gated_values * gated_values, axis=1))


def norm_input(values, gain):
    mean_square = jnp.mean(values * values, axis=1, keepdims=True)
    return values * lax.rsqrt(mean_square + norm_eps) * gain


def rows_times(left, right):
    return lax.dot_general(
        left, right, (((1,), (1,)), ((), ())), preferred_element_type=jnp.float32
    )


def tokens_out(left, right):
    return lax.dot_general(
        left, right, (((0,), (0,)), ((), ())), preferred_element_type=jnp.float32
    )


def mix_state(old_state, fresh_term):
    return decay_rate * old_state + (1.0 - decay_rate) * fresh_term


def normalized(unit, square_total, entries):
    return unit * lax.rsqrt(square_total / entries + unit_eps)


def swap(value, axis, bit):
    size = lax.axis_size(axis)
    return lax.ppermute(value, axis, [(place, place ^ bit) for place in range(size)])


def add_over(value, axis, bits):
    for bit in bits:
        value = value + swap(value, axis, bit)
    return value


PAIR = 2


def dp_bits():
    count = lax.axis_size("dp")
    rest = [1 << place for place in reversed(range(count.bit_length() - 1)) if 1 << place != PAIR]
    return [PAIR] + rest


def block_masks():
    bits = dp_bits()
    return [
        sum(bit for place, bit in enumerate(bits) if (number >> place) & 1)
        for number in range(lax.axis_size("dp"))
    ]


def place_of(offset):
    return sum(
        ((offset // bit) % 2) << place for place, bit in enumerate(dp_bits())
    )


def to_relative(values, mine):
    blocks = lax.axis_size("dp")
    width = values.shape[-1] // blocks
    return jnp.concatenate(
        [
            lax.dynamic_slice_in_dim(values, (mine ^ mask) * width, width, values.ndim - 1)
            for mask in block_masks()
        ],
        axis=-1,
    )


def from_relative(values, mine):
    blocks = lax.axis_size("dp")
    width = values.shape[-1] // blocks
    return jnp.concatenate(
        [
            lax.dynamic_slice_in_dim(values, place_of(mine ^ block) * width, width, values.ndim - 1)
            for block in range(blocks)
        ],
        axis=-1,
    )


def halves(values, half, axis):
    width = values.shape[axis] // 2
    mine = lax.dynamic_slice_in_dim(values, half * width, width, axis)
    other = lax.dynamic_slice_in_dim(values, (1 - half) * width, width, axis)
    return mine, other


def join_halves(mine, other, half, axis):
    return jnp.where(
        half == 0,
        jnp.concatenate([mine, other], axis=axis),
        jnp.concatenate([other, mine], axis=axis),
    )


def gather_rows(weight, half):
    mine, other = halves(weight.astype(jnp.bfloat16), half, 1)
    held = jnp.concatenate([mine, swap(other, "dp", PAIR)], axis=0)
    for bit in dp_bits()[1:]:
        held = jnp.concatenate([held, swap(held, "dp", bit)], axis=0)
    return held


def reduce_rows(terms, half):
    held = terms
    for bit in reversed(dp_bits()[1:]):
        rows = held.shape[0] // 2
        held = held[:rows] + swap(held[rows:].astype(jnp.bfloat16), "dp", bit).astype(jnp.float32)
    rows = held.shape[0] // 2
    other = swap(held[rows:].astype(jnp.bfloat16), "dp", PAIR).astype(jnp.float32)
    return join_halves(held[:rows], other, half, 1)


def reduce_small(terms, axis):
    held = terms
    for bit in reversed(dp_bits()):
        rows = held.shape[axis] // 2
        low = lax.slice_in_dim(held, 0, rows, axis=axis)
        high = lax.slice_in_dim(held, rows, 2 * rows, axis=axis)
        held = low + swap(high, "dp", bit)
    return held


def share_tokens(terms, tensor_at, kind):
    held = terms
    for bit in (1, 2):
        mine, other = halves(held, (tensor_at // bit) % 2, 1)
        held = mine + swap(other.astype(kind), "tensor", bit).astype(jnp.float32)
    return held[0], swap(held[1].astype(kind), "dp", PAIR).astype(jnp.float32)


def flip_pairs(values):
    blocks = lax.axis_size("dp")
    width = values.shape[-1] // blocks
    pieces = [values[..., (place ^ 1) * width : ((place ^ 1) + 1) * width] for place in range(blocks)]
    return jnp.concatenate(pieces, axis=-1)


def whole_tokens(values, tensor_at):
    for bit in (2, 1):
        values = join_halves(values, swap(values, "tensor", bit), (tensor_at // bit) % 2, 0)
    return values


def shards(
    block_input,
    out_grad,
    seg_ids,
    slot_live,
    norm_gain,
    z_weight,
    x_weight,
    bc_weight,
    dt_weight,
    conv_x,
    conv_bc,
    head_params,
    gated_gain,
    out_weight,
    norm_gain_sq,
    z_rows,
    z_cols,
    x_rows,
    x_cols,
    bc_rows,
    bc_cols,
    dt_rows,
    dt_cols,
    conv_x_sq,
    conv_bc_sq,
    head_sq,
    gated_gain_sq,
    out_rows,
    out_cols,
):
    data_count = lax.axis_size("dp")
    data_at = lax.axis_index("dp")
    tensor_at = lax.axis_index("tensor")
    half = (data_at // PAIR) % 2
    core = tensor_at % 2
    row_count = z_weight.shape[0]
    quarter = row_count // 4
    slot_tokens = block_input.shape[1]
    f32, bf16 = jnp.float32, jnp.bfloat16

    def pair_tokens(values):
        mine, _ = halves(values, core, 0)
        far = swap(mine, "dp", PAIR)
        near = swap(far, "tensor", 1)
        return jnp.stack([values, join_halves(far, near, core, 0)])

    whole_numbers = jnp.concatenate(
        [seg_ids[0], jnp.broadcast_to(slot_live, (128,))]
    ).reshape(-1, 128)
    far_numbers = swap(whole_numbers, "dp", PAIR)
    segments = jnp.stack([seg_ids[0], far_numbers[:-1].reshape(-1)])
    live = jnp.stack([slot_live[0], far_numbers[-1, 0]]).astype(f32)

    both_in = pair_tokens(block_input[0])
    dt_rows_low = dt_weight.astype(bf16).T
    bc_mine = lax.dynamic_slice_in_dim(bc_weight.astype(bf16), tensor_at * quarter, quarter, 0)
    small = jnp.concatenate([bc_mine.reshape(-1, 128), dt_rows_low.reshape(-1, 128)], axis=0)[None]
    for bit in dp_bits():
        small = jnp.concatenate([small, swap(small, "dp", bit)], axis=0)
    bc_piece_rows = quarter * bc_weight.shape[1] // 128
    low_dt = (
        small[:, bc_piece_rows:].reshape(data_count, dt_weight.shape[1], row_count).transpose(1, 0, 2)
    ).reshape(dt_weight.shape[1], -1)
    low_dt, _ = halves(low_dt, half, 0)
    bc_held = small[:, :bc_piece_rows].reshape(data_count, quarter, -1)
    bc_held = join_halves(bc_held, swap(bc_held, "tensor", 1), core, 1)
    bc_held = join_halves(bc_held, swap(bc_held, "tensor", 2), tensor_at // 2, 1)
    low_bc = bc_held.reshape(data_count * row_count, -1)

    low_x = gather_rows(x_weight, half)
    low_z = gather_rows(z_weight, half)
    low_out = gather_rows(out_weight, half)
    both_grad = pair_tokens(out_grad[0])

    taps_x, _ = halves(conv_x, half, 1)
    per_head, _ = halves(head_params, half, 1)
    gain_inner, _ = halves(gated_gain, half, 0)

    gain_rel = to_relative(norm_gain, data_at)
    in_rel = to_relative(both_in, data_at).astype(f32)
    mean_square = jnp.mean(in_rel * in_rel, axis=-1, keepdims=True)
    normed_low = (in_rel * lax.rsqrt(mean_square + norm_eps) * gain_rel).astype(bf16)
    normed_flat = normed_low.reshape(-1, normed_low.shape[-1])
    tokens = normed_flat.shape[0]

    def per_slot(values):
        return values.reshape(2, slot_tokens, -1)

    x_raw = per_slot(jnp.dot(normed_flat, low_x, preferred_element_type=f32))
    bc_raw = per_slot(jnp.dot(normed_flat, low_bc, preferred_element_type=f32))
    dt_raw = per_slot(rows_times(normed_flat, low_dt))
    gate_z = per_slot(jnp.dot(normed_flat, low_z, preferred_element_type=f32))

    def local_mixer(gate_in, x_in_raw, bc_in_raw, dt_in_raw, taps_x, taps_bc, per_head, gain_inner):
        return jax.vmap(mixer, in_axes=(0, 0, 0, 0, None, None, None, None, 0))(
            gate_in, x_in_raw, bc_in_raw, dt_in_raw, taps_x, taps_bc, per_head, gain_inner, segments
        )

    (scaled, squares), mixer_pull = jax.vjp(
        local_mixer, gate_z, x_raw, bc_raw, dt_raw, taps_x, conv_bc, per_head, gain_inner
    )
    scaled_low = scaled.astype(bf16).reshape(tokens, -1)

    def all_heads(values):
        values = add_over(values, "tensor", (1, 2))
        far = swap(values[1], "dp", PAIR)
        mine = values[0] + far
        return jnp.stack([mine, swap(mine, "dp", PAIR)])

    def all_heads_once(values):
        values = add_over(values, "tensor", (1, 2))
        return values + swap(values, "dp", PAIR)[::-1]

    total_squares = all_heads_once(squares)
    projected = per_slot(rows_times(scaled_low, low_out))
    inv_rms = lax.rsqrt(total_squares / INNER + norm_eps)
    cot_rel = to_relative(both_grad, data_at).astype(f32) * live[:, None, None]
    proj_grad = (cot_rel * inv_rms[:, :, None]).astype(bf16).reshape(tokens, -1)
    rms_grad = all_heads_once(jnp.sum(cot_rel * projected, axis=-1))
    squares_grad = rms_grad * -0.5 * inv_rms * inv_rms * inv_rms / INNER
    scaled_grad = per_slot(jnp.dot(proj_grad, low_out, preferred_element_type=f32))
    out_part = tokens_out(proj_grad, scaled_low)
    out_share = reduce_rows(out_part, half)

    share = slot_tokens // 4
    share_at = (core * 2 + tensor_at // 2) * share
    own, far = share_tokens(projected, tensor_at, bf16)
    projected_mine = own + flip_pairs(far)
    inv_mine = lax.dynamic_slice_in_dim(inv_rms[0], share_at, share, 0)
    in_mine = lax.dynamic_slice_in_dim(in_rel[0], share_at, share, 0)
    cot_mine = lax.dynamic_slice_in_dim(cot_rel[0], share_at, share, 0)
    output_mine = (in_mine + inv_mine[:, None] * projected_mine).astype(bf16)
    output = whole_tokens(from_relative(output_mine, data_at), tensor_at)

    (
        z_grad_raw,
        x_grad_raw,
        bc_grad_part,
        dt_grad_raw,
        convx_slot,
        convbc_part,
        head_slot,
        gated_slot,
    ) = mixer_pull((scaled_grad, squares_grad))
    z_low = z_grad_raw.astype(bf16).reshape(tokens, -1)
    x_low = x_grad_raw.astype(bf16).reshape(tokens, -1)
    dt_low = dt_grad_raw.astype(bf16).reshape(tokens, -1)
    z_share = reduce_rows(tokens_out(normed_flat, z_low), half)
    x_share = reduce_rows(tokens_out(normed_flat, x_low), half)
    input_part = per_slot(
        rows_times(z_low, low_z)
        + rows_times(x_low, low_x)
        + jnp.dot(dt_low, low_dt, preferred_element_type=f32)
    )
    bc_own, bc_far = share_tokens(bc_grad_part, tensor_at, f32)
    bc_low_mine = (bc_own + bc_far).astype(bf16)
    own, far = share_tokens(input_part, tensor_at, bf16)
    normed_grad = own + flip_pairs(far) + rows_times(bc_low_mine, low_bc)

    _, norm_pull = jax.vjp(norm_input, in_mine, gain_rel)
    block_grad, gain_slot = norm_pull(normed_grad)
    input_grad = whole_tokens(
        from_relative((cot_mine + block_grad).astype(bf16), data_at), tensor_at
    )

    bc_low = whole_tokens(bc_low_mine, tensor_at)
    bc_rows_part = tokens_out(normed_low[0], bc_low).reshape(data_count, row_count, -1)
    bc_rows_part = lax.dynamic_slice_in_dim(bc_rows_part, tensor_at * quarter, quarter, 1)
    dt_rows_part = tokens_out(dt_low, normed_flat).reshape(-1, data_count, row_count)
    small_part = jnp.concatenate(
        [
            bc_rows_part.reshape(data_count, -1, 128),
            dt_rows_part.transpose(1, 0, 2).reshape(data_count, -1, 128),
        ],
        axis=1,
    )
    held = small_part
    for bit in reversed(dp_bits()[1:]):
        count = held.shape[0] // 2
        held = held[:count] + swap(held[count:], "dp", bit)
    far = swap(held[1], "dp", PAIR)
    bc_share = (held[0, :bc_piece_rows] + far[:bc_piece_rows]).reshape(quarter, -1)
    dt_mine = held[0, bc_piece_rows:].reshape(-1, row_count)
    dt_other = far[bc_piece_rows:].reshape(-1, row_count)
    dt_share = join_halves(dt_mine, dt_other, half, 0).T
    bc_share = join_halves(bc_share, swap(bc_share, "tensor", 1), core, 0)
    bc_share = join_halves(bc_share, swap(bc_share, "tensor", 2), tensor_at // 2, 0)

    z_square = z_share * z_share + tiny_eps
    x_square = x_share * x_share + tiny_eps
    bc_square = bc_share * bc_share + tiny_eps
    dt_square = dt_share * dt_share + tiny_eps
    out_square = out_share * out_share + tiny_eps
    row_sums = jnp.stack(
        [
            jnp.sum(z_square, axis=1),
            jnp.sum(x_square, axis=1),
            jnp.sum(dt_square, axis=1),
            jnp.sum(out_square, axis=1),
        ]
    )
    z_row_sum, x_row_sum, dt_row_sum, out_row_sum = add_over(row_sums, "tensor", (1, 2))
    bc_row_sum = jnp.sum(bc_square, axis=1)

    def in_half(values):
        return join_halves(values, jnp.zeros_like(values), half, values.ndim - 1)

    def packed_sum(pieces, axis_bits):
        sizes = [piece.size for piece in pieces]
        flat = jnp.concatenate([piece.reshape(-1) for piece in pieces])
        fill = -flat.size % 128
        flat = jnp.pad(flat, (0, fill)).reshape(-1, 128)
        for axis, bits in axis_bits:
            flat = add_over(flat, axis, bits)
        flat = flat.reshape(-1)
        result, at = [], 0
        for piece, size in zip(pieces, sizes):
            result.append(flat[at : at + size].reshape(piece.shape))
            at += size
        return result

    norm_total, convbc_total = packed_sum(
        [from_relative(gain_slot, data_at), convbc_part],
        [("tensor", (1, 2)), ("dp", dp_bits())],
    )
    gated_total, convx_total, head_total = packed_sum(
        [in_half(gated_slot), in_half(convx_slot), in_half(head_slot)], [("dp", dp_bits())]
    )
    z_col_sum, x_col_sum, bc_col_sum, dt_col_sum, out_col_sum = packed_sum(
        [
            jnp.sum(z_square, axis=0),
            jnp.sum(x_square, axis=0),
            jnp.sum(bc_square, axis=0),
            jnp.sum(dt_square, axis=0),
            jnp.sum(out_square, axis=0),
        ],
        [("dp", dp_bits())],
    )
    z_rows_new = mix_state(z_rows, z_row_sum / INNER)
    x_rows_new = mix_state(x_rows, x_row_sum / INNER)
    bc_rows_new = mix_state(bc_rows, bc_row_sum / (2 * STATE))
    dt_rows_new = mix_state(dt_rows, dt_row_sum / HEADS)
    out_rows_new = mix_state(out_rows, out_row_sum / INNER)
    z_cols_new = mix_state(z_cols, z_col_sum / D)
    x_cols_new = mix_state(x_cols, x_col_sum / D)
    bc_cols_new = mix_state(bc_cols, bc_col_sum / D)
    dt_cols_new = mix_state(dt_cols, dt_col_sum / D)
    out_cols_new = mix_state(out_cols, out_col_sum / D)
    norm_second = mix_state(norm_gain_sq, norm_total * norm_total + tiny_eps)
    gated_second = mix_state(gated_gain_sq, gated_total * gated_total + tiny_eps)
    convx_second = mix_state(conv_x_sq, convx_total * convx_total + tiny_eps)
    convbc_second = mix_state(conv_bc_sq, convbc_total * convbc_total + tiny_eps)
    head_second = mix_state(head_sq, head_total * head_total + tiny_eps)
    norm_unit = norm_total * lax.rsqrt(norm_second)
    gated_unit = gated_total * lax.rsqrt(gated_second)
    convx_unit = convx_total * lax.rsqrt(convx_second)
    convbc_unit = convbc_total * lax.rsqrt(convbc_second)
    head_unit = head_total * lax.rsqrt(head_second)
    z_unit = z_share * lax.rsqrt(z_rows_new[:, None] * z_cols_new[None, :])
    x_unit = x_share * lax.rsqrt(x_rows_new[:, None] * x_cols_new[None, :])
    bc_unit = bc_share * lax.rsqrt(bc_rows_new[:, None] * bc_cols_new[None, :])
    dt_unit = dt_share * lax.rsqrt(dt_rows_new[:, None] * dt_cols_new[None, :])
    out_unit = out_share * lax.rsqrt(out_rows_new[:, None] * out_cols_new[None, :])
    tensor_count = lax.axis_size("tensor")
    unit_sums = jnp.stack(
        [
            jnp.sum(z_unit * z_unit),
            jnp.sum(x_unit * x_unit),
            jnp.sum(bc_unit * bc_unit) / tensor_count,
            jnp.sum(dt_unit * dt_unit),
            jnp.sum(out_unit * out_unit),
            jnp.sum(gated_unit * gated_unit) / data_count,
            jnp.sum(convx_unit * convx_unit) / data_count,
            jnp.sum(head_unit * head_unit) / data_count,
        ]
    )
    unit_sums = jnp.broadcast_to(unit_sums[:, None], (8, 128))
    unit_sums = add_over(add_over(unit_sums, "tensor", (1, 2)), "dp", dp_bits())
    (
        z_total,
        x_total,
        bc_total_sq,
        dt_total,
        out_total,
        gated_sq_total,
        convx_sq_total,
        head_sq_total,
    ) = unit_sums[:, 0]
    norm_sq_total = jnp.sum(norm_unit * norm_unit)
    convbc_sq_total = jnp.sum(convbc_unit * convbc_unit)
    in_rate = D ** (-0.5)
    out_rate = INNER ** (-0.5)
    z_upd = -in_rate * normalized(z_unit, z_total, D * INNER)
    x_upd = -in_rate * normalized(x_unit, x_total, D * INNER)
    bc_upd = -in_rate * normalized(bc_unit, bc_total_sq, D * 2 * STATE)
    dt_upd = -in_rate * normalized(dt_unit, dt_total, D * HEADS)
    out_upd = -out_rate * normalized(out_unit, out_total, D * INNER)
    norm_upd = -vector_rate * normalized(norm_unit, norm_sq_total, D)
    gated_upd = -vector_rate * normalized(gated_unit, gated_sq_total, INNER)
    convx_upd = -vector_rate * normalized(convx_unit, convx_sq_total, KCONV * INNER)
    convbc_upd = -vector_rate * normalized(convbc_unit, convbc_sq_total, KCONV * 2 * STATE)
    head_upd = -vector_rate * normalized(head_unit, head_sq_total, 3 * HEADS)
    return (
        output[None],
        input_grad[None],
        norm_total,
        norm_upd,
        norm_second,
        z_share,
        z_upd,
        z_rows_new,
        z_cols_new,
        x_share,
        x_upd,
        x_rows_new,
        x_cols_new,
        bc_share,
        bc_upd,
        bc_rows_new,
        bc_cols_new,
        dt_share,
        dt_upd,
        dt_rows_new,
        dt_cols_new,
        convx_total,
        convx_upd,
        convx_second,
        convbc_total,
        convbc_upd,
        convbc_second,
        head_total,
        head_upd,
        head_second,
        gated_total,
        gated_upd,
        gated_second,
        out_share,
        out_upd,
        out_rows_new,
        out_cols_new,
    )


def solution(mesh):
    in_specs = (
        P("dp", None, None),
        P("dp", None, None),
        P("dp", None),
        P("dp"),
        P(),
        P("dp", "tensor"),
        P("dp", "tensor"),
        P("dp", None),
        P("dp", "tensor"),
        P(None, "tensor"),
        P(),
        P(None, "tensor"),
        P("tensor"),
        P("dp", "tensor"),
        P(),
        P("dp"),
        P("tensor"),
        P("dp"),
        P("tensor"),
        P("dp"),
        P(),
        P("dp"),
        P("tensor"),
        P(None, "tensor"),
        P(),
        P(None, "tensor"),
        P("tensor"),
        P("dp"),
        P("tensor"),
    )
    out_specs = (
        P("dp", None, None),
        P("dp", None, None),
        P(),
        P(),
        P(),
        P("dp", "tensor"),
        P("dp", "tensor"),
        P("dp"),
        P("tensor"),
        P("dp", "tensor"),
        P("dp", "tensor"),
        P("dp"),
        P("tensor"),
        P("dp", None),
        P("dp", None),
        P("dp"),
        P(),
        P("dp", "tensor"),
        P("dp", "tensor"),
        P("dp"),
        P("tensor"),
        P(None, "tensor"),
        P(None, "tensor"),
        P(None, "tensor"),
        P(),
        P(),
        P(),
        P(None, "tensor"),
        P(None, "tensor"),
        P(None, "tensor"),
        P("tensor"),
        P("tensor"),
        P("tensor"),
        P("dp", "tensor"),
        P("dp", "tensor"),
        P("dp"),
        P("tensor"),
    )
    return jax.shard_map(shards, mesh=mesh, in_specs=in_specs, out_specs=out_specs, check_vma=False)
```

```python
import jax
import jax.numpy as jnp
from jax import lax
from jax.experimental import pallas as pl
from jax.experimental.pallas import tpu as pltpu
from jax.sharding import PartitionSpec as P

D = 2048
HEADS = 64
STATE = 128
INNER = 4096
KCONV = 4


norm_eps = 1e-05
decay_rate = 0.5
tiny_eps = 1e-30
unit_eps = 1e-06
vector_rate = 0.05


LANES = 128
PART = 256
WIDTH = 64


def cost_of(micros):
    return pl.CostEstimate(flops=micros * 1_000_000_000, bytes_accessed=1 << 20, transcendentals=0)


def two_parts(values):
    high = values.astype(jnp.bfloat16)
    return high, (values - high.astype(jnp.float32)).astype(jnp.bfloat16)


def plain(left, right):
    return lax.dot_general(
        left, right, (((1,), (0,)), ((), ())), preferred_element_type=jnp.float32
    )


def turned(left, right):
    return lax.dot_general(
        left, right, (((1,), (1,)), ((), ())), preferred_element_type=jnp.float32
    )


def fine(product, left, right):
    left_high, left_low = two_parts(left)
    right_high, right_low = two_parts(right)
    return (
        product(left_high, right_high)
        + product(left_high, right_low)
        + product(left_low, right_high)
    )


def running_sum(values, backward):
    rows = lax.broadcasted_iota(jnp.int32, (PART, PART), 0)
    columns = lax.broadcasted_iota(jnp.int32, (PART, PART), 1)
    within = (rows <= columns) if backward else (rows >= columns)
    ones = within.astype(jnp.float32).astype(jnp.bfloat16)

    def inside(block):
        high, rest = block.astype(jnp.bfloat16), block
        total = plain(ones, high)
        rest = block - high.astype(jnp.float32)
        for _ in range(2):
            part = rest.astype(jnp.bfloat16)
            total = total + plain(ones, part)
            rest = rest - part.astype(jnp.float32)
        return total

    blocks = [inside(values[:PART]), inside(values[PART:])]
    if backward:
        blocks[0] = blocks[0] + blocks[1][0:1]
    else:
        blocks[1] = blocks[1] + blocks[0][PART - 1 : PART]
    return jnp.concatenate(blocks, axis=0)


def sigmoid(values):
    return 1.0 / (1.0 + jnp.exp(-values))


def conv_rows(values, taps, same):
    result = taps[0:1] * values
    for offset in range(1, 4):
        shifted = pltpu.roll(values, offset, 0)
        result = result + taps[offset : offset + 1] * (shifted * same[offset - 1])
    return result


def conv_rows_back(grad, values, taps, same):
    length = values.shape[0]
    result = taps[0:1] * grad
    tap_rows = [jnp.sum(grad * values, axis=0, keepdims=True)]
    for offset in range(1, 4):
        kept = grad * same[offset - 1]
        result = result + pltpu.roll(taps[offset : offset + 1] * kept, length - offset, 0)
        tap_rows.append(
            jnp.sum(kept * pltpu.roll(values, offset, 0), axis=0, keepdims=True)
        )
    return result, tap_rows


def softplus(values):
    return jnp.maximum(values, 0.0) + jnp.log1p(jnp.exp(-jnp.abs(values)))


def marks_of(marks_ref):
    marks = marks_ref[0]
    same = [marks[:, place : place + 1] for place in (1, 2, 3)]
    return marks[:, 0:1], same, marks[:, 4:5]


def prepare(transposed, marks_ref, row_ref, bc_ref, dt_ref, taps_bc_ref, head_ref,
            bc_pre_ref, bc_ref_out, dt_out, cum_wide, dt_wide, cum_rows, score, bias):
    doc, same, _ = marks_of(marks_ref)
    bc_pre = conv_rows(bc_ref[0], taps_bc_ref[...], same)
    bc = bc_pre * sigmoid(bc_pre)
    bc_pre_ref[...] = bc_pre
    bc_ref_out[...] = bc
    b_mat, c_mat = bc[:, :LANES], bc[:, LANES:]
    first, second = slice(0, PART), slice(PART, 2 * PART)
    for place, (out_rows, in_rows) in enumerate(((first, first), (second, second), (second, first))):
        if transposed:
            score[place] = fine(turned, b_mat[in_rows], c_mat[out_rows])
        else:
            score[place] = fine(turned, c_mat[out_rows], b_mat[in_rows])
    rows = lax.broadcasted_iota(jnp.int32, (PART, PART), 0)
    columns = lax.broadcasted_iota(jnp.int32, (PART, PART), 1)
    causal = (rows <= columns) if transposed else (rows >= columns)
    doc_row = row_ref[0][0:1]
    for place, part in enumerate((first, second)):
        seen = causal & (doc[part] == doc_row[:, part])
        bias[place] = jnp.where(seen, 0.0, -1e30)
    step = softplus(dt_ref[0] + head_ref[0:1])
    decay = step * -jnp.exp(head_ref[1:2])
    total = running_sum(decay, False)
    dt_out[...] = step
    flipped = total.T
    lane = lax.broadcasted_iota(jnp.int32, (2 * PART, LANES), 1)
    for pair in range(cum_wide.shape[0]):
        one, two = 2 * pair, 2 * pair + 1
        cum_wide[pair] = jnp.where(lane < WIDTH, total[:, one : one + 1], total[:, two : two + 1])
        dt_wide[pair] = jnp.where(lane < WIDTH, step[:, one : one + 1], step[:, two : two + 1])
        cum_rows[one] = flipped[one : one + 1]
        cum_rows[two] = flipped[two : two + 1]


def edge_weights(wide, in_last):
    edge = wide[PART - 1 : PART]
    after = jnp.exp(wide[PART:] - edge) * in_last[PART:]
    before = jnp.exp(edge - wide[:PART]) * in_last[:PART]
    return after, before


def forward_body(marks_ref, row_ref, bc_ref, dt_ref, taps_bc_ref, head_ref, x_ref, z_ref, vec_ref,
                 scaled_ref, scan_ref, squares_ref,
                 bc_pre, bc_act, dt_act, cum_wide, dt_wide, cum_rows, score, bias):
    pair = pl.program_id(1)

    @pl.when(pair == 0)
    def _():
        prepare(False, marks_ref, row_ref, bc_ref, dt_ref, taps_bc_ref, head_ref,
                bc_pre, bc_act, dt_act, cum_wide, dt_wide, cum_rows, score, bias)
        squares_ref[...] = jnp.zeros_like(squares_ref)

    _, same, in_last = marks_of(marks_ref)
    vec = vec_ref[...]
    pre = conv_rows(x_ref[0], vec[0:4], same)
    values = pre * sigmoid(pre)
    wide = cum_wide[pair]
    stepped = dt_wide[pair] * values
    high, low_part = two_parts(stepped)
    both = jnp.concatenate([high, low_part], axis=1)
    lane = lax.broadcasted_iota(jnp.int32, (PART, LANES), 1)
    blocks = []
    for place in range(2):
        part = slice(place * PART, (place + 1) * PART)
        answers = []
        for k in range(2):
            row = cum_rows[2 * pair + k][:, part]
            kernel = jnp.exp(wide[part, k * WIDTH : k * WIDTH + 1] - row + bias[place])
            mixing_high, mixing_low = two_parts(score[place] * kernel)
            answer = plain(mixing_high, both[part])
            answers.append(
                answer[:, :LANES] + answer[:, LANES:] + plain(mixing_low, high[part])
            )
        blocks.append(jnp.where(lane < WIDTH, answers[0], answers[1]))
    after, before = edge_weights(wide, in_last)
    blocks[1] = blocks[1] + after * fine(plain, score[2], before * stepped[:PART])
    scanned = jnp.concatenate(blocks, axis=0)
    scan_ref[0] = scanned
    gate = z_ref[0]
    gated = (scanned + vec[5:6] * values) * (gate * sigmoid(gate))
    squares_ref[0] = squares_ref[0] + gated * gated
    scaled_ref[0] = (gated * vec[4:5]).astype(scaled_ref.dtype)


def backward_body(marks_ref, row_ref, bc_ref, dt_ref, taps_bc_ref, head_ref, x_ref, z_ref, vec_ref,
                  scan_ref, grad_ref, sq_grad_ref,
                  z_out, x_out, bc_out, dt_out, vec_out, taps_bc_out, head_out,
                  bc_pre, bc_act, dt_act, cum_wide, dt_wide, cum_rows, score, bias,
                  score_grad, from_rows, from_columns, from_in):
    pair = pl.program_id(1)

    @pl.when(pair == 0)
    def _():
        prepare(True, marks_ref, row_ref, bc_ref, dt_ref, taps_bc_ref, head_ref,
                bc_pre, bc_act, dt_act, cum_wide, dt_wide, cum_rows, score, bias)
        score_grad[...] = jnp.zeros_like(score_grad)
        from_rows[...] = jnp.zeros_like(from_rows)
        from_columns[...] = jnp.zeros_like(from_columns)
        from_in[...] = jnp.zeros_like(from_in)

    _, same, in_last = marks_of(marks_ref)
    vec = vec_ref[...]
    taps, gain, skip = vec[0:4], vec[4:5], vec[5:6]
    x_raw = x_ref[0]
    pre = conv_rows(x_raw, taps, same)
    pre_sig = sigmoid(pre)
    values = pre * pre_sig
    wide = cum_wide[pair]
    step = dt_wide[pair]
    stepped = step * values
    gate = z_ref[0]
    gate_sig = sigmoid(gate)
    gate_act = gate * gate_sig
    scanned = scan_ref[0]
    mixed = scanned + skip * values
    gated = mixed * gate_act
    scaled_grad = grad_ref[0]
    gated_grad = scaled_grad * gain + 2.0 * sq_grad_ref[0][:, 0:1] * gated
    z_out[0] = (gated_grad * mixed * (gate_sig * (1.0 + gate * (1.0 - gate_sig)))).astype(z_out.dtype)
    grad = gated_grad * gate_act
    rows = [
        None, None, None, None,
        jnp.sum(scaled_grad * gated, axis=0, keepdims=True),
        jnp.sum(grad * values, axis=0, keepdims=True),
    ]
    high, low_part = two_parts(grad)
    both = jnp.concatenate([high, low_part], axis=1)
    lane = lax.broadcasted_iota(jnp.int32, (PART, LANES), 1)

    def add_exponents(head, out_part, in_part, terms):
        from_rows[head, :, out_part] += jnp.sum(terms, axis=0, keepdims=True)
        gone = jnp.sum(terms, axis=1, keepdims=True)
        from_columns[in_part] += jnp.where(lane == head, gone, 0.0)

    blocks = []
    for place in range(2):
        part = slice(place * PART, (place + 1) * PART)
        answers = []
        total = score_grad[place]
        for k in range(2):
            row = cum_rows[2 * pair + k][:, part]
            kernel = jnp.exp(row - wide[part, k * WIDTH : k * WIDTH + 1] + bias[place])
            mixing = score[place] * kernel
            mixing_high, mixing_low = two_parts(mixing)
            answer = plain(mixing_high, both[part])
            answers.append(
                answer[:, :LANES] + answer[:, LANES:] + plain(mixing_low, high[part])
            )
            own = (lane < WIDTH) if k == 0 else (lane >= WIDTH)
            own_high, own_low = two_parts(jnp.where(own, stepped[part], 0.0))
            pulled = turned(
                jnp.concatenate([own_high, own_high], axis=1), both[part]
            ) + turned(own_low, high[part])
            total = total + pulled * kernel
            add_exponents(2 * pair + k, part, part, pulled * mixing)
        score_grad[place] = total
        blocks.append(jnp.where(lane < WIDTH, answers[0], answers[1]))
    after, before = edge_weights(wide, in_last)
    late = after * grad[PART:]
    early = before * stepped[:PART]
    blocks[0] = blocks[0] + before * fine(plain, score[2], late)
    for k in range(2):
        own = (lane < WIDTH) if k == 0 else (lane >= WIDTH)
        pulled = fine(turned, jnp.where(own, early, 0.0), late)
        score_grad[2] = score_grad[2] + pulled
        add_exponents(2 * pair + k, slice(PART, 2 * PART), slice(0, PART), pulled * score[2])
    pulled_in = jnp.concatenate(blocks, axis=0)
    places = lax.broadcasted_iota(jnp.int32, (LANES, LANES), 0) // WIDTH + 2 * pair
    columns = lax.broadcasted_iota(jnp.int32, (LANES, LANES), 1)
    chosen = (places == columns).astype(jnp.float32).astype(jnp.bfloat16)
    chosen = jnp.concatenate([chosen, chosen], axis=0)
    from_in[...] += plain(jnp.concatenate(two_parts(values * pulled_in), axis=1), chosen)
    pre_grad = (skip * grad + step * pulled_in) * (pre_sig * (1.0 + pre * (1.0 - pre_sig)))
    x_grad, rows[:4] = conv_rows_back(pre_grad, x_raw, taps, same)
    x_out[0] = x_grad.astype(x_out.dtype)
    vec_out[0] = jnp.concatenate(rows + [jnp.zeros((2, LANES), jnp.float32)], axis=0)

    @pl.when(pair == pl.num_programs(1) - 1)
    def _():
        steps = dt_act[...]
        rate = -jnp.exp(head_ref[1:2])
        direct = from_in[...]
        heads = from_rows.shape[0]
        arrived = jnp.concatenate(
            [from_rows[head] for head in range(heads)]
            + [jnp.zeros((LANES - heads, 2 * PART), jnp.float32)],
            axis=0,
        ).T
        decay_grad = running_sum(arrived - from_columns[...], True)
        step_grad = (direct + rate * decay_grad) * sigmoid(dt_ref[0] + head_ref[0:1])
        dt_out[0] = step_grad
        head_out[0] = jnp.concatenate(
            [
                jnp.sum(step_grad, axis=0, keepdims=True),
                rate * jnp.sum(decay_grad * steps, axis=0, keepdims=True),
                jnp.zeros((6, LANES), jnp.float32),
            ],
            axis=0,
        )
        b_mat, c_mat = bc_act[:, :LANES], bc_act[:, LANES:]
        first, second, cross = score_grad[0], score_grad[1], score_grad[2]
        b_grad = jnp.concatenate(
            [
                fine(plain, first, c_mat[:PART]) + fine(plain, cross, c_mat[PART:]),
                fine(plain, second, c_mat[PART:]),
            ],
            axis=0,
        )
        c_grad = jnp.concatenate(
            [
                fine(plain, first.T, b_mat[:PART]),
                fine(plain, second.T, b_mat[PART:]) + fine(plain, cross.T, b_mat[:PART]),
            ],
            axis=0,
        )
        shape = bc_pre[...]
        slope = sigmoid(shape)
        slope = slope * (1.0 + shape * (1.0 - slope))
        bc_grad, tap_rows = conv_rows_back(
            jnp.concatenate([b_grad, c_grad], axis=1) * slope, bc_ref[0], taps_bc_ref[...], same
        )
        bc_out[0] = bc_grad
        taps_bc_out[0] = jnp.concatenate(
            tap_rows + [jnp.zeros((4, 2 * LANES), jnp.float32)], axis=0
        )


def slot_block(first, *shape):
    return pl.BlockSpec((1,) + shape, lambda slot, pair: (slot + first, 0, 0))


def whole_block(*shape):
    return pl.BlockSpec(shape, lambda slot, pair: (0,) * len(shape))


def pair_block(first, length):
    return pl.BlockSpec((1, length, LANES), lambda slot, pair: (slot + first, 0, pair))


def common_specs(first, length):
    return [
        slot_block(first, length, 8),
        slot_block(first, 8, length),
        slot_block(first, length, 2 * LANES),
        slot_block(first, length, LANES),
        whole_block(4, 2 * LANES),
        whole_block(8, LANES),
        pair_block(first, length),
        pair_block(first, length),
        pl.BlockSpec((8, LANES), lambda slot, pair: (0, pair)),
    ]


def common_scratch(length, pairs):
    return [
        pltpu.VMEM((length, 2 * LANES), jnp.float32),
        pltpu.VMEM((length, 2 * LANES), jnp.float32),
        pltpu.VMEM((length, LANES), jnp.float32),
        pltpu.VMEM((pairs, length, LANES), jnp.float32),
        pltpu.VMEM((pairs, length, LANES), jnp.float32),
        pltpu.VMEM((2 * pairs, 1, length), jnp.float32),
        pltpu.VMEM((3, PART, PART), jnp.float32),
        pltpu.VMEM((2, PART, PART), jnp.float32),
    ]


def mixer_forward(common, interpret=False):
    slots, length, width = common[6].shape
    pairs = width // LANES
    return pl.pallas_call(
        forward_body,
        grid=(slots, pairs),
        in_specs=common_specs(0, length),
        out_specs=[pair_block(0, length), pair_block(0, length), slot_block(0, length, LANES)],
        out_shape=[
            jax.ShapeDtypeStruct((slots, length, width), jnp.bfloat16),
            jax.ShapeDtypeStruct((slots, length, width), jnp.float32),
            jax.ShapeDtypeStruct((slots, length, LANES), jnp.float32),
        ],
        scratch_shapes=common_scratch(length, pairs),
        cost_estimate=cost_of(16),
        name="mixer_forward",
        interpret=interpret,
    )(*common)


def mixer_backward(common, scanned, scaled_grad, sq_grad, slot, earlier=(), interpret=False):
    slots, length, width = common[6].shape
    pairs = width // LANES
    given = len(common) + 3

    def body(*refs):
        backward_body(*refs[:given], *refs[given + len(earlier) :])

    return pl.pallas_call(
        body,
        grid=(1, pairs),
        in_specs=common_specs(slot, length)
        + [pair_block(slot, length), pair_block(slot, length), slot_block(slot, length, 8)]
        + [pl.BlockSpec(memory_space=pl.ANY) for _ in earlier],
        out_specs=[
            pair_block(slot, length),
            pair_block(slot, length),
            slot_block(slot, length, 2 * LANES),
            slot_block(slot, length, LANES),
            pl.BlockSpec((1, 8, LANES), lambda _, pair: (slot, 0, pair)),
            slot_block(slot, 8, 2 * LANES),
            slot_block(slot, 8, LANES),
        ],
        out_shape=[
            jax.ShapeDtypeStruct((slots, length, width), jnp.bfloat16),
            jax.ShapeDtypeStruct((slots, length, width), jnp.bfloat16),
            jax.ShapeDtypeStruct((slots, length, 2 * LANES), jnp.float32),
            jax.ShapeDtypeStruct((slots, length, LANES), jnp.float32),
            jax.ShapeDtypeStruct((slots, 8, width), jnp.float32),
            jax.ShapeDtypeStruct((slots, 8, 2 * LANES), jnp.float32),
            jax.ShapeDtypeStruct((slots, 8, LANES), jnp.float32),
        ],
        input_output_aliases={given + place: place for place in range(len(earlier))},
        scratch_shapes=common_scratch(length, pairs)
        + [
            pltpu.VMEM((3, PART, PART), jnp.float32),
            pltpu.VMEM((2 * pairs, 1, length), jnp.float32),
            pltpu.VMEM((length, LANES), jnp.float32),
            pltpu.VMEM((length, LANES), jnp.float32),
        ],
        cost_estimate=cost_of(16),
        name="mixer_backward",
        interpret=interpret,
    )(*common, scanned, scaled_grad, sq_grad, *earlier)


def input_body(place_ref, z_ref, x_ref, dt_ref, z_rows_ref, x_rows_ref, dt_rows_ref, *rest):
    del place_ref

    def flat(ref):
        return ref[...].reshape(-1, ref.shape[-1])

    total = (
        turned(flat(z_ref), z_rows_ref[...])
        + turned(flat(x_ref), x_rows_ref[...])
        + plain(flat(dt_ref), dt_rows_ref[...])
    ).reshape(rest[-1].shape)
    for added in rest[:-1]:
        total = total + added[...]
    rest[-1][...] = total


def input_terms(place, z_low, x_low, dt_low, low_z, low_x, low_dt, *added):
    tokens = z_low.shape[0] // 4
    width = low_z.shape[1]
    features = low_z.shape[0]
    block = features // 4

    def by_half(values):
        return values.reshape(2, 2, tokens, -1)

    def half_block(values):
        return pl.BlockSpec((2, 1, tokens, values.shape[1]), lambda at, where: (0, where[0], 0, 0))

    weight = pl.BlockSpec((block, width), lambda at, where: (at, 0))
    out = pl.BlockSpec((2, tokens, block), lambda at, where: (0, 0, at))
    return pl.pallas_call(
        input_body,
        grid_spec=pltpu.PrefetchScalarGridSpec(
            num_scalar_prefetch=1,
            grid=(4,),
            in_specs=[
                half_block(z_low),
                half_block(x_low),
                half_block(dt_low),
                weight,
                weight,
                pl.BlockSpec((low_dt.shape[0], block), lambda at, where: (0, at)),
            ]
            + [out] * len(added),
            out_specs=out,
        ),
        out_shape=jax.ShapeDtypeStruct((2, tokens, features), jnp.float32),
        cost_estimate=cost_of(6),
        name="input_terms",
    )(
        place.astype(jnp.int32).reshape(1),
        by_half(z_low),
        by_half(x_low),
        by_half(dt_low),
        low_z,
        low_x,
        low_dt,
        *added,
    )


def document_marks(segments):
    slots, length = segments.shape
    docs = segments.astype(jnp.float32)
    columns = [docs]
    for offset in (1, 2, 3):
        same = (segments[:, offset:] == segments[:, :-offset]).astype(jnp.float32)
        columns.append(jnp.pad(same, ((0, 0), (offset, 0))))
    columns.append((segments == segments[:, PART - 1 : PART]).astype(jnp.float32))
    zero = jnp.zeros_like(docs)
    marks = jnp.stack(columns + [zero] * 3, axis=-1)
    return marks, jnp.broadcast_to(docs[:, None, :], (slots, 8, length))


def norm_input(values, gain):
    mean_square = jnp.mean(values * values, axis=1, keepdims=True)
    return values * lax.rsqrt(mean_square + norm_eps) * gain


def rows_times(left, right):
    return lax.dot_general(
        left, right, (((1,), (1,)), ((), ())), preferred_element_type=jnp.float32
    )


def tokens_out(left, right):
    return lax.dot_general(
        left, right, (((0,), (0,)), ((), ())), preferred_element_type=jnp.float32
    )


def mix_state(old_state, fresh_term):
    return decay_rate * old_state + (1.0 - decay_rate) * fresh_term


def normalized(unit, square_total, entries):
    return unit * lax.rsqrt(square_total / entries + unit_eps)


def swap(value, axis, bit):
    size = lax.axis_size(axis)
    return lax.ppermute(value, axis, [(place, place ^ bit) for place in range(size)])


def add_over(value, axis, bits):
    for bit in bits:
        value = value + swap(value, axis, bit)
    return value


PAIR = 2


def dp_bits():
    count = lax.axis_size("dp")
    rest = [1 << place for place in reversed(range(count.bit_length() - 1)) if 1 << place != PAIR]
    return [PAIR] + rest


def block_masks():
    bits = dp_bits()
    return [
        sum(bit for place, bit in enumerate(bits) if (number >> place) & 1)
        for number in range(lax.axis_size("dp"))
    ]


def place_of(offset):
    return sum(
        ((offset // bit) % 2) << place for place, bit in enumerate(dp_bits())
    )


def to_relative(values, mine):
    blocks = lax.axis_size("dp")
    width = values.shape[-1] // blocks
    return jnp.concatenate(
        [
            lax.dynamic_slice_in_dim(values, (mine ^ mask) * width, width, values.ndim - 1)
            for mask in block_masks()
        ],
        axis=-1,
    )


def from_relative(values, mine):
    blocks = lax.axis_size("dp")
    width = values.shape[-1] // blocks
    return jnp.concatenate(
        [
            lax.dynamic_slice_in_dim(values, place_of(mine ^ block) * width, width, values.ndim - 1)
            for block in range(blocks)
        ],
        axis=-1,
    )


def halves(values, half, axis):
    width = values.shape[axis] // 2
    mine = lax.dynamic_slice_in_dim(values, half * width, width, axis)
    other = lax.dynamic_slice_in_dim(values, (1 - half) * width, width, axis)
    return mine, other


def join_halves(mine, other, half, axis):
    return jnp.where(
        half == 0,
        jnp.concatenate([mine, other], axis=axis),
        jnp.concatenate([other, mine], axis=axis),
    )


def after(value, *others):
    return lax.optimization_barrier((value,) + others)[0] if others else value


def step(*values):
    return lax.optimization_barrier(values)


def gather_middle(held):
    middle = dp_bits()[1:-1]
    for bit in middle[:-1]:
        held = jnp.concatenate([held, swap(held, "dp", bit)], axis=0)
    return held, swap(held, "dp", middle[-1])


def gradient_rows(left, right, place, kind, *added):
    part = left.shape[1] // 4
    total = tokens_out(left[:, place * part : (place + 1) * part], right)
    for value in added:
        total = total + value.astype(jnp.float32)
    return total.astype(kind)


def low_bits(value):
    return value.astype(jnp.bfloat16)


def middle_sum(held, got):
    held = held + got
    for bit in reversed(dp_bits()[1:-2]):
        count = held.shape[0] // 2
        sent = swap(low_bits(held[count:]), "dp", bit)
        held = held[:count] + sent.astype(jnp.float32)
    count = held.shape[0] // 2
    return held[:count], low_bits(held[count:])


def kept_and_sent(held, tensor_at, bit, kind):
    mine, other = halves(held, (tensor_at // bit) % 2, 1)
    return mine, other.astype(kind)


def share_tokens(terms, tensor_at):
    held = terms
    for bit in (1, 2):
        mine, other = kept_and_sent(held, tensor_at, bit, jnp.float32)
        held = mine + swap(other, "tensor", bit)
    return held[0] + swap(held[1], "dp", PAIR)


def flip_pairs(values):
    blocks = lax.axis_size("dp")
    width = values.shape[-1] // blocks
    pieces = [values[..., (place ^ 1) * width : ((place ^ 1) + 1) * width] for place in range(blocks)]
    return jnp.concatenate(pieces, axis=-1)


def whole_tokens(values, tensor_at):
    for bit in (2, 1):
        values = join_halves(values, swap(values, "tensor", bit), (tensor_at // bit) % 2, 0)
    return values


def shards(
    block_input,
    out_grad,
    seg_ids,
    slot_live,
    norm_gain,
    z_weight,
    x_weight,
    bc_weight,
    dt_weight,
    conv_x,
    conv_bc,
    head_params,
    gated_gain,
    out_weight,
    norm_gain_sq,
    z_rows,
    z_cols,
    x_rows,
    x_cols,
    bc_rows,
    bc_cols,
    dt_rows,
    dt_cols,
    conv_x_sq,
    conv_bc_sq,
    head_sq,
    gated_gain_sq,
    out_rows,
    out_cols,
):
    data_count = lax.axis_size("dp")
    data_at = lax.axis_index("dp")
    tensor_at = lax.axis_index("tensor")
    half = (data_at // PAIR) % 2
    core = tensor_at % 2
    row_count = z_weight.shape[0]
    quarter = row_count // 4
    slot_tokens = block_input.shape[1]
    f32, bf16 = jnp.float32, jnp.bfloat16

    share = slot_tokens // 4
    share_at = (core * 2 + tensor_at // 2) * share
    last_bit = dp_bits()[-1]

    def share_of(values):
        return lax.dynamic_slice_in_dim(values, share_at, share, 0)

    def halves_of(weight):
        return halves(weight.astype(bf16), half, 1)

    def rows_of(*pieces):
        return jnp.concatenate(pieces, axis=0)

    whole_numbers = jnp.concatenate(
        [seg_ids[0], jnp.broadcast_to(slot_live, (8 * 128 - slot_tokens,))]
    ).astype(bf16).reshape(-1, 128)
    dt_rows_low = dt_weight.astype(bf16).T
    bc_mine = lax.dynamic_slice_in_dim(bc_weight.astype(bf16), tensor_at * quarter, quarter, 0)
    small = rows_of(bc_mine.reshape(-1, 128), dt_rows_low.reshape(-1, 128))
    small_count = small.shape[0]
    x_mine, x_other = halves_of(x_weight)
    small_far = swap(rows_of(small, whole_numbers), "dp", PAIR)
    x_far = swap(x_other, "dp", PAIR)
    small_far, x_far, x_mine, small, z_weight, out_weight, block_input, out_grad = step(
        small_far, x_far, x_mine, small, z_weight, out_weight, block_input, out_grad
    )

    far_numbers = small_far[small_count:].astype(jnp.int32)
    segments = jnp.stack([seg_ids[0], far_numbers.reshape(-1)[:slot_tokens]])
    live = jnp.stack([slot_live[0], far_numbers[-1, 0]]).astype(f32)
    small = jnp.stack([small, small_far[:small_count]])
    for bit in dp_bits()[1:-1]:
        small = rows_of(small, swap(small, "dp", bit))
    x_held, x_got = gather_middle(rows_of(x_mine, x_far))
    x_first = swap(x_held, "dp", last_bit)
    z_mine, z_other = halves_of(z_weight)
    out_mine, out_other = halves_of(out_weight)
    in_share, grad_share = share_of(block_input[0]), share_of(out_grad[0])
    marks, doc_rows = document_marks(segments)
    taps_x, _ = halves(conv_x, half, 1)
    per_head, _ = halves(head_params, half, 1)
    gain_inner, _ = halves(gated_gain, half, 0)
    head_count = per_head.shape[1]
    head_rows = jnp.pad(per_head, ((0, 5), (0, 128 - head_count)))
    vectors = jnp.concatenate(
        [taps_x, gain_inner[None], jnp.repeat(per_head[2], WIDTH)[None], jnp.zeros((2, taps_x.shape[1]))]
    )
    marks, doc_rows, head_rows, vectors, z_mine, out_mine = step(
        marks, doc_rows, head_rows, vectors, z_mine, out_mine
    )
    gain_rel = to_relative(norm_gain, data_at)
    own_rel = to_relative(block_input[0], data_at).astype(f32)
    x_got, x_first, small, z_other, in_share, grad_share, out_other, own_rel, marks, vectors = step(
        x_got, x_first, small, z_other, in_share, grad_share, out_other, own_rel, marks, vectors
    )

    x_second = swap(x_got, "dp", last_bit)
    small = rows_of(small, swap(small, "dp", last_bit))
    z_far = swap(z_other, "dp", PAIR)
    in_far = swap(in_share, "dp", PAIR)
    bc_piece_rows = quarter * bc_weight.shape[1] // 128
    bc_held = small[:, :bc_piece_rows].reshape(data_count, quarter, -1)
    x_second, small, z_far, in_far, z_mine, grad_share, out_other, bc_held = step(
        x_second, small, z_far, in_far, z_mine, grad_share, out_other, bc_held
    )

    z_held, z_got = gather_middle(rows_of(z_mine, z_far))
    z_first = swap(z_held, "dp", last_bit)
    in_far = join_halves(in_far, swap(in_far, "tensor", 2), tensor_at // 2, 0)
    bc_held = join_halves(bc_held, swap(bc_held, "tensor", 1), core, 1)
    low_x = rows_of(x_held, x_got, x_first, x_second)
    z_got, z_first, in_far, bc_held, grad_share, out_other, low_x = step(
        z_got, z_first, in_far, bc_held, grad_share, out_other, low_x
    )

    z_second = swap(z_got, "dp", last_bit)
    out_far = swap(out_other, "dp", PAIR)
    grad_far = swap(grad_share, "dp", PAIR)
    in_far = join_halves(in_far, swap(in_far, "tensor", 1), core, 0)
    bc_held = join_halves(bc_held, swap(bc_held, "tensor", 2), tensor_at // 2, 1)
    low_bc = bc_held.reshape(data_count * row_count, -1)
    in_rel = jnp.stack([own_rel, to_relative(in_far, data_at).astype(f32)])
    mean_square = jnp.mean(in_rel * in_rel, axis=-1, keepdims=True)
    normed_low = (in_rel * lax.rsqrt(mean_square + norm_eps) * gain_rel).astype(bf16)
    z_second, out_far, grad_far, normed_low = step(z_second, out_far, grad_far, normed_low)
    low_z = rows_of(z_held, z_got, z_first, z_second)
    out_held, out_got = gather_middle(rows_of(out_mine, out_far))
    out_first = swap(out_held, "dp", last_bit)
    grad_far = join_halves(grad_far, swap(grad_far, "tensor", 2), tensor_at // 2, 0)
    low_out = rows_of(out_held, out_got, out_first, swap(out_got, "dp", last_bit))
    grad_far = join_halves(grad_far, swap(grad_far, "tensor", 1), core, 0)
    both_grad = jnp.stack([out_grad[0], grad_far])

    low_dt = (
        small[:, bc_piece_rows:].reshape(data_count, dt_weight.shape[1], row_count).transpose(1, 0, 2)
    ).reshape(dt_weight.shape[1], -1)
    low_dt, _ = halves(low_dt, half, 0)
    low_dt = jnp.pad(low_dt, ((0, 128 - head_count), (0, 0)))
    normed_flat = normed_low.reshape(-1, normed_low.shape[-1])
    tokens = normed_flat.shape[0]

    def per_slot(values):
        return values.reshape(2, slot_tokens, -1)

    bc_raw = per_slot(jnp.dot(normed_flat, low_bc, preferred_element_type=f32))
    dt_raw = per_slot(rows_times(normed_flat, low_dt))
    x_raw = per_slot(jnp.dot(normed_flat, low_x, preferred_element_type=f32))
    gate_z = per_slot(jnp.dot(normed_flat, low_z, preferred_element_type=f32))
    common = (marks, doc_rows, bc_raw, dt_raw, conv_bc, head_rows, x_raw, gate_z, vectors)
    scaled_both, scanned, square_parts = mixer_forward(common)
    scaled_low = scaled_both.reshape(tokens, -1)

    projected = per_slot(rows_times(scaled_low, low_out))
    cot_rel = to_relative(both_grad, data_at) * live.astype(bf16)[:, None, None]
    totals = jnp.stack([jnp.sum(square_parts, axis=-1), jnp.sum(cot_rel.astype(f32) * projected, axis=-1)], axis=1)
    totals = totals + swap(totals, "tensor", 1)
    _, leaving = kept_and_sent(projected, tensor_at, 1, bf16)
    arriving = swap(after(leaving, totals), "tensor", 1)
    totals = totals + swap(totals, "tensor", 2)
    totals = totals + swap(totals, "dp", PAIR)[::-1]
    total_squares, rms_grad = totals[:, 0], totals[:, 1]
    inv_rms = lax.rsqrt(total_squares / INNER + norm_eps)
    squares_grad = rms_grad * -0.5 * inv_rms * inv_rms * inv_rms / INNER
    proj_grad = (cot_rel.astype(f32) * inv_rms[:, :, None]).astype(bf16).reshape(tokens, -1)
    scaled_grad = per_slot(jnp.dot(proj_grad, low_out, preferred_element_type=f32))

    part = low_out.shape[0] // 4
    middle_bit = dp_bits()[-2]

    def across(value, bit):
        return swap(value, "dp", bit).astype(f32)

    out_sent = [gradient_rows(proj_grad, scaled_low, place, bf16) for place in (3, 2)]
    out_passed, out_kept = [swap(value, "dp", last_bit) for value in out_sent]
    gradients = (
        after(scaled_grad, *out_sent, arriving),
        jnp.broadcast_to(squares_grad[:, :, None], (2, slot_tokens, 8)),
    )
    backward = mixer_backward(common, scanned, *gradients, 0)
    proj_later, out_passed, projected, *backward = step(proj_grad, out_passed, projected, *backward)
    shared, _ = kept_and_sent(projected, tensor_at, 1, bf16)
    shared, leaving = kept_and_sent(shared + arriving.astype(f32), tensor_at, 2, bf16)
    out_middle = gradient_rows(proj_later, scaled_low, 1, bf16, out_passed)
    out_middle, leaving, *backward = step(out_middle, leaving, *backward)
    out_got = across(out_middle, middle_bit)
    arriving = swap(leaving, "tensor", 2)
    inv_mine = lax.dynamic_slice_in_dim(inv_rms[0], share_at, share, 0)
    in_mine = to_relative(share_of(block_input[0]), data_at).astype(f32)
    cot_mine = to_relative(share_of(out_grad[0]), data_at).astype(f32) * live[0]
    z_both, x_both, bc_grad_part, dt_both, vector_terms, taps_bc_terms, head_terms = mixer_backward(
        common, scanned, *gradients, 1, backward
    )
    x_both, z_both, bc_grad_part, out_got, out_kept, arriving = step(
        x_both, z_both, bc_grad_part, out_got, out_kept, arriving
    )
    vector_terms = jnp.sum(vector_terms, axis=0)
    convx_slot, gated_slot = vector_terms[:4], vector_terms[4]
    convbc_part = jnp.sum(taps_bc_terms, axis=0)[:4]
    head_slot = jnp.concatenate(
        [
            jnp.sum(head_terms, axis=0)[:2, :head_count],
            jnp.sum(vector_terms[5].reshape(head_count, -1), axis=1)[None],
        ]
    )
    bc_kept, bc_leaving = kept_and_sent(bc_grad_part, tensor_at, 1, f32)
    bc_arriving = swap(bc_leaving, "tensor", 1)
    z_low = z_both.reshape(tokens, -1)
    x_low = x_both.reshape(tokens, -1)
    dt_low = dt_both.astype(bf16).reshape(tokens, -1)
    matrices = (low_z, low_x, low_dt)
    x_sent = gradient_rows(normed_flat, x_low, 3, bf16)
    x_low, z_low, x_sent, bc_arriving = step(x_low, z_low, x_sent, bc_arriving)

    x_passed = swap(x_sent, "dp", last_bit)
    bc_kept, bc_leaving = kept_and_sent(bc_kept + bc_arriving, tensor_at, 2, f32)
    bc_arriving = swap(bc_leaving, "tensor", 2)
    x_low, z_low, bc_leaving = step(x_low, z_low, bc_leaving)
    z_sent = gradient_rows(normed_flat, z_low, 3, bf16)
    both_sent = jnp.concatenate(
        [gradient_rows(normed_flat, values, 2, bf16) for values in (x_low, z_low)], axis=0
    )
    input_leaving = input_terms(1 - core, z_low, x_low, dt_low, *matrices)
    x_low, z_low, x_passed, z_sent, both_sent, input_leaving, bc_arriving = step(
        x_low, z_low, x_passed, z_sent, both_sent, input_leaving, bc_arriving
    )

    x_middle = gradient_rows(normed_flat, x_low, 1, bf16, x_passed)
    x_got = across(x_middle, middle_bit)
    z_passed = swap(z_sent, "dp", last_bit)
    input_arriving = swap(input_leaving, "tensor", 1)
    bc_kept = bc_kept + bc_arriving
    bc_far = swap(bc_kept[1], "dp", PAIR)
    x_low, z_low, x_middle, bc_kept, arriving = step(x_low, z_low, x_middle, bc_kept, arriving)
    input_kept = input_terms(core, z_low, x_low, dt_low, *matrices)
    shared = shared + arriving.astype(f32)
    out_mine, out_leaving = middle_sum(gradient_rows(proj_later, scaled_low, 0, f32, out_kept), out_got)
    x_low, z_low, input_kept, z_passed, input_arriving, bc_far, shared, out_mine, out_leaving = step(
        x_low, z_low, input_kept, z_passed, input_arriving, bc_far, shared, out_mine, out_leaving
    )

    z_middle = gradient_rows(normed_flat, z_low, 1, bf16, z_passed)
    z_got = across(z_middle, middle_bit)
    both_kept = swap(both_sent, "dp", last_bit)
    bc_low_mine = (bc_kept[0] + bc_far).astype(bf16)
    bc_far = swap(bc_low_mine, "tensor", 2)
    x_low, z_low, z_middle, bc_low_mine = step(x_low, z_low, z_middle, bc_low_mine)
    input_kept, input_leaving = kept_and_sent(input_kept + input_arriving, tensor_at, 2, bf16)
    bc_far, input_kept, input_leaving = step(bc_far, input_kept, input_leaving)

    input_arriving = swap(input_leaving, "tensor", 2)
    bc_low = join_halves(bc_low_mine, bc_far, tensor_at // 2, 0)
    bc_far = swap(bc_low, "tensor", 1)
    dt_part = tokens_out(dt_low, normed_flat)[:head_count]
    bc_far, dt_part = step(bc_far, dt_part)

    bc_low = join_halves(bc_low, bc_far, core, 0)
    bc_columns = bc_low.shape[1] // 4
    bc_part = tokens_out(
        lax.dynamic_slice_in_dim(bc_low, tensor_at * bc_columns, bc_columns, 1), normed_low[0]
    )
    held = jnp.concatenate([bc_part, dt_part], axis=0)
    held = jnp.stack(
        [held[:, block * row_count : (block + 1) * row_count] for block in range(data_count)]
    )
    both_kept, held, x_got = step(both_kept, held, x_got)

    count = held.shape[0] // 2
    held = held[:count] + swap(held[count:], "dp", last_bit)
    out_far = across(out_leaving, PAIR)
    projected_far = across(low_bits(shared[1]), PAIR)
    x_terms = gradient_rows(normed_flat, x_low, 0, f32, both_kept[:part])
    z_terms = gradient_rows(normed_flat, z_low, 0, f32, both_kept[part:])
    x_mine, x_leaving = middle_sum(x_terms, x_got)
    input_arriving, held, z_terms, x_leaving, z_got, projected_far, out_far = step(
        input_arriving, held, z_terms, x_leaving, z_got, projected_far, out_far
    )

    input_mine = input_kept + input_arriving.astype(f32)
    input_far = swap(low_bits(input_mine[1]), "dp", PAIR)
    for bit in reversed(dp_bits()[1:-1]):
        count = held.shape[0] // 2
        held = held[:count] + swap(held[count:], "dp", bit)
    z_mine, z_leaving = middle_sum(z_terms, z_got)
    both_far = across(jnp.concatenate([x_leaving, z_leaving], axis=0), PAIR)
    projected_mine = shared[0] + flip_pairs(projected_far)
    output = from_relative((in_mine + inv_mine[:, None] * projected_mine).astype(bf16), data_at)
    output_far = swap(output, "tensor", 2)
    out_share = join_halves(out_mine, out_far, half, 1)
    input_far, held, out_share = step(input_far, held, out_share)

    small_far = swap(held[1], "dp", PAIR)
    normed_grad = (
        input_mine[0] + flip_pairs(input_far.astype(f32)) + rows_times(bc_low_mine, low_bc)
    )

    _, norm_pull = jax.vjp(norm_input, in_mine, gain_rel)
    block_grad, gain_slot = norm_pull(normed_grad)
    input_grad = from_relative((cot_mine + block_grad).astype(bf16), data_at)
    both_far, small_far, gain_slot, output_far = step(both_far, small_far, gain_slot, output_far)
    output = join_halves(output, output_far, tensor_at // 2, 0)
    output = join_halves(output, swap(output, "tensor", 1), core, 0)
    x_share = join_halves(x_mine, both_far[: x_mine.shape[0]], half, 1)
    z_share = join_halves(z_mine, both_far[x_mine.shape[0] :], half, 1)

    bc_share = held[0, :bc_columns] + small_far[:bc_columns]
    dt_share = join_halves(held[0, bc_columns:], small_far[bc_columns:], half, 0).T
    bc_share = join_halves(bc_share, swap(bc_share, "tensor", 1), core, 0)
    bc_share = join_halves(bc_share, swap(bc_share, "tensor", 2), tensor_at // 2, 0).T

    def in_half(values):
        return join_halves(values, jnp.zeros_like(values), half, values.ndim - 1)

    def packed_sum(pieces, axis_bits):
        sizes = [piece.size for piece in pieces]
        flat = jnp.concatenate([piece.reshape(-1) for piece in pieces])
        fill = -flat.size % 128
        flat = jnp.pad(flat, (0, fill)).reshape(-1, 128)
        for axis, bits in axis_bits:
            flat = add_over(flat, axis, bits)
        flat = flat.reshape(-1)
        result, at = [], 0
        for piece, size in zip(pieces, sizes):
            result.append(flat[at : at + size].reshape(piece.shape))
            at += size
        return result

    norm_sum, convbc_sum = packed_sum(
        [from_relative(gain_slot, data_at), convbc_part], [("tensor", (1, 2))]
    )
    z_share, bc_share, norm_sum, convbc_sum = step(z_share, bc_share, norm_sum, convbc_sum)
    z_square = z_share * z_share + tiny_eps
    x_square = x_share * x_share + tiny_eps
    bc_square = bc_share * bc_share + tiny_eps
    dt_square = dt_share * dt_share + tiny_eps
    out_square = out_share * out_share + tiny_eps
    row_sums = jnp.stack(
        [
            jnp.sum(z_square, axis=1),
            jnp.sum(x_square, axis=1),
            jnp.sum(dt_square, axis=1),
            jnp.sum(out_square, axis=1),
        ]
    )
    z_row_sum, x_row_sum, dt_row_sum, out_row_sum = add_over(row_sums, "tensor", (1, 2))
    bc_row_sum = jnp.sum(bc_square, axis=1)

    (
        norm_total,
        convbc_total,
        gated_total,
        convx_total,
        head_total,
        z_col_sum,
        x_col_sum,
        bc_col_sum,
        dt_col_sum,
        out_col_sum,
    ) = packed_sum(
        [
            norm_sum,
            convbc_sum,
            in_half(gated_slot),
            in_half(convx_slot),
            in_half(head_slot),
            jnp.sum(z_square, axis=0),
            jnp.sum(x_square, axis=0),
            jnp.sum(bc_square, axis=0),
            jnp.sum(dt_square, axis=0),
            jnp.sum(out_square, axis=0),
        ],
        [("dp", dp_bits())],
    )
    z_rows_new = mix_state(z_rows, z_row_sum / INNER)
    x_rows_new = mix_state(x_rows, x_row_sum / INNER)
    bc_rows_new = mix_state(bc_rows, bc_row_sum / (2 * STATE))
    dt_rows_new = mix_state(dt_rows, dt_row_sum / HEADS)
    out_rows_new = mix_state(out_rows, out_row_sum / INNER)
    z_cols_new = mix_state(z_cols, z_col_sum / D)
    x_cols_new = mix_state(x_cols, x_col_sum / D)
    bc_cols_new = mix_state(bc_cols, bc_col_sum / D)
    dt_cols_new = mix_state(dt_cols, dt_col_sum / D)
    out_cols_new = mix_state(out_cols, out_col_sum / D)
    norm_second = mix_state(norm_gain_sq, norm_total * norm_total + tiny_eps)
    gated_second = mix_state(gated_gain_sq, gated_total * gated_total + tiny_eps)
    convx_second = mix_state(conv_x_sq, convx_total * convx_total + tiny_eps)
    convbc_second = mix_state(conv_bc_sq, convbc_total * convbc_total + tiny_eps)
    head_second = mix_state(head_sq, head_total * head_total + tiny_eps)
    norm_unit = norm_total * lax.rsqrt(norm_second)
    gated_unit = gated_total * lax.rsqrt(gated_second)
    convx_unit = convx_total * lax.rsqrt(convx_second)
    convbc_unit = convbc_total * lax.rsqrt(convbc_second)
    head_unit = head_total * lax.rsqrt(head_second)
    z_unit = z_share * lax.rsqrt(z_rows_new[:, None] * z_cols_new[None, :])
    x_unit = x_share * lax.rsqrt(x_rows_new[:, None] * x_cols_new[None, :])
    bc_unit = bc_share * lax.rsqrt(bc_rows_new[:, None] * bc_cols_new[None, :])
    dt_unit = dt_share * lax.rsqrt(dt_rows_new[:, None] * dt_cols_new[None, :])
    out_unit = out_share * lax.rsqrt(out_rows_new[:, None] * out_cols_new[None, :])
    tensor_count = lax.axis_size("tensor")
    unit_sums = jnp.stack(
        [
            jnp.sum(z_unit * z_unit),
            jnp.sum(x_unit * x_unit),
            jnp.sum(bc_unit * bc_unit) / tensor_count,
            jnp.sum(dt_unit * dt_unit),
            jnp.sum(out_unit * out_unit),
            jnp.sum(gated_unit * gated_unit) / data_count,
            jnp.sum(convx_unit * convx_unit) / data_count,
            jnp.sum(head_unit * head_unit) / data_count,
        ]
    )
    unit_sums = jnp.broadcast_to(unit_sums[:, None], (8, 128))
    unit_sums = add_over(unit_sums, "tensor", (1, 2))
    unit_sums, input_grad, output = step(unit_sums, input_grad, output)
    input_far = swap(input_grad, "tensor", 2)
    unit_sums = add_over(unit_sums, "dp", dp_bits())
    input_far, unit_sums = step(input_far, unit_sums)
    input_grad = join_halves(input_grad, input_far, tensor_at // 2, 0)
    input_grad = join_halves(input_grad, swap(input_grad, "tensor", 1), core, 0)
    (
        z_total,
        x_total,
        bc_total_sq,
        dt_total,
        out_total,
        gated_sq_total,
        convx_sq_total,
        head_sq_total,
    ) = unit_sums[:, 0]
    norm_sq_total = jnp.sum(norm_unit * norm_unit)
    convbc_sq_total = jnp.sum(convbc_unit * convbc_unit)
    in_rate = D ** (-0.5)
    out_rate = INNER ** (-0.5)
    z_upd = -in_rate * normalized(z_unit, z_total, D * INNER)
    x_upd = -in_rate * normalized(x_unit, x_total, D * INNER)
    bc_upd = -in_rate * normalized(bc_unit, bc_total_sq, D * 2 * STATE)
    dt_upd = -in_rate * normalized(dt_unit, dt_total, D * HEADS)
    out_upd = -out_rate * normalized(out_unit, out_total, D * INNER)
    norm_upd = -vector_rate * normalized(norm_unit, norm_sq_total, D)
    gated_upd = -vector_rate * normalized(gated_unit, gated_sq_total, INNER)
    convx_upd = -vector_rate * normalized(convx_unit, convx_sq_total, KCONV * INNER)
    convbc_upd = -vector_rate * normalized(convbc_unit, convbc_sq_total, KCONV * 2 * STATE)
    head_upd = -vector_rate * normalized(head_unit, head_sq_total, 3 * HEADS)
    return (
        output[None],
        input_grad[None],
        norm_total,
        norm_upd,
        norm_second,
        z_share,
        z_upd,
        z_rows_new,
        z_cols_new,
        x_share,
        x_upd,
        x_rows_new,
        x_cols_new,
        bc_share,
        bc_upd,
        bc_rows_new,
        bc_cols_new,
        dt_share,
        dt_upd,
        dt_rows_new,
        dt_cols_new,
        convx_total,
        convx_upd,
        convx_second,
        convbc_total,
        convbc_upd,
        convbc_second,
        head_total,
        head_upd,
        head_second,
        gated_total,
        gated_upd,
        gated_second,
        out_share,
        out_upd,
        out_rows_new,
        out_cols_new,
    )


def solution(mesh):
    in_specs = (
        P("dp", None, None),
        P("dp", None, None),
        P("dp", None),
        P("dp"),
        P(),
        P("dp", "tensor"),
        P("dp", "tensor"),
        P("dp", None),
        P("dp", "tensor"),
        P(None, "tensor"),
        P(),
        P(None, "tensor"),
        P("tensor"),
        P("dp", "tensor"),
        P(),
        P("dp"),
        P("tensor"),
        P("dp"),
        P("tensor"),
        P("dp"),
        P(),
        P("dp"),
        P("tensor"),
        P(None, "tensor"),
        P(),
        P(None, "tensor"),
        P("tensor"),
        P("dp"),
        P("tensor"),
    )
    out_specs = (
        P("dp", None, None),
        P("dp", None, None),
        P(),
        P(),
        P(),
        P("dp", "tensor"),
        P("dp", "tensor"),
        P("dp"),
        P("tensor"),
        P("dp", "tensor"),
        P("dp", "tensor"),
        P("dp"),
        P("tensor"),
        P("dp", None),
        P("dp", None),
        P("dp"),
        P(),
        P("dp", "tensor"),
        P("dp", "tensor"),
        P("dp"),
        P("tensor"),
        P(None, "tensor"),
        P(None, "tensor"),
        P(None, "tensor"),
        P(),
        P(),
        P(),
        P(None, "tensor"),
        P(None, "tensor"),
        P(None, "tensor"),
        P("tensor"),
        P("tensor"),
        P("tensor"),
        P("dp", "tensor"),
        P("dp", "tensor"),
        P("dp"),
        P("tensor"),
    )
    return jax.shard_map(shards, mesh=mesh, in_specs=in_specs, out_specs=out_specs, check_vma=False)
```

```python
import jax
import jax.numpy as jnp
from jax import lax
from jax.experimental import pallas as pl
from jax.experimental.pallas import tpu as pltpu
from jax.sharding import PartitionSpec as P

D = 2048
HEADS = 64
STATE = 128
INNER = 4096
KCONV = 4


norm_eps = 1e-05
decay_rate = 0.5
tiny_eps = 1e-30
unit_eps = 1e-06
vector_rate = 0.05


LANES = 128
PART = 256
WIDTH = 64


def cost_of(micros):
    return pl.CostEstimate(flops=micros * 1_000_000_000, bytes_accessed=1 << 20, transcendentals=0)


def two_parts(values):
    high = values.astype(jnp.bfloat16)
    return high, (values - high.astype(jnp.float32)).astype(jnp.bfloat16)


def plain(left, right):
    return lax.dot_general(
        left, right, (((1,), (0,)), ((), ())), preferred_element_type=jnp.float32
    )


def turned(left, right):
    return lax.dot_general(
        left, right, (((1,), (1,)), ((), ())), preferred_element_type=jnp.float32
    )


def fine(product, left, right):
    left_high, left_low = two_parts(left)
    right_high, right_low = two_parts(right)
    return (
        product(left_high, right_high)
        + product(left_high, right_low)
        + product(left_low, right_high)
    )


def running_sum(values, backward):
    rows = lax.broadcasted_iota(jnp.int32, (PART, PART), 0)
    columns = lax.broadcasted_iota(jnp.int32, (PART, PART), 1)
    within = (rows <= columns) if backward else (rows >= columns)
    ones = within.astype(jnp.float32).astype(jnp.bfloat16)

    def inside(block):
        high, rest = block.astype(jnp.bfloat16), block
        total = plain(ones, high)
        rest = block - high.astype(jnp.float32)
        for _ in range(2):
            part = rest.astype(jnp.bfloat16)
            total = total + plain(ones, part)
            rest = rest - part.astype(jnp.float32)
        return total

    blocks = [inside(values[:PART]), inside(values[PART:])]
    if backward:
        blocks[0] = blocks[0] + blocks[1][0:1]
    else:
        blocks[1] = blocks[1] + blocks[0][PART - 1 : PART]
    return jnp.concatenate(blocks, axis=0)


def sigmoid(values):
    return 1.0 / (1.0 + jnp.exp(-values))


def conv_rows(values, taps, same):
    result = taps[0:1] * values
    for offset in range(1, 4):
        shifted = pltpu.roll(values, offset, 0)
        result = result + taps[offset : offset + 1] * (shifted * same[offset - 1])
    return result


def conv_rows_back(grad, values, taps, same):
    length = values.shape[0]
    result = taps[0:1] * grad
    tap_rows = [jnp.sum(grad * values, axis=0, keepdims=True)]
    for offset in range(1, 4):
        kept = grad * same[offset - 1]
        result = result + pltpu.roll(taps[offset : offset + 1] * kept, length - offset, 0)
        tap_rows.append(
            jnp.sum(kept * pltpu.roll(values, offset, 0), axis=0, keepdims=True)
        )
    return result, tap_rows


def softplus(values):
    return jnp.maximum(values, 0.0) + jnp.log1p(jnp.exp(-jnp.abs(values)))


def marks_of(marks_ref):
    marks = marks_ref[0]
    same = [marks[:, place : place + 1] for place in (1, 2, 3)]
    return marks[:, 0:1], same, marks[:, 4:5]


def prepare(transposed, marks_ref, row_ref, bc_ref, dt_ref, taps_bc_ref, head_ref,
            bc_pre_ref, bc_ref_out, dt_out, cum_wide, dt_wide, cum_rows, score, bias):
    doc, same, _ = marks_of(marks_ref)
    bc_pre = conv_rows(bc_ref[0], taps_bc_ref[...], same)
    bc = bc_pre * sigmoid(bc_pre)
    bc_pre_ref[...] = bc_pre
    bc_ref_out[...] = bc
    b_mat, c_mat = bc[:, :LANES], bc[:, LANES:]
    first, second = slice(0, PART), slice(PART, 2 * PART)
    for place, (out_rows, in_rows) in enumerate(((first, first), (second, second), (second, first))):
        if transposed:
            score[place] = fine(turned, b_mat[in_rows], c_mat[out_rows])
        else:
            score[place] = fine(turned, c_mat[out_rows], b_mat[in_rows])
    rows = lax.broadcasted_iota(jnp.int32, (PART, PART), 0)
    columns = lax.broadcasted_iota(jnp.int32, (PART, PART), 1)
    causal = (rows <= columns) if transposed else (rows >= columns)
    doc_row = row_ref[0][0:1]
    for place, part in enumerate((first, second)):
        seen = causal & (doc[part] == doc_row[:, part])
        bias[place] = jnp.where(seen, 0.0, -1e30)
    step = softplus(dt_ref[0] + head_ref[0:1])
    decay = step * -jnp.exp(head_ref[1:2])
    total = running_sum(decay, False)
    dt_out[...] = step
    flipped = total.T
    lane = lax.broadcasted_iota(jnp.int32, (2 * PART, LANES), 1)
    for pair in range(cum_wide.shape[0]):
        one, two = 2 * pair, 2 * pair + 1
        cum_wide[pair] = jnp.where(lane < WIDTH, total[:, one : one + 1], total[:, two : two + 1])
        dt_wide[pair] = jnp.where(lane < WIDTH, step[:, one : one + 1], step[:, two : two + 1])
        cum_rows[one] = flipped[one : one + 1]
        cum_rows[two] = flipped[two : two + 1]


def edge_weights(wide, in_last):
    edge = wide[PART - 1 : PART]
    after = jnp.exp(wide[PART:] - edge) * in_last[PART:]
    before = jnp.exp(edge - wide[:PART]) * in_last[:PART]
    return after, before


def forward_body(marks_ref, row_ref, bc_ref, dt_ref, taps_bc_ref, head_ref, x_ref, z_ref, vec_ref,
                 scaled_ref, scan_ref, squares_ref,
                 bc_pre, bc_act, dt_act, cum_wide, dt_wide, cum_rows, score, bias):
    pair = pl.program_id(1)

    @pl.when(pair == 0)
    def _():
        prepare(False, marks_ref, row_ref, bc_ref, dt_ref, taps_bc_ref, head_ref,
                bc_pre, bc_act, dt_act, cum_wide, dt_wide, cum_rows, score, bias)
        squares_ref[...] = jnp.zeros_like(squares_ref)

    _, same, in_last = marks_of(marks_ref)
    vec = vec_ref[...]
    pre = conv_rows(x_ref[0], vec[0:4], same)
    values = pre * sigmoid(pre)
    wide = cum_wide[pair]
    stepped = dt_wide[pair] * values
    high, low_part = two_parts(stepped)
    both = jnp.concatenate([high, low_part], axis=1)
    lane = lax.broadcasted_iota(jnp.int32, (PART, LANES), 1)
    blocks = []
    for place in range(2):
        part = slice(place * PART, (place + 1) * PART)
        answers = []
        for k in range(2):
            row = cum_rows[2 * pair + k][:, part]
            kernel = jnp.exp(wide[part, k * WIDTH : k * WIDTH + 1] - row + bias[place])
            mixing_high, mixing_low = two_parts(score[place] * kernel)
            answer = plain(mixing_high, both[part])
            answers.append(
                answer[:, :LANES] + answer[:, LANES:] + plain(mixing_low, high[part])
            )
        blocks.append(jnp.where(lane < WIDTH, answers[0], answers[1]))
    after, before = edge_weights(wide, in_last)
    blocks[1] = blocks[1] + after * fine(plain, score[2], before * stepped[:PART])
    scanned = jnp.concatenate(blocks, axis=0)
    scan_ref[0] = scanned
    gate = z_ref[0]
    gated = (scanned + vec[5:6] * values) * (gate * sigmoid(gate))
    squares_ref[0] = squares_ref[0] + gated * gated
    scaled_ref[0] = (gated * vec[4:5]).astype(scaled_ref.dtype)


def backward_body(marks_ref, row_ref, bc_ref, dt_ref, taps_bc_ref, head_ref, x_ref, z_ref, vec_ref,
                  scan_ref, grad_ref, sq_grad_ref,
                  z_out, x_out, bc_out, dt_out, vec_out, taps_bc_out, head_out,
                  bc_pre, bc_act, dt_act, cum_wide, dt_wide, cum_rows, score, bias,
                  score_grad, from_rows, from_columns, from_in):
    pair = pl.program_id(1)

    @pl.when(pair == 0)
    def _():
        prepare(True, marks_ref, row_ref, bc_ref, dt_ref, taps_bc_ref, head_ref,
                bc_pre, bc_act, dt_act, cum_wide, dt_wide, cum_rows, score, bias)
        score_grad[...] = jnp.zeros_like(score_grad)
        from_rows[...] = jnp.zeros_like(from_rows)
        from_columns[...] = jnp.zeros_like(from_columns)
        from_in[...] = jnp.zeros_like(from_in)

    _, same, in_last = marks_of(marks_ref)
    vec = vec_ref[...]
    taps, gain, skip = vec[0:4], vec[4:5], vec[5:6]
    x_raw = x_ref[0]
    pre = conv_rows(x_raw, taps, same)
    pre_sig = sigmoid(pre)
    values = pre * pre_sig
    wide = cum_wide[pair]
    step = dt_wide[pair]
    stepped = step * values
    gate = z_ref[0]
    gate_sig = sigmoid(gate)
    gate_act = gate * gate_sig
    scanned = scan_ref[0]
    mixed = scanned + skip * values
    gated = mixed * gate_act
    scaled_grad = grad_ref[0]
    gated_grad = scaled_grad * gain + 2.0 * sq_grad_ref[0][:, 0:1] * gated
    z_out[0] = (gated_grad * mixed * (gate_sig * (1.0 + gate * (1.0 - gate_sig)))).astype(z_out.dtype)
    grad = gated_grad * gate_act
    rows = [
        None, None, None, None,
        jnp.sum(scaled_grad * gated, axis=0, keepdims=True),
        jnp.sum(grad * values, axis=0, keepdims=True),
    ]
    high, low_part = two_parts(grad)
    both = jnp.concatenate([high, low_part], axis=1)
    lane = lax.broadcasted_iota(jnp.int32, (PART, LANES), 1)

    def add_exponents(head, out_part, in_part, terms):
        from_rows[head, :, out_part] += jnp.sum(terms, axis=0, keepdims=True)
        gone = jnp.sum(terms, axis=1, keepdims=True)
        from_columns[in_part] += jnp.where(lane == head, gone, 0.0)

    blocks = []
    for place in range(2):
        part = slice(place * PART, (place + 1) * PART)
        answers = []
        total = score_grad[place]
        for k in range(2):
            row = cum_rows[2 * pair + k][:, part]
            kernel = jnp.exp(row - wide[part, k * WIDTH : k * WIDTH + 1] + bias[place])
            mixing = score[place] * kernel
            mixing_high, mixing_low = two_parts(mixing)
            answer = plain(mixing_high, both[part])
            answers.append(
                answer[:, :LANES] + answer[:, LANES:] + plain(mixing_low, high[part])
            )
            own = (lane < WIDTH) if k == 0 else (lane >= WIDTH)
            own_high, own_low = two_parts(jnp.where(own, stepped[part], 0.0))
            pulled = turned(
                jnp.concatenate([own_high, own_high], axis=1), both[part]
            ) + turned(own_low, high[part])
            total = total + pulled * kernel
            add_exponents(2 * pair + k, part, part, pulled * mixing)
        score_grad[place] = total
        blocks.append(jnp.where(lane < WIDTH, answers[0], answers[1]))
    after, before = edge_weights(wide, in_last)
    late = after * grad[PART:]
    early = before * stepped[:PART]
    blocks[0] = blocks[0] + before * fine(plain, score[2], late)
    for k in range(2):
        own = (lane < WIDTH) if k == 0 else (lane >= WIDTH)
        pulled = fine(turned, jnp.where(own, early, 0.0), late)
        score_grad[2] = score_grad[2] + pulled
        add_exponents(2 * pair + k, slice(PART, 2 * PART), slice(0, PART), pulled * score[2])
    pulled_in = jnp.concatenate(blocks, axis=0)
    places = lax.broadcasted_iota(jnp.int32, (LANES, LANES), 0) // WIDTH + 2 * pair
    columns = lax.broadcasted_iota(jnp.int32, (LANES, LANES), 1)
    chosen = (places == columns).astype(jnp.float32).astype(jnp.bfloat16)
    chosen = jnp.concatenate([chosen, chosen], axis=0)
    from_in[...] += plain(jnp.concatenate(two_parts(values * pulled_in), axis=1), chosen)
    pre_grad = (skip * grad + step * pulled_in) * (pre_sig * (1.0 + pre * (1.0 - pre_sig)))
    x_grad, rows[:4] = conv_rows_back(pre_grad, x_raw, taps, same)
    x_out[0] = x_grad.astype(x_out.dtype)
    vec_out[0] = jnp.concatenate(rows + [jnp.zeros((2, LANES), jnp.float32)], axis=0)

    @pl.when(pair == pl.num_programs(1) - 1)
    def _():
        steps = dt_act[...]
        rate = -jnp.exp(head_ref[1:2])
        direct = from_in[...]
        heads = from_rows.shape[0]
        arrived = jnp.concatenate(
            [from_rows[head] for head in range(heads)]
            + [jnp.zeros((LANES - heads, 2 * PART), jnp.float32)],
            axis=0,
        ).T
        decay_grad = running_sum(arrived - from_columns[...], True)
        step_grad = (direct + rate * decay_grad) * sigmoid(dt_ref[0] + head_ref[0:1])
        dt_out[0] = step_grad
        head_out[0] = jnp.concatenate(
            [
                jnp.sum(step_grad, axis=0, keepdims=True),
                rate * jnp.sum(decay_grad * steps, axis=0, keepdims=True),
                jnp.zeros((6, LANES), jnp.float32),
            ],
            axis=0,
        )
        b_mat, c_mat = bc_act[:, :LANES], bc_act[:, LANES:]
        first, second, cross = score_grad[0], score_grad[1], score_grad[2]
        b_grad = jnp.concatenate(
            [
                fine(plain, first, c_mat[:PART]) + fine(plain, cross, c_mat[PART:]),
                fine(plain, second, c_mat[PART:]),
            ],
            axis=0,
        )
        c_grad = jnp.concatenate(
            [
                fine(plain, first.T, b_mat[:PART]),
                fine(plain, second.T, b_mat[PART:]) + fine(plain, cross.T, b_mat[:PART]),
            ],
            axis=0,
        )
        shape = bc_pre[...]
        slope = sigmoid(shape)
        slope = slope * (1.0 + shape * (1.0 - slope))
        bc_grad, tap_rows = conv_rows_back(
            jnp.concatenate([b_grad, c_grad], axis=1) * slope, bc_ref[0], taps_bc_ref[...], same
        )
        bc_out[0] = bc_grad
        taps_bc_out[0] = jnp.concatenate(
            tap_rows + [jnp.zeros((4, 2 * LANES), jnp.float32)], axis=0
        )


def slot_block(first, *shape):
    return pl.BlockSpec((1,) + shape, lambda slot, pair: (slot + first, 0, 0))


def whole_block(*shape):
    return pl.BlockSpec(shape, lambda slot, pair: (0,) * len(shape))


def pair_block(first, length):
    return pl.BlockSpec((1, length, LANES), lambda slot, pair: (slot + first, 0, pair))


def common_specs(first, length):
    return [
        slot_block(first, length, 8),
        slot_block(first, 8, length),
        slot_block(first, length, 2 * LANES),
        slot_block(first, length, LANES),
        whole_block(4, 2 * LANES),
        whole_block(8, LANES),
        pair_block(first, length),
        pair_block(first, length),
        pl.BlockSpec((8, LANES), lambda slot, pair: (0, pair)),
    ]


def common_scratch(length, pairs):
    return [
        pltpu.VMEM((length, 2 * LANES), jnp.float32),
        pltpu.VMEM((length, 2 * LANES), jnp.float32),
        pltpu.VMEM((length, LANES), jnp.float32),
        pltpu.VMEM((pairs, length, LANES), jnp.float32),
        pltpu.VMEM((pairs, length, LANES), jnp.float32),
        pltpu.VMEM((2 * pairs, 1, length), jnp.float32),
        pltpu.VMEM((3, PART, PART), jnp.float32),
        pltpu.VMEM((2, PART, PART), jnp.float32),
    ]


def mixer_forward(common, interpret=False):
    slots, length, width = common[6].shape
    pairs = width // LANES
    return pl.pallas_call(
        forward_body,
        grid=(slots, pairs),
        in_specs=common_specs(0, length),
        out_specs=[pair_block(0, length), pair_block(0, length), slot_block(0, length, LANES)],
        out_shape=[
            jax.ShapeDtypeStruct((slots, length, width), jnp.bfloat16),
            jax.ShapeDtypeStruct((slots, length, width), jnp.float32),
            jax.ShapeDtypeStruct((slots, length, LANES), jnp.float32),
        ],
        scratch_shapes=common_scratch(length, pairs),
        cost_estimate=cost_of(16),
        name="mixer_forward",
        interpret=interpret,
    )(*common)


def mixer_backward(common, scanned, scaled_grad, sq_grad, slot, earlier=(), interpret=False):
    slots, length, width = common[6].shape
    pairs = width // LANES
    given = len(common) + 3

    def body(*refs):
        backward_body(*refs[:given], *refs[given + len(earlier) :])

    return pl.pallas_call(
        body,
        grid=(1, pairs),
        in_specs=common_specs(slot, length)
        + [pair_block(slot, length), pair_block(slot, length), slot_block(slot, length, 8)]
        + [pl.BlockSpec(memory_space=pl.ANY) for _ in earlier],
        out_specs=[
            pair_block(slot, length),
            pair_block(slot, length),
            slot_block(slot, length, 2 * LANES),
            slot_block(slot, length, LANES),
            pl.BlockSpec((1, 8, LANES), lambda _, pair: (slot, 0, pair)),
            slot_block(slot, 8, 2 * LANES),
            slot_block(slot, 8, LANES),
        ],
        out_shape=[
            jax.ShapeDtypeStruct((slots, length, width), jnp.bfloat16),
            jax.ShapeDtypeStruct((slots, length, width), jnp.bfloat16),
            jax.ShapeDtypeStruct((slots, length, 2 * LANES), jnp.float32),
            jax.ShapeDtypeStruct((slots, length, LANES), jnp.float32),
            jax.ShapeDtypeStruct((slots, 8, width), jnp.float32),
            jax.ShapeDtypeStruct((slots, 8, 2 * LANES), jnp.float32),
            jax.ShapeDtypeStruct((slots, 8, LANES), jnp.float32),
        ],
        input_output_aliases={given + place: place for place in range(len(earlier))},
        scratch_shapes=common_scratch(length, pairs)
        + [
            pltpu.VMEM((3, PART, PART), jnp.float32),
            pltpu.VMEM((2 * pairs, 1, length), jnp.float32),
            pltpu.VMEM((length, LANES), jnp.float32),
            pltpu.VMEM((length, LANES), jnp.float32),
        ],
        cost_estimate=cost_of(16),
        name="mixer_backward",
        interpret=interpret,
    )(*common, scanned, scaled_grad, sq_grad, *earlier)


def input_body(place_ref, z_ref, x_ref, dt_ref, z_rows_ref, x_rows_ref, dt_rows_ref, *rest):
    del place_ref

    def flat(ref):
        return ref[...].reshape(-1, ref.shape[-1])

    total = (
        turned(flat(z_ref), z_rows_ref[...])
        + turned(flat(x_ref), x_rows_ref[...])
        + plain(flat(dt_ref), dt_rows_ref[...])
    ).reshape(rest[-1].shape)
    for added in rest[:-1]:
        total = total + added[...]
    rest[-1][...] = total


def input_terms(place, z_low, x_low, dt_low, low_z, low_x, low_dt, *added):
    tokens = z_low.shape[0] // 4
    width = low_z.shape[1]
    features = low_z.shape[0]
    block = features // 4

    def by_half(values):
        return values.reshape(2, 2, tokens, -1)

    def half_block(values):
        return pl.BlockSpec((2, 1, tokens, values.shape[1]), lambda at, where: (0, where[0], 0, 0))

    weight = pl.BlockSpec((block, width), lambda at, where: (at, 0))
    out = pl.BlockSpec((2, tokens, block), lambda at, where: (0, 0, at))
    return pl.pallas_call(
        input_body,
        grid_spec=pltpu.PrefetchScalarGridSpec(
            num_scalar_prefetch=1,
            grid=(4,),
            in_specs=[
                half_block(z_low),
                half_block(x_low),
                half_block(dt_low),
                weight,
                weight,
                pl.BlockSpec((low_dt.shape[0], block), lambda at, where: (0, at)),
            ]
            + [out] * len(added),
            out_specs=out,
        ),
        out_shape=jax.ShapeDtypeStruct((2, tokens, features), jnp.float32),
        cost_estimate=cost_of(6),
        name="input_terms",
    )(
        place.astype(jnp.int32).reshape(1),
        by_half(z_low),
        by_half(x_low),
        by_half(dt_low),
        low_z,
        low_x,
        low_dt,
        *added,
    )


def document_marks(segments):
    slots, length = segments.shape
    docs = segments.astype(jnp.float32)
    columns = [docs]
    for offset in (1, 2, 3):
        same = (segments[:, offset:] == segments[:, :-offset]).astype(jnp.float32)
        columns.append(jnp.pad(same, ((0, 0), (offset, 0))))
    columns.append((segments == segments[:, PART - 1 : PART]).astype(jnp.float32))
    zero = jnp.zeros_like(docs)
    marks = jnp.stack(columns + [zero] * 3, axis=-1)
    return marks, jnp.broadcast_to(docs[:, None, :], (slots, 8, length))


def norm_input(values, gain):
    mean_square = jnp.mean(values * values, axis=1, keepdims=True)
    return values * lax.rsqrt(mean_square + norm_eps) * gain


def rows_times(left, right):
    return lax.dot_general(
        left, right, (((1,), (1,)), ((), ())), preferred_element_type=jnp.float32
    )


def tokens_out(left, right):
    return lax.dot_general(
        left, right, (((0,), (0,)), ((), ())), preferred_element_type=jnp.float32
    )


def mix_state(old_state, fresh_term):
    return decay_rate * old_state + (1.0 - decay_rate) * fresh_term


def normalized(unit, square_total, entries):
    return unit * lax.rsqrt(square_total / entries + unit_eps)


def swap(value, axis, bit):
    size = lax.axis_size(axis)
    return lax.ppermute(value, axis, [(place, place ^ bit) for place in range(size)])


def add_over(value, axis, bits):
    for bit in bits:
        value = value + swap(value, axis, bit)
    return value


PAIR = 2


def dp_bits():
    count = lax.axis_size("dp")
    rest = [1 << place for place in reversed(range(count.bit_length() - 1)) if 1 << place != PAIR]
    return [PAIR] + rest


def block_masks():
    bits = dp_bits()
    return [
        sum(bit for place, bit in enumerate(bits) if (number >> place) & 1)
        for number in range(lax.axis_size("dp"))
    ]


def place_of(offset):
    return sum(
        ((offset // bit) % 2) << place for place, bit in enumerate(dp_bits())
    )


def to_relative(values, mine):
    blocks = lax.axis_size("dp")
    width = values.shape[-1] // blocks
    return jnp.concatenate(
        [
            lax.dynamic_slice_in_dim(values, (mine ^ mask) * width, width, values.ndim - 1)
            for mask in block_masks()
        ],
        axis=-1,
    )


def from_relative(values, mine):
    blocks = lax.axis_size("dp")
    width = values.shape[-1] // blocks
    return jnp.concatenate(
        [
            lax.dynamic_slice_in_dim(values, place_of(mine ^ block) * width, width, values.ndim - 1)
            for block in range(blocks)
        ],
        axis=-1,
    )


def halves(values, half, axis):
    width = values.shape[axis] // 2
    mine = lax.dynamic_slice_in_dim(values, half * width, width, axis)
    other = lax.dynamic_slice_in_dim(values, (1 - half) * width, width, axis)
    return mine, other


def join_halves(mine, other, half, axis):
    low, high = jnp.where(half == 0, mine, other), jnp.where(half == 0, other, mine)
    return jnp.concatenate([low, high], axis=axis)


def after(value, *others):
    return lax.optimization_barrier((value,) + others)[0] if others else value


def step(*values):
    return lax.optimization_barrier(values)


def gather_middle(held):
    middle = dp_bits()[1:-1]
    for bit in middle[:-1]:
        held = jnp.concatenate([held, swap(held, "dp", bit)], axis=0)
    return held, swap(held, "dp", middle[-1])


def gradient_rows(left, right, place, kind, *added):
    part = left.shape[1] // 4
    total = tokens_out(left[:, place * part : (place + 1) * part], right)
    for value in added:
        total = total + value.astype(jnp.float32)
    return total.astype(kind)


def low_bits(value):
    return value.astype(jnp.bfloat16)


def middle_sum(held, got):
    held = held + got.astype(jnp.float32)
    for bit in reversed(dp_bits()[1:-2]):
        count = held.shape[0] // 2
        sent = swap(low_bits(held[count:]), "dp", bit)
        held = held[:count] + sent.astype(jnp.float32)
    count = held.shape[0] // 2
    return held[:count], low_bits(held[count:])


def kept_and_sent(held, tensor_at, bit, kind):
    mine, other = halves(held, (tensor_at // bit) % 2, 1)
    return mine, other.astype(kind)


def share_tokens(terms, tensor_at):
    held = terms
    for bit in (1, 2):
        mine, other = kept_and_sent(held, tensor_at, bit, jnp.float32)
        held = mine + swap(other, "tensor", bit)
    return held[0] + swap(held[1], "dp", PAIR)


def flip_pairs(values):
    blocks = lax.axis_size("dp")
    width = values.shape[-1] // blocks
    pieces = [values[..., (place ^ 1) * width : ((place ^ 1) + 1) * width] for place in range(blocks)]
    return jnp.concatenate(pieces, axis=-1)


def whole_tokens(values, tensor_at):
    for bit in (2, 1):
        values = join_halves(values, swap(values, "tensor", bit), (tensor_at // bit) % 2, 0)
    return values


def shards(
    block_input,
    out_grad,
    seg_ids,
    slot_live,
    norm_gain,
    z_weight,
    x_weight,
    bc_weight,
    dt_weight,
    conv_x,
    conv_bc,
    head_params,
    gated_gain,
    out_weight,
    norm_gain_sq,
    z_rows,
    z_cols,
    x_rows,
    x_cols,
    bc_rows,
    bc_cols,
    dt_rows,
    dt_cols,
    conv_x_sq,
    conv_bc_sq,
    head_sq,
    gated_gain_sq,
    out_rows,
    out_cols,
):
    data_count = lax.axis_size("dp")
    data_at = lax.axis_index("dp")
    tensor_at = lax.axis_index("tensor")
    half = (data_at // PAIR) % 2
    core = tensor_at % 2
    row_count = z_weight.shape[0]
    quarter = row_count // 4
    slot_tokens = block_input.shape[1]
    f32, bf16 = jnp.float32, jnp.bfloat16

    share = slot_tokens // 4
    share_at = (core * 2 + tensor_at // 2) * share
    last_bit = dp_bits()[-1]

    def share_of(values):
        return lax.dynamic_slice_in_dim(values, share_at, share, 0)

    def halves_of(weight):
        return halves(weight.astype(bf16), half, 1)

    def rows_of(*pieces):
        return jnp.concatenate(pieces, axis=0)

    whole_numbers = jnp.concatenate(
        [seg_ids[0], jnp.broadcast_to(slot_live, (8 * 128 - slot_tokens,))]
    ).astype(bf16).reshape(-1, 128)
    dt_rows_low = dt_weight.astype(bf16).T
    bc_mine = lax.dynamic_slice_in_dim(bc_weight.astype(bf16), tensor_at * quarter, quarter, 0)
    small = rows_of(bc_mine.reshape(-1, 128), dt_rows_low.reshape(-1, 128))
    small_count = small.shape[0]
    x_mine, x_other = halves_of(x_weight)
    small_far = swap(rows_of(small, whole_numbers), "dp", PAIR)
    x_far = swap(x_other, "dp", PAIR)
    small_far, x_far, x_mine, small, z_weight, out_weight, block_input, out_grad = step(
        small_far, x_far, x_mine, small, z_weight, out_weight, block_input, out_grad
    )

    far_numbers = small_far[small_count:].astype(jnp.int32)
    segments = jnp.stack([seg_ids[0], far_numbers.reshape(-1)[:slot_tokens]])
    live = jnp.stack([slot_live[0], far_numbers[-1, 0]]).astype(f32)
    small = jnp.stack([small, small_far[:small_count]])
    for bit in dp_bits()[1:-1]:
        small = rows_of(small, swap(small, "dp", bit))
    x_held, x_got = gather_middle(rows_of(x_mine, x_far))
    x_first = swap(x_held, "dp", last_bit)
    z_mine, z_other = halves_of(z_weight)
    out_mine, out_other = halves_of(out_weight)
    in_share, grad_share = share_of(block_input[0]), share_of(out_grad[0])
    marks, doc_rows = document_marks(segments)
    taps_x, _ = halves(conv_x, half, 1)
    per_head, _ = halves(head_params, half, 1)
    gain_inner, _ = halves(gated_gain, half, 0)
    head_count = per_head.shape[1]
    head_rows = jnp.pad(per_head, ((0, 5), (0, 128 - head_count)))
    vectors = jnp.concatenate(
        [taps_x, gain_inner[None], jnp.repeat(per_head[2], WIDTH)[None], jnp.zeros((2, taps_x.shape[1]))]
    )
    marks, doc_rows, head_rows, vectors, z_mine, out_mine = step(
        marks, doc_rows, head_rows, vectors, z_mine, out_mine
    )
    gain_rel = to_relative(norm_gain, data_at)
    own_rel = to_relative(block_input[0], data_at).astype(f32)
    x_got, x_first, small, z_other, in_share, grad_share, out_other, own_rel, marks, vectors = step(
        x_got, x_first, small, z_other, in_share, grad_share, out_other, own_rel, marks, vectors
    )

    x_second = swap(x_got, "dp", last_bit)
    small = rows_of(small, swap(small, "dp", last_bit))
    z_far = swap(z_other, "dp", PAIR)
    in_far = swap(in_share, "dp", PAIR)
    bc_piece_rows = quarter * bc_weight.shape[1] // 128
    bc_held = small[:, :bc_piece_rows].reshape(data_count, quarter, -1)
    x_second, small, z_far, in_far, z_mine, grad_share, out_other, bc_held = step(
        x_second, small, z_far, in_far, z_mine, grad_share, out_other, bc_held
    )

    z_held, z_got = gather_middle(rows_of(z_mine, z_far))
    z_first = swap(z_held, "dp", last_bit)
    in_far = join_halves(in_far, swap(in_far, "tensor", 2), tensor_at // 2, 0)
    bc_held = join_halves(bc_held, swap(bc_held, "tensor", 1), core, 1)
    low_x = rows_of(x_held, x_got, x_first, x_second)
    z_got, z_first, in_far, bc_held, grad_share, out_other, low_x = step(
        z_got, z_first, in_far, bc_held, grad_share, out_other, low_x
    )

    z_second = swap(z_got, "dp", last_bit)
    out_far = swap(out_other, "dp", PAIR)
    grad_far = swap(grad_share, "dp", PAIR)
    in_far = join_halves(in_far, swap(in_far, "tensor", 1), core, 0)
    bc_held = join_halves(bc_held, swap(bc_held, "tensor", 2), tensor_at // 2, 1)
    low_bc = bc_held.reshape(data_count * row_count, -1)
    in_rel = jnp.stack([own_rel, to_relative(in_far, data_at).astype(f32)])
    mean_square = jnp.mean(in_rel * in_rel, axis=-1, keepdims=True)
    normed_low = (in_rel * lax.rsqrt(mean_square + norm_eps) * gain_rel).astype(bf16)
    z_second, out_far, grad_far, normed_low = step(z_second, out_far, grad_far, normed_low)
    low_z = rows_of(z_held, z_got, z_first, z_second)
    out_held, out_got = gather_middle(rows_of(out_mine, out_far))
    out_first = swap(out_held, "dp", last_bit)
    grad_far = join_halves(grad_far, swap(grad_far, "tensor", 2), tensor_at // 2, 0)
    low_out = rows_of(out_held, out_got, out_first, swap(out_got, "dp", last_bit))
    grad_far = join_halves(grad_far, swap(grad_far, "tensor", 1), core, 0)
    both_grad = jnp.stack([out_grad[0], grad_far])

    low_dt = (
        small[:, bc_piece_rows:].reshape(data_count, dt_weight.shape[1], row_count).transpose(1, 0, 2)
    ).reshape(dt_weight.shape[1], -1)
    low_dt, _ = halves(low_dt, half, 0)
    low_dt = jnp.pad(low_dt, ((0, 128 - head_count), (0, 0)))
    normed_flat = normed_low.reshape(-1, normed_low.shape[-1])
    tokens = normed_flat.shape[0]

    def per_slot(values):
        return values.reshape(2, slot_tokens, -1)

    bc_raw = per_slot(jnp.dot(normed_flat, low_bc, preferred_element_type=f32))
    dt_raw = per_slot(rows_times(normed_flat, low_dt))
    x_raw = per_slot(jnp.dot(normed_flat, low_x, preferred_element_type=f32))
    gate_z = per_slot(jnp.dot(normed_flat, low_z, preferred_element_type=f32))
    common = (marks, doc_rows, bc_raw, dt_raw, conv_bc, head_rows, x_raw, gate_z, vectors)
    scaled_both, scanned, square_parts = mixer_forward(common)
    scaled_low = scaled_both.reshape(tokens, -1)

    projected = per_slot(rows_times(scaled_low, low_out))
    cot_rel = to_relative(both_grad, data_at) * live.astype(bf16)[:, None, None]
    totals = jnp.stack([jnp.sum(square_parts, axis=-1), jnp.sum(cot_rel.astype(f32) * projected, axis=-1)], axis=1)
    totals = totals + swap(totals, "tensor", 1)
    _, leaving = kept_and_sent(projected, tensor_at, 1, bf16)
    arriving = swap(after(leaving, totals), "tensor", 1)
    totals = totals + swap(totals, "tensor", 2)
    totals = totals + swap(totals, "dp", PAIR)[::-1]
    total_squares, rms_grad = totals[:, 0], totals[:, 1]
    inv_rms = lax.rsqrt(total_squares / INNER + norm_eps)
    squares_grad = rms_grad * -0.5 * inv_rms * inv_rms * inv_rms / INNER
    proj_grad = (cot_rel.astype(f32) * inv_rms[:, :, None]).astype(bf16).reshape(tokens, -1)
    scaled_grad = per_slot(jnp.dot(proj_grad, low_out, preferred_element_type=f32))

    part = low_out.shape[0] // 4
    middle_bit = dp_bits()[-2]

    def across(value, bit):
        return swap(value, "dp", bit)

    out_sent = [gradient_rows(proj_grad, scaled_low, place, bf16) for place in (3, 2)]
    out_passed, out_kept = [swap(value, "dp", last_bit) for value in out_sent]
    gradients = (
        after(scaled_grad, *out_sent, arriving),
        jnp.broadcast_to(squares_grad[:, :, None], (2, slot_tokens, 8)),
    )
    backward = mixer_backward(common, scanned, *gradients, 0)
    proj_later, out_passed, projected, *backward = step(proj_grad, out_passed, projected, *backward)
    shared, _ = kept_and_sent(projected, tensor_at, 1, bf16)
    shared, leaving = kept_and_sent(shared + arriving.astype(f32), tensor_at, 2, bf16)
    out_middle = gradient_rows(proj_later, scaled_low, 1, bf16, out_passed)
    out_middle, leaving, *backward = step(out_middle, leaving, *backward)
    out_got = across(out_middle, middle_bit)
    arriving = swap(leaving, "tensor", 2)
    inv_mine = lax.dynamic_slice_in_dim(inv_rms[0], share_at, share, 0)
    in_mine = to_relative(share_of(block_input[0]), data_at).astype(f32)
    cot_mine = to_relative(share_of(out_grad[0]), data_at).astype(f32) * live[0]
    z_both, x_both, bc_grad_part, dt_both, vector_terms, taps_bc_terms, head_terms = mixer_backward(
        common, scanned, *gradients, 1, backward
    )
    x_both, z_both, bc_grad_part, out_kept, arriving = step(
        x_both, z_both, bc_grad_part, out_kept, arriving
    )
    vector_terms = jnp.sum(vector_terms, axis=0)
    convx_slot, gated_slot = vector_terms[:4], vector_terms[4]
    convbc_part = jnp.sum(taps_bc_terms, axis=0)[:4]
    head_slot = jnp.concatenate(
        [
            jnp.sum(head_terms, axis=0)[:2, :head_count],
            jnp.sum(vector_terms[5].reshape(head_count, -1), axis=1)[None],
        ]
    )
    bc_kept, bc_leaving = kept_and_sent(bc_grad_part, tensor_at, 1, f32)
    bc_arriving = swap(bc_leaving, "tensor", 1)
    z_low = z_both.reshape(tokens, -1)
    x_low = x_both.reshape(tokens, -1)
    dt_low = dt_both.astype(bf16).reshape(tokens, -1)
    matrices = (low_z, low_x, low_dt)
    x_sent = gradient_rows(normed_flat, x_low, 3, bf16)
    x_low, z_low, x_sent, bc_arriving, out_got = step(x_low, z_low, x_sent, bc_arriving, out_got)

    x_passed = swap(x_sent, "dp", last_bit)
    bc_kept, bc_leaving = kept_and_sent(bc_kept + bc_arriving, tensor_at, 2, f32)
    bc_arriving = swap(bc_leaving, "tensor", 2)
    x_low, z_low, bc_leaving = step(x_low, z_low, bc_leaving)
    z_sent = gradient_rows(normed_flat, z_low, 3, bf16)
    both_sent = jnp.concatenate(
        [gradient_rows(normed_flat, values, 2, bf16) for values in (x_low, z_low)], axis=0
    )
    input_leaving = input_terms(1 - core, z_low, x_low, dt_low, *matrices)
    x_low, z_low, x_passed, z_sent, both_sent, input_leaving, bc_arriving = step(
        x_low, z_low, x_passed, z_sent, both_sent, input_leaving, bc_arriving
    )

    x_middle = gradient_rows(normed_flat, x_low, 1, bf16, x_passed)
    x_got = across(x_middle, middle_bit)
    z_passed = swap(z_sent, "dp", last_bit)
    input_arriving = swap(input_leaving, "tensor", 1)
    bc_kept = bc_kept + bc_arriving
    bc_far = swap(bc_kept[1], "dp", PAIR)
    x_low, z_low, x_middle, bc_kept, arriving = step(x_low, z_low, x_middle, bc_kept, arriving)
    shared = shared + arriving.astype(f32)
    shared_leaving = low_bits(shared[1])
    out_mine, out_leaving = middle_sum(gradient_rows(proj_later, scaled_low, 0, f32, out_kept), out_got)
    x_low, z_low, bc_far, shared_leaving, out_mine, out_leaving = step(
        x_low, z_low, bc_far, shared_leaving, out_mine, out_leaving
    )
    out_far = across(out_leaving, PAIR)
    projected_far = across(shared_leaving, PAIR)
    input_kept = input_terms(core, z_low, x_low, dt_low, *matrices)
    x_low, z_low, input_kept, z_passed, input_arriving, out_far, projected_far, both_sent = step(
        x_low, z_low, input_kept, z_passed, input_arriving, out_far, projected_far, both_sent
    )

    z_middle = gradient_rows(normed_flat, z_low, 1, bf16, z_passed)
    z_got = across(z_middle, middle_bit)
    both_kept = swap(both_sent, "dp", last_bit)
    bc_low_mine = (bc_kept[0] + bc_far).astype(bf16)
    bc_far = swap(bc_low_mine, "tensor", 2)
    x_low, z_low, z_middle, bc_low_mine = step(x_low, z_low, z_middle, bc_low_mine)
    input_kept, input_leaving = kept_and_sent(input_kept + input_arriving, tensor_at, 2, bf16)
    bc_far, input_kept, input_leaving = step(bc_far, input_kept, input_leaving)

    input_arriving = swap(input_leaving, "tensor", 2)
    bc_low = join_halves(bc_low_mine, bc_far, tensor_at // 2, 0)
    bc_far = swap(bc_low, "tensor", 1)
    dt_part = tokens_out(dt_low, normed_flat)[:head_count]
    bc_far, dt_part = step(bc_far, dt_part)

    bc_low = join_halves(bc_low, bc_far, core, 0)
    bc_columns = bc_low.shape[1] // 4
    bc_part = tokens_out(
        lax.dynamic_slice_in_dim(bc_low, tensor_at * bc_columns, bc_columns, 1), normed_low[0]
    )
    held = jnp.concatenate([bc_part, dt_part], axis=0)
    held = jnp.stack(
        [held[:, block * row_count : (block + 1) * row_count] for block in range(data_count)]
    )
    count = held.shape[0] // 2
    held = held[:count] + swap(held[count:], "dp", last_bit)
    projected_mine = shared[0] + flip_pairs(projected_far.astype(f32))
    output = from_relative((in_mine + inv_mine[:, None] * projected_mine).astype(bf16), data_at)
    output_far = swap(output, "tensor", 2)
    out_share = join_halves(out_mine, out_far.astype(f32), half, 1)
    x_got, held, output, out_share = step(x_got, held, output, out_share)
    for bit in reversed(dp_bits()[1:-1]):
        count = held.shape[0] // 2
        held = held[:count] + swap(held[count:], "dp", bit)
    x_terms = gradient_rows(normed_flat, x_low, 0, f32, both_kept[:part])
    z_terms = gradient_rows(normed_flat, z_low, 0, f32, both_kept[part:])
    x_mine, x_leaving = middle_sum(x_terms, x_got)
    input_arriving, held, z_terms, x_leaving, z_got, output_far = step(
        input_arriving, held, z_terms, x_leaving, z_got, output_far
    )

    small_far = swap(held[1], "dp", PAIR)
    input_mine = input_kept + input_arriving.astype(f32)
    input_far = swap(low_bits(input_mine[1]), "dp", PAIR)
    z_mine, z_leaving = middle_sum(z_terms, z_got)
    both_far = across(jnp.concatenate([x_leaving, z_leaving], axis=0), PAIR)
    input_far, small_far = step(input_far, small_far)
    output = join_halves(output, output_far, tensor_at // 2, 0)
    normed_grad = (
        input_mine[0] + flip_pairs(input_far.astype(f32)) + rows_times(bc_low_mine, low_bc)
    )

    _, norm_pull = jax.vjp(norm_input, in_mine, gain_rel)
    block_grad, gain_slot = norm_pull(normed_grad)
    input_grad = from_relative((cot_mine + block_grad).astype(bf16), data_at)
    both_far, gain_slot, small_far, output = step(both_far, gain_slot, small_far, output)
    output = join_halves(output, swap(output, "tensor", 1), core, 0)
    x_share = join_halves(x_mine, both_far[: x_mine.shape[0]].astype(f32), half, 1)
    z_share = join_halves(z_mine, both_far[x_mine.shape[0] :].astype(f32), half, 1)

    bc_share = held[0, :bc_columns] + small_far[:bc_columns]
    dt_share = join_halves(held[0, bc_columns:], small_far[bc_columns:], half, 0).T
    bc_share = join_halves(bc_share, swap(bc_share, "tensor", 1), core, 0)
    bc_share = join_halves(bc_share, swap(bc_share, "tensor", 2), tensor_at // 2, 0).T

    def in_half(values):
        return join_halves(values, jnp.zeros_like(values), half, values.ndim - 1)

    def packed_sum(pieces, axis_bits):
        sizes = [piece.size for piece in pieces]
        flat = jnp.concatenate([piece.reshape(-1) for piece in pieces])
        fill = -flat.size % 128
        flat = jnp.pad(flat, (0, fill)).reshape(-1, 128)
        for axis, bits in axis_bits:
            flat = add_over(flat, axis, bits)
        flat = flat.reshape(-1)
        result, at = [], 0
        for piece, size in zip(pieces, sizes):
            result.append(flat[at : at + size].reshape(piece.shape))
            at += size
        return result

    norm_sum, convbc_sum = packed_sum(
        [from_relative(gain_slot, data_at), convbc_part], [("tensor", (1, 2))]
    )
    z_share, bc_share, norm_sum, convbc_sum = step(z_share, bc_share, norm_sum, convbc_sum)
    z_square = z_share * z_share + tiny_eps
    x_square = x_share * x_share + tiny_eps
    bc_square = bc_share * bc_share + tiny_eps
    dt_square = dt_share * dt_share + tiny_eps
    out_square = out_share * out_share + tiny_eps
    row_sums = jnp.stack(
        [
            jnp.sum(z_square, axis=1),
            jnp.sum(x_square, axis=1),
            jnp.sum(dt_square, axis=1),
            jnp.sum(out_square, axis=1),
        ]
    )
    z_row_sum, x_row_sum, dt_row_sum, out_row_sum = add_over(row_sums, "tensor", (1, 2))
    bc_row_sum = jnp.sum(bc_square, axis=1)

    (
        norm_total,
        convbc_total,
        gated_total,
        convx_total,
        head_total,
        z_col_sum,
        x_col_sum,
        bc_col_sum,
        dt_col_sum,
        out_col_sum,
    ) = packed_sum(
        [
            norm_sum,
            convbc_sum,
            in_half(gated_slot),
            in_half(convx_slot),
            in_half(head_slot),
            jnp.sum(z_square, axis=0),
            jnp.sum(x_square, axis=0),
            jnp.sum(bc_square, axis=0),
            jnp.sum(dt_square, axis=0),
            jnp.sum(out_square, axis=0),
        ],
        [("dp", dp_bits())],
    )
    z_rows_new = mix_state(z_rows, z_row_sum / INNER)
    x_rows_new = mix_state(x_rows, x_row_sum / INNER)
    bc_rows_new = mix_state(bc_rows, bc_row_sum / (2 * STATE))
    dt_rows_new = mix_state(dt_rows, dt_row_sum / HEADS)
    out_rows_new = mix_state(out_rows, out_row_sum / INNER)
    z_cols_new = mix_state(z_cols, z_col_sum / D)
    x_cols_new = mix_state(x_cols, x_col_sum / D)
    bc_cols_new = mix_state(bc_cols, bc_col_sum / D)
    dt_cols_new = mix_state(dt_cols, dt_col_sum / D)
    out_cols_new = mix_state(out_cols, out_col_sum / D)
    norm_second = mix_state(norm_gain_sq, norm_total * norm_total + tiny_eps)
    gated_second = mix_state(gated_gain_sq, gated_total * gated_total + tiny_eps)
    convx_second = mix_state(conv_x_sq, convx_total * convx_total + tiny_eps)
    convbc_second = mix_state(conv_bc_sq, convbc_total * convbc_total + tiny_eps)
    head_second = mix_state(head_sq, head_total * head_total + tiny_eps)
    norm_unit = norm_total * lax.rsqrt(norm_second)
    gated_unit = gated_total * lax.rsqrt(gated_second)
    convx_unit = convx_total * lax.rsqrt(convx_second)
    convbc_unit = convbc_total * lax.rsqrt(convbc_second)
    head_unit = head_total * lax.rsqrt(head_second)
    z_unit = z_share * lax.rsqrt(z_rows_new[:, None] * z_cols_new[None, :])
    x_unit = x_share * lax.rsqrt(x_rows_new[:, None] * x_cols_new[None, :])
    bc_unit = bc_share * lax.rsqrt(bc_rows_new[:, None] * bc_cols_new[None, :])
    dt_unit = dt_share * lax.rsqrt(dt_rows_new[:, None] * dt_cols_new[None, :])
    out_unit = out_share * lax.rsqrt(out_rows_new[:, None] * out_cols_new[None, :])
    tensor_count = lax.axis_size("tensor")
    unit_sums = jnp.stack(
        [
            jnp.sum(z_unit * z_unit),
            jnp.sum(x_unit * x_unit),
            jnp.sum(bc_unit * bc_unit) / tensor_count,
            jnp.sum(dt_unit * dt_unit),
            jnp.sum(out_unit * out_unit),
            jnp.sum(gated_unit * gated_unit) / data_count,
            jnp.sum(convx_unit * convx_unit) / data_count,
            jnp.sum(head_unit * head_unit) / data_count,
        ]
    )
    unit_sums = jnp.broadcast_to(unit_sums[:, None], (8, 128))
    unit_sums = add_over(unit_sums, "tensor", (1, 2))
    unit_sums, input_grad, output = step(unit_sums, input_grad, output)
    input_far = swap(input_grad, "tensor", 2)
    unit_sums = add_over(unit_sums, "dp", dp_bits())
    input_far, unit_sums = step(input_far, unit_sums)
    input_grad = join_halves(input_grad, input_far, tensor_at // 2, 0)
    input_grad = join_halves(input_grad, swap(input_grad, "tensor", 1), core, 0)
    (
        z_total,
        x_total,
        bc_total_sq,
        dt_total,
        out_total,
        gated_sq_total,
        convx_sq_total,
        head_sq_total,
    ) = unit_sums[:, 0]
    norm_sq_total = jnp.sum(norm_unit * norm_unit)
    convbc_sq_total = jnp.sum(convbc_unit * convbc_unit)
    in_rate = D ** (-0.5)
    out_rate = INNER ** (-0.5)
    z_upd = -in_rate * normalized(z_unit, z_total, D * INNER)
    x_upd = -in_rate * normalized(x_unit, x_total, D * INNER)
    bc_upd = -in_rate * normalized(bc_unit, bc_total_sq, D * 2 * STATE)
    dt_upd = -in_rate * normalized(dt_unit, dt_total, D * HEADS)
    out_upd = -out_rate * normalized(out_unit, out_total, D * INNER)
    norm_upd = -vector_rate * normalized(norm_unit, norm_sq_total, D)
    gated_upd = -vector_rate * normalized(gated_unit, gated_sq_total, INNER)
    convx_upd = -vector_rate * normalized(convx_unit, convx_sq_total, KCONV * INNER)
    convbc_upd = -vector_rate * normalized(convbc_unit, convbc_sq_total, KCONV * 2 * STATE)
    head_upd = -vector_rate * normalized(head_unit, head_sq_total, 3 * HEADS)
    return (
        output[None],
        input_grad[None],
        norm_total,
        norm_upd,
        norm_second,
        z_share,
        z_upd,
        z_rows_new,
        z_cols_new,
        x_share,
        x_upd,
        x_rows_new,
        x_cols_new,
        bc_share,
        bc_upd,
        bc_rows_new,
        bc_cols_new,
        dt_share,
        dt_upd,
        dt_rows_new,
        dt_cols_new,
        convx_total,
        convx_upd,
        convx_second,
        convbc_total,
        convbc_upd,
        convbc_second,
        head_total,
        head_upd,
        head_second,
        gated_total,
        gated_upd,
        gated_second,
        out_share,
        out_upd,
        out_rows_new,
        out_cols_new,
    )


def solution(mesh):
    in_specs = (
        P("dp", None, None),
        P("dp", None, None),
        P("dp", None),
        P("dp"),
        P(),
        P("dp", "tensor"),
        P("dp", "tensor"),
        P("dp", None),
        P("dp", "tensor"),
        P(None, "tensor"),
        P(),
        P(None, "tensor"),
        P("tensor"),
        P("dp", "tensor"),
        P(),
        P("dp"),
        P("tensor"),
        P("dp"),
        P("tensor"),
        P("dp"),
        P(),
        P("dp"),
        P("tensor"),
        P(None, "tensor"),
        P(),
        P(None, "tensor"),
        P("tensor"),
        P("dp"),
        P("tensor"),
    )
    out_specs = (
        P("dp", None, None),
        P("dp", None, None),
        P(),
        P(),
        P(),
        P("dp", "tensor"),
        P("dp", "tensor"),
        P("dp"),
        P("tensor"),
        P("dp", "tensor"),
        P("dp", "tensor"),
        P("dp"),
        P("tensor"),
        P("dp", None),
        P("dp", None),
        P("dp"),
        P(),
        P("dp", "tensor"),
        P("dp", "tensor"),
        P("dp"),
        P("tensor"),
        P(None, "tensor"),
        P(None, "tensor"),
        P(None, "tensor"),
        P(),
        P(),
        P(),
        P(None, "tensor"),
        P(None, "tensor"),
        P(None, "tensor"),
        P("tensor"),
        P("tensor"),
        P("tensor"),
        P("dp", "tensor"),
        P("dp", "tensor"),
        P("dp"),
        P("tensor"),
    )
    return jax.shard_map(shards, mesh=mesh, in_specs=in_specs, out_specs=out_specs, check_vma=False)
```

```python
import jax
import jax.numpy as jnp
from jax import lax
from jax.experimental import pallas as pl
from jax.experimental.pallas import tpu as pltpu
from jax.sharding import PartitionSpec as P

D = 2048
HEADS = 64
STATE = 128
INNER = 4096
KCONV = 4


norm_eps = 1e-05
decay_rate = 0.5
tiny_eps = 1e-30
unit_eps = 1e-06
vector_rate = 0.05


LANES = 128
PART = 256
WIDTH = 64


def cost_of(micros):
    return pl.CostEstimate(flops=micros * 1_000_000_000, bytes_accessed=1 << 20, transcendentals=0)


def two_parts(values):
    high = values.astype(jnp.bfloat16)
    return high, (values - high.astype(jnp.float32)).astype(jnp.bfloat16)


def plain(left, right):
    return lax.dot_general(
        left, right, (((1,), (0,)), ((), ())), preferred_element_type=jnp.float32
    )


def turned(left, right):
    return lax.dot_general(
        left, right, (((1,), (1,)), ((), ())), preferred_element_type=jnp.float32
    )


def fine(product, left, right):
    left_high, left_low = two_parts(left)
    right_high, right_low = two_parts(right)
    return (
        product(left_high, right_high)
        + product(left_high, right_low)
        + product(left_low, right_high)
    )


def running_sum(values, backward):
    rows = lax.broadcasted_iota(jnp.int32, (PART, PART), 0)
    columns = lax.broadcasted_iota(jnp.int32, (PART, PART), 1)
    within = (rows <= columns) if backward else (rows >= columns)
    ones = within.astype(jnp.float32).astype(jnp.bfloat16)

    def inside(block):
        high, rest = block.astype(jnp.bfloat16), block
        total = plain(ones, high)
        rest = block - high.astype(jnp.float32)
        for _ in range(2):
            part = rest.astype(jnp.bfloat16)
            total = total + plain(ones, part)
            rest = rest - part.astype(jnp.float32)
        return total

    blocks = [inside(values[:PART]), inside(values[PART:])]
    if backward:
        blocks[0] = blocks[0] + blocks[1][0:1]
    else:
        blocks[1] = blocks[1] + blocks[0][PART - 1 : PART]
    return jnp.concatenate(blocks, axis=0)


def sigmoid(values):
    return 1.0 / (1.0 + jnp.exp(-values))


def conv_rows(values, taps, same):
    result = taps[0:1] * values
    for offset in range(1, 4):
        shifted = pltpu.roll(values, offset, 0)
        result = result + taps[offset : offset + 1] * (shifted * same[offset - 1])
    return result


def conv_rows_back(grad, values, taps, same):
    length = values.shape[0]
    result = taps[0:1] * grad
    tap_rows = [jnp.sum(grad * values, axis=0, keepdims=True)]
    for offset in range(1, 4):
        kept = grad * same[offset - 1]
        result = result + pltpu.roll(taps[offset : offset + 1] * kept, length - offset, 0)
        tap_rows.append(
            jnp.sum(kept * pltpu.roll(values, offset, 0), axis=0, keepdims=True)
        )
    return result, tap_rows


def softplus(values):
    return jnp.maximum(values, 0.0) + jnp.log1p(jnp.exp(-jnp.abs(values)))


def marks_of(marks_ref):
    marks = marks_ref[0]
    same = [marks[:, place : place + 1] for place in (1, 2, 3)]
    return marks[:, 0:1], same, marks[:, 4:5]


def prepare(transposed, marks_ref, row_ref, bc_ref, dt_ref, taps_bc_ref, head_ref,
            bc_pre_ref, bc_ref_out, dt_out, cum_wide, dt_wide, cum_rows, score, bias):
    doc, same, _ = marks_of(marks_ref)
    bc_pre = conv_rows(bc_ref[0], taps_bc_ref[...], same)
    bc = bc_pre * sigmoid(bc_pre)
    bc_pre_ref[...] = bc_pre
    bc_ref_out[...] = bc
    b_mat, c_mat = bc[:, :LANES], bc[:, LANES:]
    first, second = slice(0, PART), slice(PART, 2 * PART)
    for place, (out_rows, in_rows) in enumerate(((first, first), (second, second), (second, first))):
        if transposed:
            score[place] = fine(turned, b_mat[in_rows], c_mat[out_rows])
        else:
            score[place] = fine(turned, c_mat[out_rows], b_mat[in_rows])
    rows = lax.broadcasted_iota(jnp.int32, (PART, PART), 0)
    columns = lax.broadcasted_iota(jnp.int32, (PART, PART), 1)
    causal = (rows <= columns) if transposed else (rows >= columns)
    doc_row = row_ref[0][0:1]
    for place, part in enumerate((first, second)):
        seen = causal & (doc[part] == doc_row[:, part])
        bias[place] = jnp.where(seen, 0.0, -1e30)
    step = softplus(dt_ref[0] + head_ref[0:1])
    decay = step * -jnp.exp(head_ref[1:2])
    total = running_sum(decay, False)
    dt_out[...] = step
    flipped = total.T
    lane = lax.broadcasted_iota(jnp.int32, (2 * PART, LANES), 1)
    for pair in range(cum_wide.shape[0]):
        one, two = 2 * pair, 2 * pair + 1
        cum_wide[pair] = jnp.where(lane < WIDTH, total[:, one : one + 1], total[:, two : two + 1])
        dt_wide[pair] = jnp.where(lane < WIDTH, step[:, one : one + 1], step[:, two : two + 1])
        cum_rows[one] = flipped[one : one + 1]
        cum_rows[two] = flipped[two : two + 1]


def edge_weights(wide, in_last):
    edge = wide[PART - 1 : PART]
    after = jnp.exp(wide[PART:] - edge) * in_last[PART:]
    before = jnp.exp(edge - wide[:PART]) * in_last[:PART]
    return after, before


def forward_body(marks_ref, row_ref, bc_ref, dt_ref, taps_bc_ref, head_ref, x_ref, z_ref, vec_ref,
                 scaled_ref, scan_ref, squares_ref,
                 bc_pre, bc_act, dt_act, cum_wide, dt_wide, cum_rows, score, bias):
    pair = pl.program_id(1)

    @pl.when(pair == 0)
    def _():
        prepare(False, marks_ref, row_ref, bc_ref, dt_ref, taps_bc_ref, head_ref,
                bc_pre, bc_act, dt_act, cum_wide, dt_wide, cum_rows, score, bias)
        squares_ref[...] = jnp.zeros_like(squares_ref)

    _, same, in_last = marks_of(marks_ref)
    vec = vec_ref[...]
    pre = conv_rows(x_ref[0], vec[0:4], same)
    values = pre * sigmoid(pre)
    wide = cum_wide[pair]
    stepped = dt_wide[pair] * values
    high, low_part = two_parts(stepped)
    both = jnp.concatenate([high, low_part], axis=1)
    lane = lax.broadcasted_iota(jnp.int32, (PART, LANES), 1)
    blocks = []
    for place in range(2):
        part = slice(place * PART, (place + 1) * PART)
        answers = []
        for k in range(2):
            row = cum_rows[2 * pair + k][:, part]
            kernel = jnp.exp(wide[part, k * WIDTH : k * WIDTH + 1] - row + bias[place])
            mixing_high, mixing_low = two_parts(score[place] * kernel)
            answer = plain(mixing_high, both[part])
            answers.append(
                answer[:, :LANES] + answer[:, LANES:] + plain(mixing_low, high[part])
            )
        blocks.append(jnp.where(lane < WIDTH, answers[0], answers[1]))
    after, before = edge_weights(wide, in_last)
    blocks[1] = blocks[1] + after * fine(plain, score[2], before * stepped[:PART])
    scanned = jnp.concatenate(blocks, axis=0)
    scan_ref[0] = scanned
    gate = z_ref[0]
    gated = (scanned + vec[5:6] * values) * (gate * sigmoid(gate))
    squares_ref[0] = squares_ref[0] + gated * gated
    scaled_ref[0] = (gated * vec[4:5]).astype(scaled_ref.dtype)


def backward_body(marks_ref, row_ref, bc_ref, dt_ref, taps_bc_ref, head_ref, x_ref, z_ref, vec_ref,
                  scan_ref, grad_ref, sq_grad_ref,
                  z_out, x_out, bc_out, dt_out, vec_out, taps_bc_out, head_out,
                  bc_pre, bc_act, dt_act, cum_wide, dt_wide, cum_rows, score, bias,
                  score_grad, from_rows, from_columns, from_in):
    pair = pl.program_id(1)

    @pl.when(pair == 0)
    def _():
        prepare(True, marks_ref, row_ref, bc_ref, dt_ref, taps_bc_ref, head_ref,
                bc_pre, bc_act, dt_act, cum_wide, dt_wide, cum_rows, score, bias)
        score_grad[...] = jnp.zeros_like(score_grad)
        from_rows[...] = jnp.zeros_like(from_rows)
        from_columns[...] = jnp.zeros_like(from_columns)
        from_in[...] = jnp.zeros_like(from_in)

    _, same, in_last = marks_of(marks_ref)
    vec = vec_ref[...]
    taps, gain, skip = vec[0:4], vec[4:5], vec[5:6]
    x_raw = x_ref[0]
    pre = conv_rows(x_raw, taps, same)
    pre_sig = sigmoid(pre)
    values = pre * pre_sig
    wide = cum_wide[pair]
    step = dt_wide[pair]
    stepped = step * values
    gate = z_ref[0]
    gate_sig = sigmoid(gate)
    gate_act = gate * gate_sig
    scanned = scan_ref[0]
    mixed = scanned + skip * values
    gated = mixed * gate_act
    scaled_grad = grad_ref[0]
    gated_grad = scaled_grad * gain + 2.0 * sq_grad_ref[0][:, 0:1] * gated
    z_out[0] = (gated_grad * mixed * (gate_sig * (1.0 + gate * (1.0 - gate_sig)))).astype(z_out.dtype)
    grad = gated_grad * gate_act
    rows = [
        None, None, None, None,
        jnp.sum(scaled_grad * gated, axis=0, keepdims=True),
        jnp.sum(grad * values, axis=0, keepdims=True),
    ]
    high, low_part = two_parts(grad)
    both = jnp.concatenate([high, low_part], axis=1)
    lane = lax.broadcasted_iota(jnp.int32, (PART, LANES), 1)

    def add_exponents(head, out_part, in_part, terms):
        from_rows[head, :, out_part] += jnp.sum(terms, axis=0, keepdims=True)
        gone = jnp.sum(terms, axis=1, keepdims=True)
        from_columns[in_part] += jnp.where(lane == head, gone, 0.0)

    blocks = []
    for place in range(2):
        part = slice(place * PART, (place + 1) * PART)
        answers = []
        total = score_grad[place]
        for k in range(2):
            row = cum_rows[2 * pair + k][:, part]
            kernel = jnp.exp(row - wide[part, k * WIDTH : k * WIDTH + 1] + bias[place])
            mixing = score[place] * kernel
            mixing_high, mixing_low = two_parts(mixing)
            answer = plain(mixing_high, both[part])
            answers.append(
                answer[:, :LANES] + answer[:, LANES:] + plain(mixing_low, high[part])
            )
            own = (lane < WIDTH) if k == 0 else (lane >= WIDTH)
            own_high, own_low = two_parts(jnp.where(own, stepped[part], 0.0))
            pulled = turned(
                jnp.concatenate([own_high, own_high], axis=1), both[part]
            ) + turned(own_low, high[part])
            total = total + pulled * kernel
            add_exponents(2 * pair + k, part, part, pulled * mixing)
        score_grad[place] = total
        blocks.append(jnp.where(lane < WIDTH, answers[0], answers[1]))
    after, before = edge_weights(wide, in_last)
    late = after * grad[PART:]
    early = before * stepped[:PART]
    blocks[0] = blocks[0] + before * fine(plain, score[2], late)
    for k in range(2):
        own = (lane < WIDTH) if k == 0 else (lane >= WIDTH)
        pulled = fine(turned, jnp.where(own, early, 0.0), late)
        score_grad[2] = score_grad[2] + pulled
        add_exponents(2 * pair + k, slice(PART, 2 * PART), slice(0, PART), pulled * score[2])
    pulled_in = jnp.concatenate(blocks, axis=0)
    places = lax.broadcasted_iota(jnp.int32, (LANES, LANES), 0) // WIDTH + 2 * pair
    columns = lax.broadcasted_iota(jnp.int32, (LANES, LANES), 1)
    chosen = (places == columns).astype(jnp.float32).astype(jnp.bfloat16)
    chosen = jnp.concatenate([chosen, chosen], axis=0)
    from_in[...] += plain(jnp.concatenate(two_parts(values * pulled_in), axis=1), chosen)
    pre_grad = (skip * grad + step * pulled_in) * (pre_sig * (1.0 + pre * (1.0 - pre_sig)))
    x_grad, rows[:4] = conv_rows_back(pre_grad, x_raw, taps, same)
    x_out[0] = x_grad.astype(x_out.dtype)
    vec_out[0] = jnp.concatenate(rows + [jnp.zeros((2, LANES), jnp.float32)], axis=0)

    @pl.when(pair == pl.num_programs(1) - 1)
    def _():
        steps = dt_act[...]
        rate = -jnp.exp(head_ref[1:2])
        direct = from_in[...]
        heads = from_rows.shape[0]
        arrived = jnp.concatenate(
            [from_rows[head] for head in range(heads)]
            + [jnp.zeros((LANES - heads, 2 * PART), jnp.float32)],
            axis=0,
        ).T
        decay_grad = running_sum(arrived - from_columns[...], True)
        step_grad = (direct + rate * decay_grad) * sigmoid(dt_ref[0] + head_ref[0:1])
        dt_out[0] = step_grad
        head_out[0] = jnp.concatenate(
            [
                jnp.sum(step_grad, axis=0, keepdims=True),
                rate * jnp.sum(decay_grad * steps, axis=0, keepdims=True),
                jnp.zeros((6, LANES), jnp.float32),
            ],
            axis=0,
        )
        b_mat, c_mat = bc_act[:, :LANES], bc_act[:, LANES:]
        first, second, cross = score_grad[0], score_grad[1], score_grad[2]
        b_grad = jnp.concatenate(
            [
                fine(plain, first, c_mat[:PART]) + fine(plain, cross, c_mat[PART:]),
                fine(plain, second, c_mat[PART:]),
            ],
            axis=0,
        )
        c_grad = jnp.concatenate(
            [
                fine(plain, first.T, b_mat[:PART]),
                fine(plain, second.T, b_mat[PART:]) + fine(plain, cross.T, b_mat[:PART]),
            ],
            axis=0,
        )
        shape = bc_pre[...]
        slope = sigmoid(shape)
        slope = slope * (1.0 + shape * (1.0 - slope))
        bc_grad, tap_rows = conv_rows_back(
            jnp.concatenate([b_grad, c_grad], axis=1) * slope, bc_ref[0], taps_bc_ref[...], same
        )
        bc_out[0] = bc_grad
        taps_bc_out[0] = jnp.concatenate(
            tap_rows + [jnp.zeros((4, 2 * LANES), jnp.float32)], axis=0
        )


def slot_block(first, *shape):
    return pl.BlockSpec((1,) + shape, lambda slot, pair: (slot + first, 0, 0))


def whole_block(*shape):
    return pl.BlockSpec(shape, lambda slot, pair: (0,) * len(shape))


def pair_block(first, length):
    return pl.BlockSpec((1, length, LANES), lambda slot, pair: (slot + first, 0, pair))


def common_specs(first, length):
    return [
        slot_block(first, length, 8),
        slot_block(first, 8, length),
        slot_block(first, length, 2 * LANES),
        slot_block(first, length, LANES),
        whole_block(4, 2 * LANES),
        whole_block(8, LANES),
        pair_block(first, length),
        pair_block(first, length),
        pl.BlockSpec((8, LANES), lambda slot, pair: (0, pair)),
    ]


def common_scratch(length, pairs):
    return [
        pltpu.VMEM((length, 2 * LANES), jnp.float32),
        pltpu.VMEM((length, 2 * LANES), jnp.float32),
        pltpu.VMEM((length, LANES), jnp.float32),
        pltpu.VMEM((pairs, length, LANES), jnp.float32),
        pltpu.VMEM((pairs, length, LANES), jnp.float32),
        pltpu.VMEM((2 * pairs, 1, length), jnp.float32),
        pltpu.VMEM((3, PART, PART), jnp.float32),
        pltpu.VMEM((2, PART, PART), jnp.float32),
    ]


def mixer_forward(common, interpret=False):
    slots, length, width = common[6].shape
    pairs = width // LANES
    return pl.pallas_call(
        forward_body,
        grid=(slots, pairs),
        in_specs=common_specs(0, length),
        out_specs=[pair_block(0, length), pair_block(0, length), slot_block(0, length, LANES)],
        out_shape=[
            jax.ShapeDtypeStruct((slots, length, width), jnp.bfloat16),
            jax.ShapeDtypeStruct((slots, length, width), jnp.float32),
            jax.ShapeDtypeStruct((slots, length, LANES), jnp.float32),
        ],
        scratch_shapes=common_scratch(length, pairs),
        cost_estimate=cost_of(16),
        name="mixer_forward",
        interpret=interpret,
    )(*common)


def mixer_backward(common, scanned, scaled_grad, sq_grad, slot, earlier=(), interpret=False):
    slots, length, width = common[6].shape
    pairs = width // LANES
    given = len(common) + 3

    def body(*refs):
        backward_body(*refs[:given], *refs[given + len(earlier) :])

    return pl.pallas_call(
        body,
        grid=(1, pairs),
        in_specs=common_specs(slot, length)
        + [pair_block(slot, length), pair_block(slot, length), slot_block(slot, length, 8)]
        + [pl.BlockSpec(memory_space=pl.ANY) for _ in earlier],
        out_specs=[
            pair_block(slot, length),
            pair_block(slot, length),
            slot_block(slot, length, 2 * LANES),
            slot_block(slot, length, LANES),
            pl.BlockSpec((1, 8, LANES), lambda _, pair: (slot, 0, pair)),
            slot_block(slot, 8, 2 * LANES),
            slot_block(slot, 8, LANES),
        ],
        out_shape=[
            jax.ShapeDtypeStruct((slots, length, width), jnp.bfloat16),
            jax.ShapeDtypeStruct((slots, length, width), jnp.bfloat16),
            jax.ShapeDtypeStruct((slots, length, 2 * LANES), jnp.float32),
            jax.ShapeDtypeStruct((slots, length, LANES), jnp.float32),
            jax.ShapeDtypeStruct((slots, 8, width), jnp.float32),
            jax.ShapeDtypeStruct((slots, 8, 2 * LANES), jnp.float32),
            jax.ShapeDtypeStruct((slots, 8, LANES), jnp.float32),
        ],
        input_output_aliases={given + place: place for place in range(len(earlier))},
        scratch_shapes=common_scratch(length, pairs)
        + [
            pltpu.VMEM((3, PART, PART), jnp.float32),
            pltpu.VMEM((2 * pairs, 1, length), jnp.float32),
            pltpu.VMEM((length, LANES), jnp.float32),
            pltpu.VMEM((length, LANES), jnp.float32),
        ],
        cost_estimate=cost_of(16),
        name="mixer_backward",
        interpret=interpret,
    )(*common, scanned, scaled_grad, sq_grad, *earlier)


def input_body(place_ref, z_ref, x_ref, dt_ref, z_rows_ref, x_rows_ref, dt_rows_ref, *rest):
    del place_ref

    def flat(ref):
        return ref[...].reshape(-1, ref.shape[-1])

    total = (
        turned(flat(z_ref), z_rows_ref[...])
        + turned(flat(x_ref), x_rows_ref[...])
        + plain(flat(dt_ref), dt_rows_ref[...])
    ).reshape(rest[-1].shape)
    for added in rest[:-1]:
        total = total + added[...]
    rest[-1][...] = total


def input_terms(place, z_low, x_low, dt_low, low_z, low_x, low_dt, *added):
    tokens = z_low.shape[0] // 4
    width = low_z.shape[1]
    features = low_z.shape[0]
    block = features // 4

    def by_half(values):
        return values.reshape(2, 2, tokens, -1)

    def half_block(values):
        return pl.BlockSpec((2, 1, tokens, values.shape[1]), lambda at, where: (0, where[0], 0, 0))

    weight = pl.BlockSpec((block, width), lambda at, where: (at, 0))
    out = pl.BlockSpec((2, tokens, block), lambda at, where: (0, 0, at))
    return pl.pallas_call(
        input_body,
        grid_spec=pltpu.PrefetchScalarGridSpec(
            num_scalar_prefetch=1,
            grid=(4,),
            in_specs=[
                half_block(z_low),
                half_block(x_low),
                half_block(dt_low),
                weight,
                weight,
                pl.BlockSpec((low_dt.shape[0], block), lambda at, where: (0, at)),
            ]
            + [out] * len(added),
            out_specs=out,
        ),
        out_shape=jax.ShapeDtypeStruct((2, tokens, features), jnp.float32),
        cost_estimate=cost_of(6),
        name="input_terms",
    )(
        place.astype(jnp.int32).reshape(1),
        by_half(z_low),
        by_half(x_low),
        by_half(dt_low),
        low_z,
        low_x,
        low_dt,
        *added,
    )


def document_marks(segments):
    slots, length = segments.shape
    docs = segments.astype(jnp.float32)
    columns = [docs]
    for offset in (1, 2, 3):
        same = (segments[:, offset:] == segments[:, :-offset]).astype(jnp.float32)
        columns.append(jnp.pad(same, ((0, 0), (offset, 0))))
    columns.append((segments == segments[:, PART - 1 : PART]).astype(jnp.float32))
    zero = jnp.zeros_like(docs)
    marks = jnp.stack(columns + [zero] * 3, axis=-1)
    return marks, jnp.broadcast_to(docs[:, None, :], (slots, 8, length))


def norm_input(values, gain):
    mean_square = jnp.mean(values * values, axis=1, keepdims=True)
    return values * lax.rsqrt(mean_square + norm_eps) * gain


def rows_times(left, right):
    return lax.dot_general(
        left, right, (((1,), (1,)), ((), ())), preferred_element_type=jnp.float32
    )


def tokens_out(left, right):
    return lax.dot_general(
        left, right, (((0,), (0,)), ((), ())), preferred_element_type=jnp.float32
    )


def mix_state(old_state, fresh_term):
    return decay_rate * old_state + (1.0 - decay_rate) * fresh_term


def normalized(unit, square_total, entries):
    return unit * lax.rsqrt(square_total / entries + unit_eps)


def swap(value, axis, bit):
    size = lax.axis_size(axis)
    return lax.ppermute(value, axis, [(place, place ^ bit) for place in range(size)])


def add_over(value, axis, bits):
    for bit in bits:
        value = value + swap(value, axis, bit)
    return value


PAIR = 2


def dp_bits():
    count = lax.axis_size("dp")
    rest = [1 << place for place in reversed(range(count.bit_length() - 1)) if 1 << place != PAIR]
    return [PAIR] + rest


def block_masks():
    bits = dp_bits()
    return [
        sum(bit for place, bit in enumerate(bits) if (number >> place) & 1)
        for number in range(lax.axis_size("dp"))
    ]


def place_of(offset):
    return sum(
        ((offset // bit) % 2) << place for place, bit in enumerate(dp_bits())
    )


def to_relative(values, mine):
    blocks = lax.axis_size("dp")
    width = values.shape[-1] // blocks
    return jnp.concatenate(
        [
            lax.dynamic_slice_in_dim(values, (mine ^ mask) * width, width, values.ndim - 1)
            for mask in block_masks()
        ],
        axis=-1,
    )


def from_relative(values, mine):
    blocks = lax.axis_size("dp")
    width = values.shape[-1] // blocks
    return jnp.concatenate(
        [
            lax.dynamic_slice_in_dim(values, place_of(mine ^ block) * width, width, values.ndim - 1)
            for block in range(blocks)
        ],
        axis=-1,
    )


def halves(values, half, axis):
    width = values.shape[axis] // 2
    mine = lax.dynamic_slice_in_dim(values, half * width, width, axis)
    other = lax.dynamic_slice_in_dim(values, (1 - half) * width, width, axis)
    return mine, other


def join_halves(mine, other, half, axis):
    low, high = jnp.where(half == 0, mine, other), jnp.where(half == 0, other, mine)
    return jnp.concatenate([low, high], axis=axis)


def after(value, *others):
    return lax.optimization_barrier((value,) + others)[0] if others else value


def step(*values):
    return lax.optimization_barrier(values)


def gather_middle(held):
    middle = dp_bits()[1:-1]
    for bit in middle[:-1]:
        held = jnp.concatenate([held, swap(held, "dp", bit)], axis=0)
    return held, swap(held, "dp", middle[-1])


def gradient_rows(left, right, place, kind, *added):
    part = left.shape[1] // 4
    total = tokens_out(left[:, place * part : (place + 1) * part], right)
    for value in added:
        total = total + value.astype(jnp.float32)
    return total.astype(kind)


def low_bits(value):
    return value.astype(jnp.bfloat16)


def middle_sum(held, got):
    held = held + got.astype(jnp.float32)
    for bit in reversed(dp_bits()[1:-2]):
        count = held.shape[0] // 2
        sent = swap(low_bits(held[count:]), "dp", bit)
        held = held[:count] + sent.astype(jnp.float32)
    count = held.shape[0] // 2
    return held[:count], low_bits(held[count:])


def kept_and_sent(held, tensor_at, bit, kind):
    mine, other = halves(held, (tensor_at // bit) % 2, 1)
    return mine, other.astype(kind)


def share_tokens(terms, tensor_at):
    held = terms
    for bit in (1, 2):
        mine, other = kept_and_sent(held, tensor_at, bit, jnp.float32)
        held = mine + swap(other, "tensor", bit)
    return held[0] + swap(held[1], "dp", PAIR)


def flip_pairs(values):
    blocks = lax.axis_size("dp")
    width = values.shape[-1] // blocks
    pieces = [values[..., (place ^ 1) * width : ((place ^ 1) + 1) * width] for place in range(blocks)]
    return jnp.concatenate(pieces, axis=-1)


def whole_tokens(values, tensor_at):
    for bit in (2, 1):
        values = join_halves(values, swap(values, "tensor", bit), (tensor_at // bit) % 2, 0)
    return values


def shards(
    block_input,
    out_grad,
    seg_ids,
    slot_live,
    norm_gain,
    z_weight,
    x_weight,
    bc_weight,
    dt_weight,
    conv_x,
    conv_bc,
    head_params,
    gated_gain,
    out_weight,
    norm_gain_sq,
    z_rows,
    z_cols,
    x_rows,
    x_cols,
    bc_rows,
    bc_cols,
    dt_rows,
    dt_cols,
    conv_x_sq,
    conv_bc_sq,
    head_sq,
    gated_gain_sq,
    out_rows,
    out_cols,
):
    data_count = lax.axis_size("dp")
    data_at = lax.axis_index("dp")
    tensor_at = lax.axis_index("tensor")
    half = (data_at // PAIR) % 2
    core = tensor_at % 2
    row_count = z_weight.shape[0]
    quarter = row_count // 4
    slot_tokens = block_input.shape[1]
    f32, bf16 = jnp.float32, jnp.bfloat16

    share = slot_tokens // 4
    share_at = (core * 2 + tensor_at // 2) * share
    last_bit = dp_bits()[-1]

    def share_of(values):
        return lax.dynamic_slice_in_dim(values, share_at, share, 0)

    def halves_of(weight):
        return halves(weight.astype(bf16), half, 1)

    def rows_of(*pieces):
        return jnp.concatenate(pieces, axis=0)

    whole_numbers = jnp.concatenate(
        [seg_ids[0], jnp.broadcast_to(slot_live, (8 * 128 - slot_tokens,))]
    ).astype(bf16).reshape(-1, 128)
    dt_rows_low = dt_weight.astype(bf16).T
    bc_mine = lax.dynamic_slice_in_dim(bc_weight.astype(bf16), tensor_at * quarter, quarter, 0)
    small = rows_of(bc_mine.reshape(-1, 128), dt_rows_low.reshape(-1, 128))
    small_count = small.shape[0]
    x_mine, x_other = halves_of(x_weight)
    small_far = swap(rows_of(small, whole_numbers), "dp", PAIR)
    x_far = swap(x_other, "dp", PAIR)
    small_far, x_far, x_mine, small, z_weight, out_weight, block_input, out_grad = step(
        small_far, x_far, x_mine, small, z_weight, out_weight, block_input, out_grad
    )

    far_numbers = small_far[small_count:].astype(jnp.int32)
    segments = jnp.stack([seg_ids[0], far_numbers.reshape(-1)[:slot_tokens]])
    live = jnp.stack([slot_live[0], far_numbers[-1, 0]]).astype(f32)
    small = jnp.stack([small, small_far[:small_count]])
    for bit in dp_bits()[1:-1]:
        small = rows_of(small, swap(small, "dp", bit))
    x_held, x_got = gather_middle(rows_of(x_mine, x_far))
    x_first = swap(x_held, "dp", last_bit)
    z_mine, z_other = halves_of(z_weight)
    out_mine, out_other = halves_of(out_weight)
    in_share, grad_share = share_of(block_input[0]), share_of(out_grad[0])
    marks, doc_rows = document_marks(segments)
    taps_x, _ = halves(conv_x, half, 1)
    per_head, _ = halves(head_params, half, 1)
    gain_inner, _ = halves(gated_gain, half, 0)
    head_count = per_head.shape[1]
    head_rows = jnp.pad(per_head, ((0, 5), (0, 128 - head_count)))
    vectors = jnp.concatenate(
        [taps_x, gain_inner[None], jnp.repeat(per_head[2], WIDTH)[None], jnp.zeros((2, taps_x.shape[1]))]
    )
    marks, doc_rows, head_rows, vectors, z_mine, out_mine = step(
        marks, doc_rows, head_rows, vectors, z_mine, out_mine
    )
    gain_rel = to_relative(norm_gain, data_at)
    own_rel = to_relative(block_input[0], data_at).astype(f32)
    x_got, x_first, small, z_other, in_share, grad_share, out_other, own_rel, marks, vectors = step(
        x_got, x_first, small, z_other, in_share, grad_share, out_other, own_rel, marks, vectors
    )

    x_second = swap(x_got, "dp", last_bit)
    small = rows_of(small, swap(small, "dp", last_bit))
    z_far = swap(z_other, "dp", PAIR)
    in_far = swap(in_share, "dp", PAIR)
    bc_piece_rows = quarter * bc_weight.shape[1] // 128
    bc_held = small[:, :bc_piece_rows].reshape(data_count, quarter, -1)
    x_second, small, z_far, in_far, z_mine, grad_share, out_other, bc_held = step(
        x_second, small, z_far, in_far, z_mine, grad_share, out_other, bc_held
    )

    z_held, z_got = gather_middle(rows_of(z_mine, z_far))
    z_first = swap(z_held, "dp", last_bit)
    in_far = join_halves(in_far, swap(in_far, "tensor", 2), tensor_at // 2, 0)
    bc_held = join_halves(bc_held, swap(bc_held, "tensor", 1), core, 1)
    low_x = rows_of(x_held, x_got, x_first, x_second)
    z_got, z_first, in_far, bc_held, grad_share, out_other, low_x = step(
        z_got, z_first, in_far, bc_held, grad_share, out_other, low_x
    )

    z_second = swap(z_got, "dp", last_bit)
    out_far = swap(out_other, "dp", PAIR)
    grad_far = swap(grad_share, "dp", PAIR)
    in_far = join_halves(in_far, swap(in_far, "tensor", 1), core, 0)
    bc_held = join_halves(bc_held, swap(bc_held, "tensor", 2), tensor_at // 2, 1)
    low_bc = bc_held.reshape(data_count * row_count, -1)
    in_rel = jnp.stack([own_rel, to_relative(in_far, data_at).astype(f32)])
    mean_square = jnp.mean(in_rel * in_rel, axis=-1, keepdims=True)
    normed_low = (in_rel * lax.rsqrt(mean_square + norm_eps) * gain_rel).astype(bf16)
    z_second, out_far, grad_far, normed_low = step(z_second, out_far, grad_far, normed_low)
    low_z = rows_of(z_held, z_got, z_first, z_second)
    out_held, out_got = gather_middle(rows_of(out_mine, out_far))
    out_first = swap(out_held, "dp", last_bit)
    grad_far = join_halves(grad_far, swap(grad_far, "tensor", 2), tensor_at // 2, 0)
    low_out = rows_of(out_held, out_got, out_first, swap(out_got, "dp", last_bit))
    grad_far = join_halves(grad_far, swap(grad_far, "tensor", 1), core, 0)
    both_grad = jnp.stack([out_grad[0], grad_far])

    low_dt = (
        small[:, bc_piece_rows:].reshape(data_count, dt_weight.shape[1], row_count).transpose(1, 0, 2)
    ).reshape(dt_weight.shape[1], -1)
    low_dt, _ = halves(low_dt, half, 0)
    low_dt = jnp.pad(low_dt, ((0, 128 - head_count), (0, 0)))
    normed_flat = normed_low.reshape(-1, normed_low.shape[-1])
    tokens = normed_flat.shape[0]

    def per_slot(values):
        return values.reshape(2, slot_tokens, -1)

    bc_raw = per_slot(jnp.dot(normed_flat, low_bc, preferred_element_type=f32))
    dt_raw = per_slot(rows_times(normed_flat, low_dt))
    x_raw = per_slot(jnp.dot(normed_flat, low_x, preferred_element_type=f32))
    gate_z = per_slot(jnp.dot(normed_flat, low_z, preferred_element_type=f32))
    common = (marks, doc_rows, bc_raw, dt_raw, conv_bc, head_rows, x_raw, gate_z, vectors)
    scaled_both, scanned, square_parts = mixer_forward(common)
    scaled_low = scaled_both.reshape(tokens, -1)

    projected = per_slot(rows_times(scaled_low, low_out))
    cot_rel = to_relative(both_grad, data_at) * live.astype(bf16)[:, None, None]
    totals = jnp.stack([jnp.sum(square_parts, axis=-1), jnp.sum(cot_rel.astype(f32) * projected, axis=-1)], axis=1)
    totals = totals + swap(totals, "tensor", 1)
    _, leaving = kept_and_sent(projected, tensor_at, 1, bf16)
    arriving = swap(after(leaving, totals), "tensor", 1)
    totals = totals + swap(totals, "tensor", 2)
    totals = totals + swap(totals, "dp", PAIR)[::-1]
    total_squares, rms_grad = totals[:, 0], totals[:, 1]
    inv_rms = lax.rsqrt(total_squares / INNER + norm_eps)
    squares_grad = rms_grad * -0.5 * inv_rms * inv_rms * inv_rms / INNER
    proj_grad = (cot_rel.astype(f32) * inv_rms[:, :, None]).astype(bf16).reshape(tokens, -1)
    scaled_grad = per_slot(jnp.dot(proj_grad, low_out, preferred_element_type=f32))

    part = low_out.shape[0] // 4
    middle_bit = dp_bits()[-2]

    def across(value, bit):
        return swap(value, "dp", bit)

    out_sent = [gradient_rows(proj_grad, scaled_low, place, bf16) for place in (3, 2)]
    out_passed, out_kept = [swap(value, "dp", last_bit) for value in out_sent]
    gradients = (
        after(scaled_grad, *out_sent, arriving),
        jnp.broadcast_to(squares_grad[:, :, None], (2, slot_tokens, 8)),
    )
    backward = mixer_backward(common, scanned, *gradients, 0)
    proj_later, out_passed, projected, *backward = step(proj_grad, out_passed, projected, *backward)
    shared, _ = kept_and_sent(projected, tensor_at, 1, bf16)
    shared, leaving = kept_and_sent(shared + arriving.astype(f32), tensor_at, 2, bf16)
    out_middle = gradient_rows(proj_later, scaled_low, 1, bf16, out_passed)
    out_middle, leaving, *backward = step(out_middle, leaving, *backward)
    out_got = across(out_middle, middle_bit)
    arriving = swap(leaving, "tensor", 2)
    inv_mine = lax.dynamic_slice_in_dim(inv_rms[0], share_at, share, 0)
    in_mine = to_relative(share_of(block_input[0]), data_at).astype(f32)
    cot_mine = to_relative(share_of(out_grad[0]), data_at).astype(f32) * live[0]
    z_both, x_both, bc_grad_part, dt_both, vector_terms, taps_bc_terms, head_terms = mixer_backward(
        common, scanned, *gradients, 1, backward
    )
    x_both, z_both, bc_grad_part, out_kept, arriving = step(
        x_both, z_both, bc_grad_part, out_kept, arriving
    )
    vector_terms = jnp.sum(vector_terms, axis=0)
    convx_slot, gated_slot = vector_terms[:4], vector_terms[4]
    convbc_part = jnp.sum(taps_bc_terms, axis=0)[:4]
    head_slot = jnp.concatenate(
        [
            jnp.sum(head_terms, axis=0)[:2, :head_count],
            jnp.sum(vector_terms[5].reshape(head_count, -1), axis=1)[None],
        ]
    )
    bc_kept, bc_leaving = kept_and_sent(bc_grad_part, tensor_at, 1, f32)
    bc_arriving = swap(bc_leaving, "tensor", 1)
    z_low = z_both.reshape(tokens, -1)
    x_low = x_both.reshape(tokens, -1)
    dt_low = dt_both.astype(bf16).reshape(tokens, -1)
    matrices = (low_z, low_x, low_dt)
    x_sent = gradient_rows(normed_flat, x_low, 3, bf16)
    x_low, z_low, x_sent, bc_arriving, out_got = step(x_low, z_low, x_sent, bc_arriving, out_got)

    x_passed = swap(x_sent, "dp", last_bit)
    bc_kept, bc_leaving = kept_and_sent(bc_kept + bc_arriving, tensor_at, 2, f32)
    bc_arriving = swap(bc_leaving, "tensor", 2)
    x_low, z_low, bc_leaving = step(x_low, z_low, bc_leaving)
    z_sent = gradient_rows(normed_flat, z_low, 3, bf16)
    both_sent = jnp.concatenate(
        [gradient_rows(normed_flat, values, 2, bf16) for values in (x_low, z_low)], axis=0
    )
    x_low, z_low, z_sent, both_sent, bc_arriving, arriving = step(
        x_low, z_low, z_sent, both_sent, bc_arriving, arriving
    )

    bc_kept = bc_kept + bc_arriving
    bc_far = swap(bc_kept[1], "dp", PAIR)
    shared = shared + arriving.astype(f32)
    shared_leaving = low_bits(shared[1])
    out_mine, out_leaving = middle_sum(gradient_rows(proj_later, scaled_low, 0, f32, out_kept), out_got)
    x_low, z_low, shared_leaving, out_mine, out_leaving = step(
        x_low, z_low, shared_leaving, out_mine, out_leaving
    )
    out_far = across(out_leaving, PAIR)
    projected_far = across(shared_leaving, PAIR)
    input_leaving = input_terms(1 - core, z_low, x_low, dt_low, *matrices)
    x_low, z_low, x_passed, input_leaving, bc_far, out_far, projected_far = step(
        x_low, z_low, x_passed, input_leaving, bc_far, out_far, projected_far
    )

    z_passed = swap(z_sent, "dp", last_bit)
    x_middle = gradient_rows(normed_flat, x_low, 1, bf16, x_passed)
    x_got = across(x_middle, middle_bit)
    input_arriving = swap(input_leaving, "tensor", 1)
    bc_low_mine = (bc_kept[0] + bc_far).astype(bf16)
    bc_far = swap(bc_low_mine, "tensor", 2)
    x_low, z_low, x_middle, bc_far = step(x_low, z_low, x_middle, bc_far)
    projected_mine = shared[0] + flip_pairs(projected_far.astype(f32))
    output = from_relative((in_mine + inv_mine[:, None] * projected_mine).astype(bf16), data_at)
    output_far = swap(output, "tensor", 2)
    input_kept = input_terms(core, z_low, x_low, dt_low, *matrices)
    out_share = join_halves(out_mine, out_far.astype(f32), half, 1)
    x_low, z_low, input_kept, z_passed, input_arriving, output_far, out_share = step(
        x_low, z_low, input_kept, z_passed, input_arriving, output_far, out_share
    )

    z_middle = gradient_rows(normed_flat, z_low, 1, bf16, z_passed)
    z_got = across(z_middle, middle_bit)
    both_kept = swap(both_sent, "dp", last_bit)
    bc_low = join_halves(bc_low_mine, bc_far, tensor_at // 2, 0)
    bc_far = swap(bc_low, "tensor", 1)
    x_low, z_low, z_middle, bc_low = step(x_low, z_low, z_middle, bc_low)
    input_kept, input_leaving = kept_and_sent(input_kept + input_arriving, tensor_at, 2, bf16)
    dt_part = tokens_out(dt_low, normed_flat)[:head_count]
    bc_far, dt_part, input_kept, input_leaving = step(bc_far, dt_part, input_kept, input_leaving)

    input_arriving = swap(input_leaving, "tensor", 2)
    bc_low = join_halves(bc_low, bc_far, core, 0)
    bc_columns = bc_low.shape[1] // 4
    bc_part = tokens_out(
        lax.dynamic_slice_in_dim(bc_low, tensor_at * bc_columns, bc_columns, 1), normed_low[0]
    )
    held = jnp.concatenate([bc_part, dt_part], axis=0)
    held = jnp.stack(
        [held[:, block * row_count : (block + 1) * row_count] for block in range(data_count)]
    )
    count = held.shape[0] // 2
    held = held[:count] + swap(held[count:], "dp", last_bit)
    output = join_halves(output, output_far, tensor_at // 2, 0)
    output_far = swap(output, "tensor", 1)
    held, both_kept, x_got, output_far = step(held, both_kept, x_got, output_far)
    for bit in reversed(dp_bits()[1:-1]):
        count = held.shape[0] // 2
        held = held[:count] + swap(held[count:], "dp", bit)
    x_terms = gradient_rows(normed_flat, x_low, 0, f32, both_kept[:part])
    z_terms = gradient_rows(normed_flat, z_low, 0, f32, both_kept[part:])
    x_mine, x_leaving = middle_sum(x_terms, x_got)
    output = join_halves(output, output_far, core, 0)
    input_mine = input_kept + input_arriving.astype(f32)
    input_leaving = low_bits(input_mine[1])
    held, z_terms, x_leaving, input_leaving = step(held, z_terms, x_leaving, input_leaving)

    input_far = swap(input_leaving, "dp", PAIR)
    small_far = swap(held[1], "dp", PAIR)
    z_mine, z_leaving = middle_sum(z_terms, z_got)
    z_leaving, small_far, input_far = step(z_leaving, small_far, input_far)
    both_far = across(jnp.concatenate([x_leaving, z_leaving], axis=0), PAIR)
    normed_grad = (
        input_mine[0] + flip_pairs(input_far.astype(f32)) + rows_times(bc_low_mine, low_bc)
    )

    _, norm_pull = jax.vjp(norm_input, in_mine, gain_rel)
    block_grad, gain_slot = norm_pull(normed_grad)
    input_grad = from_relative((cot_mine + block_grad).astype(bf16), data_at)
    both_far, gain_slot, output = step(both_far, gain_slot, output)
    x_share = join_halves(x_mine, both_far[: x_mine.shape[0]].astype(f32), half, 1)
    z_share = join_halves(z_mine, both_far[x_mine.shape[0] :].astype(f32), half, 1)

    bc_share = held[0, :bc_columns] + small_far[:bc_columns]
    dt_share = join_halves(held[0, bc_columns:], small_far[bc_columns:], half, 0).T
    bc_share = join_halves(bc_share, swap(bc_share, "tensor", 1), core, 0)
    bc_share = join_halves(bc_share, swap(bc_share, "tensor", 2), tensor_at // 2, 0).T

    def in_half(values):
        return join_halves(values, jnp.zeros_like(values), half, values.ndim - 1)

    def packed_sum(pieces, axis_bits):
        sizes = [piece.size for piece in pieces]
        flat = jnp.concatenate([piece.reshape(-1) for piece in pieces])
        fill = -flat.size % 128
        flat = jnp.pad(flat, (0, fill)).reshape(-1, 128)
        for axis, bits in axis_bits:
            flat = add_over(flat, axis, bits)
        flat = flat.reshape(-1)
        result, at = [], 0
        for piece, size in zip(pieces, sizes):
            result.append(flat[at : at + size].reshape(piece.shape))
            at += size
        return result

    norm_sum, convbc_sum = packed_sum(
        [from_relative(gain_slot, data_at), convbc_part], [("tensor", (1, 2))]
    )
    z_share, bc_share, norm_sum, convbc_sum = step(z_share, bc_share, norm_sum, convbc_sum)
    z_square = z_share * z_share + tiny_eps
    x_square = x_share * x_share + tiny_eps
    bc_square = bc_share * bc_share + tiny_eps
    dt_square = dt_share * dt_share + tiny_eps
    out_square = out_share * out_share + tiny_eps
    row_sums = jnp.stack(
        [
            jnp.sum(z_square, axis=1),
            jnp.sum(x_square, axis=1),
            jnp.sum(dt_square, axis=1),
            jnp.sum(out_square, axis=1),
        ]
    )
    z_row_sum, x_row_sum, dt_row_sum, out_row_sum = add_over(row_sums, "tensor", (1, 2))
    bc_row_sum = jnp.sum(bc_square, axis=1)

    (
        norm_total,
        convbc_total,
        gated_total,
        convx_total,
        head_total,
        z_col_sum,
        x_col_sum,
        bc_col_sum,
        dt_col_sum,
        out_col_sum,
    ) = packed_sum(
        [
            norm_sum,
            convbc_sum,
            in_half(gated_slot),
            in_half(convx_slot),
            in_half(head_slot),
            jnp.sum(z_square, axis=0),
            jnp.sum(x_square, axis=0),
            jnp.sum(bc_square, axis=0),
            jnp.sum(dt_square, axis=0),
            jnp.sum(out_square, axis=0),
        ],
        [("dp", dp_bits())],
    )
    z_rows_new = mix_state(z_rows, z_row_sum / INNER)
    x_rows_new = mix_state(x_rows, x_row_sum / INNER)
    bc_rows_new = mix_state(bc_rows, bc_row_sum / (2 * STATE))
    dt_rows_new = mix_state(dt_rows, dt_row_sum / HEADS)
    out_rows_new = mix_state(out_rows, out_row_sum / INNER)
    z_cols_new = mix_state(z_cols, z_col_sum / D)
    x_cols_new = mix_state(x_cols, x_col_sum / D)
    bc_cols_new = mix_state(bc_cols, bc_col_sum / D)
    dt_cols_new = mix_state(dt_cols, dt_col_sum / D)
    out_cols_new = mix_state(out_cols, out_col_sum / D)
    norm_second = mix_state(norm_gain_sq, norm_total * norm_total + tiny_eps)
    gated_second = mix_state(gated_gain_sq, gated_total * gated_total + tiny_eps)
    convx_second = mix_state(conv_x_sq, convx_total * convx_total + tiny_eps)
    convbc_second = mix_state(conv_bc_sq, convbc_total * convbc_total + tiny_eps)
    head_second = mix_state(head_sq, head_total * head_total + tiny_eps)
    norm_unit = norm_total * lax.rsqrt(norm_second)
    gated_unit = gated_total * lax.rsqrt(gated_second)
    convx_unit = convx_total * lax.rsqrt(convx_second)
    convbc_unit = convbc_total * lax.rsqrt(convbc_second)
    head_unit = head_total * lax.rsqrt(head_second)
    z_unit = z_share * lax.rsqrt(z_rows_new[:, None] * z_cols_new[None, :])
    x_unit = x_share * lax.rsqrt(x_rows_new[:, None] * x_cols_new[None, :])
    bc_unit = bc_share * lax.rsqrt(bc_rows_new[:, None] * bc_cols_new[None, :])
    dt_unit = dt_share * lax.rsqrt(dt_rows_new[:, None] * dt_cols_new[None, :])
    out_unit = out_share * lax.rsqrt(out_rows_new[:, None] * out_cols_new[None, :])
    tensor_count = lax.axis_size("tensor")
    unit_sums = jnp.stack(
        [
            jnp.sum(z_unit * z_unit),
            jnp.sum(x_unit * x_unit),
            jnp.sum(bc_unit * bc_unit) / tensor_count,
            jnp.sum(dt_unit * dt_unit),
            jnp.sum(out_unit * out_unit),
            jnp.sum(gated_unit * gated_unit) / data_count,
            jnp.sum(convx_unit * convx_unit) / data_count,
            jnp.sum(head_unit * head_unit) / data_count,
        ]
    )
    unit_sums = jnp.broadcast_to(unit_sums[:, None], (8, 128))
    unit_sums = add_over(unit_sums, "tensor", (1, 2))
    unit_sums, input_grad, output = step(unit_sums, input_grad, output)
    input_far = swap(input_grad, "tensor", 2)
    unit_sums = add_over(unit_sums, "dp", dp_bits())
    input_far, unit_sums = step(input_far, unit_sums)
    input_grad = join_halves(input_grad, input_far, tensor_at // 2, 0)
    input_grad = join_halves(input_grad, swap(input_grad, "tensor", 1), core, 0)
    (
        z_total,
        x_total,
        bc_total_sq,
        dt_total,
        out_total,
        gated_sq_total,
        convx_sq_total,
        head_sq_total,
    ) = unit_sums[:, 0]
    norm_sq_total = jnp.sum(norm_unit * norm_unit)
    convbc_sq_total = jnp.sum(convbc_unit * convbc_unit)
    in_rate = D ** (-0.5)
    out_rate = INNER ** (-0.5)
    z_upd = -in_rate * normalized(z_unit, z_total, D * INNER)
    x_upd = -in_rate * normalized(x_unit, x_total, D * INNER)
    bc_upd = -in_rate * normalized(bc_unit, bc_total_sq, D * 2 * STATE)
    dt_upd = -in_rate * normalized(dt_unit, dt_total, D * HEADS)
    out_upd = -out_rate * normalized(out_unit, out_total, D * INNER)
    norm_upd = -vector_rate * normalized(norm_unit, norm_sq_total, D)
    gated_upd = -vector_rate * normalized(gated_unit, gated_sq_total, INNER)
    convx_upd = -vector_rate * normalized(convx_unit, convx_sq_total, KCONV * INNER)
    convbc_upd = -vector_rate * normalized(convbc_unit, convbc_sq_total, KCONV * 2 * STATE)
    head_upd = -vector_rate * normalized(head_unit, head_sq_total, 3 * HEADS)
    return (
        output[None],
        input_grad[None],
        norm_total,
        norm_upd,
        norm_second,
        z_share,
        z_upd,
        z_rows_new,
        z_cols_new,
        x_share,
        x_upd,
        x_rows_new,
        x_cols_new,
        bc_share,
        bc_upd,
        bc_rows_new,
        bc_cols_new,
        dt_share,
        dt_upd,
        dt_rows_new,
        dt_cols_new,
        convx_total,
        convx_upd,
        convx_second,
        convbc_total,
        convbc_upd,
        convbc_second,
        head_total,
        head_upd,
        head_second,
        gated_total,
        gated_upd,
        gated_second,
        out_share,
        out_upd,
        out_rows_new,
        out_cols_new,
    )


def solution(mesh):
    in_specs = (
        P("dp", None, None),
        P("dp", None, None),
        P("dp", None),
        P("dp"),
        P(),
        P("dp", "tensor"),
        P("dp", "tensor"),
        P("dp", None),
        P("dp", "tensor"),
        P(None, "tensor"),
        P(),
        P(None, "tensor"),
        P("tensor"),
        P("dp", "tensor"),
        P(),
        P("dp"),
        P("tensor"),
        P("dp"),
        P("tensor"),
        P("dp"),
        P(),
        P("dp"),
        P("tensor"),
        P(None, "tensor"),
        P(),
        P(None, "tensor"),
        P("tensor"),
        P("dp"),
        P("tensor"),
    )
    out_specs = (
        P("dp", None, None),
        P("dp", None, None),
        P(),
        P(),
        P(),
        P("dp", "tensor"),
        P("dp", "tensor"),
        P("dp"),
        P("tensor"),
        P("dp", "tensor"),
        P("dp", "tensor"),
        P("dp"),
        P("tensor"),
        P("dp", None),
        P("dp", None),
        P("dp"),
        P(),
        P("dp", "tensor"),
        P("dp", "tensor"),
        P("dp"),
        P("tensor"),
        P(None, "tensor"),
        P(None, "tensor"),
        P(None, "tensor"),
        P(),
        P(),
        P(),
        P(None, "tensor"),
        P(None, "tensor"),
        P(None, "tensor"),
        P("tensor"),
        P("tensor"),
        P("tensor"),
        P("dp", "tensor"),
        P("dp", "tensor"),
        P("dp"),
        P("tensor"),
    )
    return jax.shard_map(shards, mesh=mesh, in_specs=in_specs, out_specs=out_specs, check_vma=False)
```

```python
import jax
import jax.numpy as jnp
from jax import lax
from jax.experimental import pallas as pl
from jax.experimental.pallas import tpu as pltpu
from jax.sharding import PartitionSpec as P

D = 2048
HEADS = 64
STATE = 128
INNER = 4096
KCONV = 4


norm_eps = 1e-05
decay_rate = 0.5
tiny_eps = 1e-30
unit_eps = 1e-06
vector_rate = 0.05


LANES = 128
PART = 256
WIDTH = 64


def cost_of(micros):
    return pl.CostEstimate(flops=micros * 1_000_000_000, bytes_accessed=1 << 20, transcendentals=0)


def two_parts(values):
    high = values.astype(jnp.bfloat16)
    return high, (values - high.astype(jnp.float32)).astype(jnp.bfloat16)


def plain(left, right):
    return lax.dot_general(
        left, right, (((1,), (0,)), ((), ())), preferred_element_type=jnp.float32
    )


def turned(left, right):
    return lax.dot_general(
        left, right, (((1,), (1,)), ((), ())), preferred_element_type=jnp.float32
    )


def fine(product, left, right):
    left_high, left_low = two_parts(left)
    right_high, right_low = two_parts(right)
    return (
        product(left_high, right_high)
        + product(left_high, right_low)
        + product(left_low, right_high)
    )


def running_sum(values, backward):
    rows = lax.broadcasted_iota(jnp.int32, (PART, PART), 0)
    columns = lax.broadcasted_iota(jnp.int32, (PART, PART), 1)
    within = (rows <= columns) if backward else (rows >= columns)
    ones = within.astype(jnp.float32).astype(jnp.bfloat16)

    def inside(block):
        high, rest = block.astype(jnp.bfloat16), block
        total = plain(ones, high)
        rest = block - high.astype(jnp.float32)
        for _ in range(2):
            part = rest.astype(jnp.bfloat16)
            total = total + plain(ones, part)
            rest = rest - part.astype(jnp.float32)
        return total

    blocks = [inside(values[:PART]), inside(values[PART:])]
    if backward:
        blocks[0] = blocks[0] + blocks[1][0:1]
    else:
        blocks[1] = blocks[1] + blocks[0][PART - 1 : PART]
    return jnp.concatenate(blocks, axis=0)


def sigmoid(values):
    return 1.0 / (1.0 + jnp.exp(-values))


def conv_rows(values, taps, same):
    result = taps[0:1] * values
    for offset in range(1, 4):
        shifted = pltpu.roll(values, offset, 0)
        result = result + taps[offset : offset + 1] * (shifted * same[offset - 1])
    return result


def conv_rows_back(grad, values, taps, same):
    length = values.shape[0]
    result = taps[0:1] * grad
    tap_rows = [jnp.sum(grad * values, axis=0, keepdims=True)]
    for offset in range(1, 4):
        kept = grad * same[offset - 1]
        result = result + pltpu.roll(taps[offset : offset + 1] * kept, length - offset, 0)
        tap_rows.append(
            jnp.sum(kept * pltpu.roll(values, offset, 0), axis=0, keepdims=True)
        )
    return result, tap_rows


def softplus(values):
    return jnp.maximum(values, 0.0) + jnp.log1p(jnp.exp(-jnp.abs(values)))


def marks_of(marks_ref):
    marks = marks_ref[0]
    same = [marks[:, place : place + 1] for place in (1, 2, 3)]
    return marks[:, 0:1], same, marks[:, 4:5]


def prepare(transposed, marks_ref, row_ref, bc_ref, dt_ref, taps_bc_ref, head_ref,
            bc_pre_ref, bc_ref_out, dt_out, cum_wide, dt_wide, cum_rows, score, bias):
    doc, same, _ = marks_of(marks_ref)
    bc_pre = conv_rows(bc_ref[0], taps_bc_ref[...], same)
    bc = bc_pre * sigmoid(bc_pre)
    bc_pre_ref[...] = bc_pre
    bc_ref_out[...] = bc
    b_mat, c_mat = bc[:, :LANES], bc[:, LANES:]
    first, second = slice(0, PART), slice(PART, 2 * PART)
    for place, (out_rows, in_rows) in enumerate(((first, first), (second, second), (second, first))):
        if transposed:
            score[place] = fine(turned, b_mat[in_rows], c_mat[out_rows])
        else:
            score[place] = fine(turned, c_mat[out_rows], b_mat[in_rows])
    rows = lax.broadcasted_iota(jnp.int32, (PART, PART), 0)
    columns = lax.broadcasted_iota(jnp.int32, (PART, PART), 1)
    causal = (rows <= columns) if transposed else (rows >= columns)
    doc_row = row_ref[0][0:1]
    for place, part in enumerate((first, second)):
        seen = causal & (doc[part] == doc_row[:, part])
        bias[place] = jnp.where(seen, 0.0, -1e30)
    step = softplus(dt_ref[0] + head_ref[0:1])
    decay = step * -jnp.exp(head_ref[1:2])
    total = running_sum(decay, False)
    dt_out[...] = step
    flipped = total.T
    lane = lax.broadcasted_iota(jnp.int32, (2 * PART, LANES), 1)
    for pair in range(cum_wide.shape[0]):
        one, two = 2 * pair, 2 * pair + 1
        cum_wide[pair] = jnp.where(lane < WIDTH, total[:, one : one + 1], total[:, two : two + 1])
        dt_wide[pair] = jnp.where(lane < WIDTH, step[:, one : one + 1], step[:, two : two + 1])
        cum_rows[one] = flipped[one : one + 1]
        cum_rows[two] = flipped[two : two + 1]


def edge_weights(wide, in_last):
    edge = wide[PART - 1 : PART]
    after = jnp.exp(wide[PART:] - edge) * in_last[PART:]
    before = jnp.exp(edge - wide[:PART]) * in_last[:PART]
    return after, before


def forward_body(marks_ref, row_ref, bc_ref, dt_ref, taps_bc_ref, head_ref, x_ref, z_ref, vec_ref,
                 scaled_ref, scan_ref, squares_ref,
                 bc_pre, bc_act, dt_act, cum_wide, dt_wide, cum_rows, score, bias):
    pair = pl.program_id(1)

    @pl.when(pair == 0)
    def _():
        prepare(False, marks_ref, row_ref, bc_ref, dt_ref, taps_bc_ref, head_ref,
                bc_pre, bc_act, dt_act, cum_wide, dt_wide, cum_rows, score, bias)
        squares_ref[...] = jnp.zeros_like(squares_ref)

    _, same, in_last = marks_of(marks_ref)
    vec = vec_ref[...]
    pre = conv_rows(x_ref[0], vec[0:4], same)
    values = pre * sigmoid(pre)
    wide = cum_wide[pair]
    stepped = dt_wide[pair] * values
    high, low_part = two_parts(stepped)
    both = jnp.concatenate([high, low_part], axis=1)
    lane = lax.broadcasted_iota(jnp.int32, (PART, LANES), 1)
    blocks = []
    for place in range(2):
        part = slice(place * PART, (place + 1) * PART)
        answers = []
        for k in range(2):
            row = cum_rows[2 * pair + k][:, part]
            kernel = jnp.exp(wide[part, k * WIDTH : k * WIDTH + 1] - row + bias[place])
            mixing_high, mixing_low = two_parts(score[place] * kernel)
            answer = plain(mixing_high, both[part])
            answers.append(
                answer[:, :LANES] + answer[:, LANES:] + plain(mixing_low, high[part])
            )
        blocks.append(jnp.where(lane < WIDTH, answers[0], answers[1]))
    after, before = edge_weights(wide, in_last)
    blocks[1] = blocks[1] + after * fine(plain, score[2], before * stepped[:PART])
    scanned = jnp.concatenate(blocks, axis=0)
    scan_ref[0] = scanned
    gate = z_ref[0]
    gated = (scanned + vec[5:6] * values) * (gate * sigmoid(gate))
    squares_ref[0] = squares_ref[0] + gated * gated
    scaled_ref[0] = (gated * vec[4:5]).astype(scaled_ref.dtype)


def backward_body(marks_ref, row_ref, bc_ref, dt_ref, taps_bc_ref, head_ref, x_ref, z_ref, vec_ref,
                  scan_ref, grad_ref, sq_grad_ref,
                  z_out, x_out, bc_out, dt_out, vec_out, taps_bc_out, head_out,
                  bc_pre, bc_act, dt_act, cum_wide, dt_wide, cum_rows, score, bias,
                  score_grad, from_rows, from_columns, from_in):
    pair = pl.program_id(1)

    @pl.when(pair == 0)
    def _():
        prepare(True, marks_ref, row_ref, bc_ref, dt_ref, taps_bc_ref, head_ref,
                bc_pre, bc_act, dt_act, cum_wide, dt_wide, cum_rows, score, bias)
        score_grad[...] = jnp.zeros_like(score_grad)
        from_rows[...] = jnp.zeros_like(from_rows)
        from_columns[...] = jnp.zeros_like(from_columns)
        from_in[...] = jnp.zeros_like(from_in)

    _, same, in_last = marks_of(marks_ref)
    vec = vec_ref[...]
    taps, gain, skip = vec[0:4], vec[4:5], vec[5:6]
    x_raw = x_ref[0]
    pre = conv_rows(x_raw, taps, same)
    pre_sig = sigmoid(pre)
    values = pre * pre_sig
    wide = cum_wide[pair]
    step = dt_wide[pair]
    stepped = step * values
    gate = z_ref[0]
    gate_sig = sigmoid(gate)
    gate_act = gate * gate_sig
    scanned = scan_ref[0]
    mixed = scanned + skip * values
    gated = mixed * gate_act
    scaled_grad = grad_ref[0]
    gated_grad = scaled_grad * gain + 2.0 * sq_grad_ref[0][:, 0:1] * gated
    z_out[0] = (gated_grad * mixed * (gate_sig * (1.0 + gate * (1.0 - gate_sig)))).astype(z_out.dtype)
    grad = gated_grad * gate_act
    rows = [
        None, None, None, None,
        jnp.sum(scaled_grad * gated, axis=0, keepdims=True),
        jnp.sum(grad * values, axis=0, keepdims=True),
    ]
    high, low_part = two_parts(grad)
    both = jnp.concatenate([high, low_part], axis=1)
    lane = lax.broadcasted_iota(jnp.int32, (PART, LANES), 1)

    def add_exponents(head, out_part, in_part, terms):
        from_rows[head, :, out_part] += jnp.sum(terms, axis=0, keepdims=True)
        gone = jnp.sum(terms, axis=1, keepdims=True)
        from_columns[in_part] += jnp.where(lane == head, gone, 0.0)

    blocks = []
    for place in range(2):
        part = slice(place * PART, (place + 1) * PART)
        answers = []
        total = score_grad[place]
        for k in range(2):
            row = cum_rows[2 * pair + k][:, part]
            kernel = jnp.exp(row - wide[part, k * WIDTH : k * WIDTH + 1] + bias[place])
            mixing = score[place] * kernel
            mixing_high, mixing_low = two_parts(mixing)
            answer = plain(mixing_high, both[part])
            answers.append(
                answer[:, :LANES] + answer[:, LANES:] + plain(mixing_low, high[part])
            )
            own = (lane < WIDTH) if k == 0 else (lane >= WIDTH)
            own_high, own_low = two_parts(jnp.where(own, stepped[part], 0.0))
            pulled = turned(
                jnp.concatenate([own_high, own_high], axis=1), both[part]
            ) + turned(own_low, high[part])
            total = total + pulled * kernel
            add_exponents(2 * pair + k, part, part, pulled * mixing)
        score_grad[place] = total
        blocks.append(jnp.where(lane < WIDTH, answers[0], answers[1]))
    after, before = edge_weights(wide, in_last)
    late = after * grad[PART:]
    early = before * stepped[:PART]
    blocks[0] = blocks[0] + before * fine(plain, score[2], late)
    for k in range(2):
        own = (lane < WIDTH) if k == 0 else (lane >= WIDTH)
        pulled = fine(turned, jnp.where(own, early, 0.0), late)
        score_grad[2] = score_grad[2] + pulled
        add_exponents(2 * pair + k, slice(PART, 2 * PART), slice(0, PART), pulled * score[2])
    pulled_in = jnp.concatenate(blocks, axis=0)
    places = lax.broadcasted_iota(jnp.int32, (LANES, LANES), 0) // WIDTH + 2 * pair
    columns = lax.broadcasted_iota(jnp.int32, (LANES, LANES), 1)
    chosen = (places == columns).astype(jnp.float32).astype(jnp.bfloat16)
    chosen = jnp.concatenate([chosen, chosen], axis=0)
    from_in[...] += plain(jnp.concatenate(two_parts(values * pulled_in), axis=1), chosen)
    pre_grad = (skip * grad + step * pulled_in) * (pre_sig * (1.0 + pre * (1.0 - pre_sig)))
    x_grad, rows[:4] = conv_rows_back(pre_grad, x_raw, taps, same)
    x_out[0] = x_grad.astype(x_out.dtype)
    vec_out[0] = jnp.concatenate(rows + [jnp.zeros((2, LANES), jnp.float32)], axis=0)

    @pl.when(pair == pl.num_programs(1) - 1)
    def _():
        steps = dt_act[...]
        rate = -jnp.exp(head_ref[1:2])
        direct = from_in[...]
        heads = from_rows.shape[0]
        arrived = jnp.concatenate(
            [from_rows[head] for head in range(heads)]
            + [jnp.zeros((LANES - heads, 2 * PART), jnp.float32)],
            axis=0,
        ).T
        decay_grad = running_sum(arrived - from_columns[...], True)
        step_grad = (direct + rate * decay_grad) * sigmoid(dt_ref[0] + head_ref[0:1])
        dt_out[0] = step_grad
        head_out[0] = jnp.concatenate(
            [
                jnp.sum(step_grad, axis=0, keepdims=True),
                rate * jnp.sum(decay_grad * steps, axis=0, keepdims=True),
                jnp.zeros((6, LANES), jnp.float32),
            ],
            axis=0,
        )
        b_mat, c_mat = bc_act[:, :LANES], bc_act[:, LANES:]
        first, second, cross = score_grad[0], score_grad[1], score_grad[2]
        b_grad = jnp.concatenate(
            [
                fine(plain, first, c_mat[:PART]) + fine(plain, cross, c_mat[PART:]),
                fine(plain, second, c_mat[PART:]),
            ],
            axis=0,
        )
        c_grad = jnp.concatenate(
            [
                fine(plain, first.T, b_mat[:PART]),
                fine(plain, second.T, b_mat[PART:]) + fine(plain, cross.T, b_mat[:PART]),
            ],
            axis=0,
        )
        shape = bc_pre[...]
        slope = sigmoid(shape)
        slope = slope * (1.0 + shape * (1.0 - slope))
        bc_grad, tap_rows = conv_rows_back(
            jnp.concatenate([b_grad, c_grad], axis=1) * slope, bc_ref[0], taps_bc_ref[...], same
        )
        bc_out[0] = bc_grad
        taps_bc_out[0] = jnp.concatenate(
            tap_rows + [jnp.zeros((4, 2 * LANES), jnp.float32)], axis=0
        )


def slot_block(first, *shape):
    return pl.BlockSpec((1,) + shape, lambda slot, pair: (slot + first, 0, 0))


def whole_block(*shape):
    return pl.BlockSpec(shape, lambda slot, pair: (0,) * len(shape))


def pair_block(first, length):
    return pl.BlockSpec((1, length, LANES), lambda slot, pair: (slot + first, 0, pair))


def common_specs(first, length):
    return [
        slot_block(first, length, 8),
        slot_block(first, 8, length),
        slot_block(first, length, 2 * LANES),
        slot_block(first, length, LANES),
        whole_block(4, 2 * LANES),
        whole_block(8, LANES),
        pair_block(first, length),
        pair_block(first, length),
        pl.BlockSpec((8, LANES), lambda slot, pair: (0, pair)),
    ]


def common_scratch(length, pairs):
    return [
        pltpu.VMEM((length, 2 * LANES), jnp.float32),
        pltpu.VMEM((length, 2 * LANES), jnp.float32),
        pltpu.VMEM((length, LANES), jnp.float32),
        pltpu.VMEM((pairs, length, LANES), jnp.float32),
        pltpu.VMEM((pairs, length, LANES), jnp.float32),
        pltpu.VMEM((2 * pairs, 1, length), jnp.float32),
        pltpu.VMEM((3, PART, PART), jnp.float32),
        pltpu.VMEM((2, PART, PART), jnp.float32),
    ]


def mixer_forward(common, interpret=False):
    slots, length, width = common[6].shape
    pairs = width // LANES
    return pl.pallas_call(
        forward_body,
        grid=(slots, pairs),
        in_specs=common_specs(0, length),
        out_specs=[pair_block(0, length), pair_block(0, length), slot_block(0, length, LANES)],
        out_shape=[
            jax.ShapeDtypeStruct((slots, length, width), jnp.bfloat16),
            jax.ShapeDtypeStruct((slots, length, width), jnp.float32),
            jax.ShapeDtypeStruct((slots, length, LANES), jnp.float32),
        ],
        scratch_shapes=common_scratch(length, pairs),
        cost_estimate=cost_of(16),
        name="mixer_forward",
        interpret=interpret,
    )(*common)


def mixer_backward(common, scanned, scaled_grad, sq_grad, slot, earlier=(), interpret=False):
    slots, length, width = common[6].shape
    pairs = width // LANES
    given = len(common) + 3

    def body(*refs):
        backward_body(*refs[:given], *refs[given + len(earlier) :])

    return pl.pallas_call(
        body,
        grid=(1, pairs),
        in_specs=common_specs(slot, length)
        + [pair_block(slot, length), pair_block(slot, length), slot_block(slot, length, 8)]
        + [pl.BlockSpec(memory_space=pl.ANY) for _ in earlier],
        out_specs=[
            pair_block(slot, length),
            pair_block(slot, length),
            slot_block(slot, length, 2 * LANES),
            slot_block(slot, length, LANES),
            pl.BlockSpec((1, 8, LANES), lambda _, pair: (slot, 0, pair)),
            slot_block(slot, 8, 2 * LANES),
            slot_block(slot, 8, LANES),
        ],
        out_shape=[
            jax.ShapeDtypeStruct((slots, length, width), jnp.bfloat16),
            jax.ShapeDtypeStruct((slots, length, width), jnp.bfloat16),
            jax.ShapeDtypeStruct((slots, length, 2 * LANES), jnp.float32),
            jax.ShapeDtypeStruct((slots, length, LANES), jnp.float32),
            jax.ShapeDtypeStruct((slots, 8, width), jnp.float32),
            jax.ShapeDtypeStruct((slots, 8, 2 * LANES), jnp.float32),
            jax.ShapeDtypeStruct((slots, 8, LANES), jnp.float32),
        ],
        input_output_aliases={given + place: place for place in range(len(earlier))},
        scratch_shapes=common_scratch(length, pairs)
        + [
            pltpu.VMEM((3, PART, PART), jnp.float32),
            pltpu.VMEM((2 * pairs, 1, length), jnp.float32),
            pltpu.VMEM((length, LANES), jnp.float32),
            pltpu.VMEM((length, LANES), jnp.float32),
        ],
        cost_estimate=cost_of(16),
        name="mixer_backward",
        interpret=interpret,
    )(*common, scanned, scaled_grad, sq_grad, *earlier)


def input_body(place_ref, z_ref, x_ref, dt_ref, z_rows_ref, x_rows_ref, dt_rows_ref, *rest):
    del place_ref

    def flat(ref):
        return ref[...].reshape(-1, ref.shape[-1])

    total = (
        turned(flat(z_ref), z_rows_ref[...])
        + turned(flat(x_ref), x_rows_ref[...])
        + plain(flat(dt_ref), dt_rows_ref[...])
    ).reshape(rest[-1].shape)
    for added in rest[:-1]:
        total = total + added[...]
    rest[-1][...] = total


def input_terms(place, z_low, x_low, dt_low, low_z, low_x, low_dt, *added):
    tokens = z_low.shape[0] // 4
    width = low_z.shape[1]
    features = low_z.shape[0]
    block = features // 4

    def by_half(values):
        return values.reshape(2, 2, tokens, -1)

    def half_block(values):
        return pl.BlockSpec((2, 1, tokens, values.shape[1]), lambda at, where: (0, where[0], 0, 0))

    weight = pl.BlockSpec((block, width), lambda at, where: (at, 0))
    out = pl.BlockSpec((2, tokens, block), lambda at, where: (0, 0, at))
    return pl.pallas_call(
        input_body,
        grid_spec=pltpu.PrefetchScalarGridSpec(
            num_scalar_prefetch=1,
            grid=(4,),
            in_specs=[
                half_block(z_low),
                half_block(x_low),
                half_block(dt_low),
                weight,
                weight,
                pl.BlockSpec((low_dt.shape[0], block), lambda at, where: (0, at)),
            ]
            + [out] * len(added),
            out_specs=out,
        ),
        out_shape=jax.ShapeDtypeStruct((2, tokens, features), jnp.float32),
        cost_estimate=cost_of(6),
        name="input_terms",
    )(
        place.astype(jnp.int32).reshape(1),
        by_half(z_low),
        by_half(x_low),
        by_half(dt_low),
        low_z,
        low_x,
        low_dt,
        *added,
    )


def document_marks(segments):
    slots, length = segments.shape
    docs = segments.astype(jnp.float32)
    columns = [docs]
    for offset in (1, 2, 3):
        same = (segments[:, offset:] == segments[:, :-offset]).astype(jnp.float32)
        columns.append(jnp.pad(same, ((0, 0), (offset, 0))))
    columns.append((segments == segments[:, PART - 1 : PART]).astype(jnp.float32))
    zero = jnp.zeros_like(docs)
    marks = jnp.stack(columns + [zero] * 3, axis=-1)
    return marks, jnp.broadcast_to(docs[:, None, :], (slots, 8, length))


def norm_input(values, gain):
    mean_square = jnp.mean(values * values, axis=1, keepdims=True)
    return values * lax.rsqrt(mean_square + norm_eps) * gain


def rows_times(left, right):
    return lax.dot_general(
        left, right, (((1,), (1,)), ((), ())), preferred_element_type=jnp.float32
    )


def tokens_out(left, right):
    return lax.dot_general(
        left, right, (((0,), (0,)), ((), ())), preferred_element_type=jnp.float32
    )


def mix_state(old_state, fresh_term):
    return decay_rate * old_state + (1.0 - decay_rate) * fresh_term


def normalized(unit, square_total, entries):
    return unit * lax.rsqrt(square_total / entries + unit_eps)


def swap(value, axis, bit):
    size = lax.axis_size(axis)
    return lax.ppermute(value, axis, [(place, place ^ bit) for place in range(size)])


def add_over(value, axis, bits):
    for bit in bits:
        value = value + swap(value, axis, bit)
    return value


PAIR = 2


def dp_bits():
    count = lax.axis_size("dp")
    rest = [1 << place for place in reversed(range(count.bit_length() - 1)) if 1 << place != PAIR]
    return [PAIR] + rest


def block_masks():
    bits = dp_bits()
    return [
        sum(bit for place, bit in enumerate(bits) if (number >> place) & 1)
        for number in range(lax.axis_size("dp"))
    ]


def place_of(offset):
    return sum(
        ((offset // bit) % 2) << place for place, bit in enumerate(dp_bits())
    )


def to_relative(values, mine):
    blocks = lax.axis_size("dp")
    width = values.shape[-1] // blocks
    return jnp.concatenate(
        [
            lax.dynamic_slice_in_dim(values, (mine ^ mask) * width, width, values.ndim - 1)
            for mask in block_masks()
        ],
        axis=-1,
    )


def from_relative(values, mine):
    blocks = lax.axis_size("dp")
    width = values.shape[-1] // blocks
    return jnp.concatenate(
        [
            lax.dynamic_slice_in_dim(values, place_of(mine ^ block) * width, width, values.ndim - 1)
            for block in range(blocks)
        ],
        axis=-1,
    )


def halves(values, half, axis):
    width = values.shape[axis] // 2
    mine = lax.dynamic_slice_in_dim(values, half * width, width, axis)
    other = lax.dynamic_slice_in_dim(values, (1 - half) * width, width, axis)
    return mine, other


def join_halves(mine, other, half, axis):
    low, high = jnp.where(half == 0, mine, other), jnp.where(half == 0, other, mine)
    return jnp.concatenate([low, high], axis=axis)


def after(value, *others):
    return lax.optimization_barrier((value,) + others)[0] if others else value


def step(*values):
    return lax.optimization_barrier(values)


def gather_middle(held):
    middle = dp_bits()[1:-1]
    for bit in middle[:-1]:
        held = jnp.concatenate([held, swap(held, "dp", bit)], axis=0)
    return held, swap(held, "dp", middle[-1])


def gradient_rows(left, right, place, kind, *added):
    part = left.shape[1] // 4
    total = tokens_out(left[:, place * part : (place + 1) * part], right)
    for value in added:
        total = total + value.astype(jnp.float32)
    return total.astype(kind)


def low_bits(value):
    return value.astype(jnp.bfloat16)


def middle_sum(held, got):
    held = held + got.astype(jnp.float32)
    for bit in reversed(dp_bits()[1:-2]):
        count = held.shape[0] // 2
        sent = swap(low_bits(held[count:]), "dp", bit)
        held = held[:count] + sent.astype(jnp.float32)
    count = held.shape[0] // 2
    return held[:count], low_bits(held[count:])


def kept_and_sent(held, tensor_at, bit, kind):
    mine, other = halves(held, (tensor_at // bit) % 2, 1)
    return mine, other.astype(kind)


def share_tokens(terms, tensor_at):
    held = terms
    for bit in (1, 2):
        mine, other = kept_and_sent(held, tensor_at, bit, jnp.float32)
        held = mine + swap(other, "tensor", bit)
    return held[0] + swap(held[1], "dp", PAIR)


def flip_pairs(values):
    blocks = lax.axis_size("dp")
    width = values.shape[-1] // blocks
    pieces = [values[..., (place ^ 1) * width : ((place ^ 1) + 1) * width] for place in range(blocks)]
    return jnp.concatenate(pieces, axis=-1)


def whole_tokens(values, tensor_at):
    for bit in (2, 1):
        values = join_halves(values, swap(values, "tensor", bit), (tensor_at // bit) % 2, 0)
    return values


def shards(
    block_input,
    out_grad,
    seg_ids,
    slot_live,
    norm_gain,
    z_weight,
    x_weight,
    bc_weight,
    dt_weight,
    conv_x,
    conv_bc,
    head_params,
    gated_gain,
    out_weight,
    norm_gain_sq,
    z_rows,
    z_cols,
    x_rows,
    x_cols,
    bc_rows,
    bc_cols,
    dt_rows,
    dt_cols,
    conv_x_sq,
    conv_bc_sq,
    head_sq,
    gated_gain_sq,
    out_rows,
    out_cols,
):
    data_count = lax.axis_size("dp")
    data_at = lax.axis_index("dp")
    tensor_at = lax.axis_index("tensor")
    half = (data_at // PAIR) % 2
    core = tensor_at % 2
    row_count = z_weight.shape[0]
    quarter = row_count // 4
    slot_tokens = block_input.shape[1]
    f32, bf16 = jnp.float32, jnp.bfloat16

    share = slot_tokens // 4
    share_at = (core * 2 + tensor_at // 2) * share
    last_bit = dp_bits()[-1]

    def share_of(values):
        return lax.dynamic_slice_in_dim(values, share_at, share, 0)

    def halves_of(weight):
        return halves(weight.astype(bf16), half, 1)

    def rows_of(*pieces):
        return jnp.concatenate(pieces, axis=0)

    whole_numbers = jnp.concatenate(
        [seg_ids[0], jnp.broadcast_to(slot_live, (8 * 128 - slot_tokens,))]
    ).astype(bf16).reshape(-1, 128)
    dt_rows_low = dt_weight.astype(bf16).T
    bc_mine = lax.dynamic_slice_in_dim(bc_weight.astype(bf16), tensor_at * quarter, quarter, 0)
    small = rows_of(bc_mine.reshape(-1, 128), dt_rows_low.reshape(-1, 128))
    small_count = small.shape[0]
    x_mine, x_other = halves_of(x_weight)
    small_far = swap(rows_of(small, whole_numbers), "dp", PAIR)
    x_far = swap(x_other, "dp", PAIR)
    small_far, x_far, x_mine, small, z_weight, out_weight, block_input, out_grad = step(
        small_far, x_far, x_mine, small, z_weight, out_weight, block_input, out_grad
    )

    far_numbers = small_far[small_count:].astype(jnp.int32)
    segments = jnp.stack([seg_ids[0], far_numbers.reshape(-1)[:slot_tokens]])
    live = jnp.stack([slot_live[0], far_numbers[-1, 0]]).astype(f32)
    small = jnp.stack([small, small_far[:small_count]])
    for bit in dp_bits()[1:-1]:
        small = rows_of(small, swap(small, "dp", bit))
    x_held, x_got = gather_middle(rows_of(x_mine, x_far))
    x_first = swap(x_held, "dp", last_bit)
    z_mine, z_other = halves_of(z_weight)
    out_mine, out_other = halves_of(out_weight)
    in_share, grad_share = share_of(block_input[0]), share_of(out_grad[0])
    marks, doc_rows = document_marks(segments)
    taps_x, _ = halves(conv_x, half, 1)
    per_head, _ = halves(head_params, half, 1)
    gain_inner, _ = halves(gated_gain, half, 0)
    head_count = per_head.shape[1]
    head_rows = jnp.pad(per_head, ((0, 5), (0, 128 - head_count)))
    vectors = jnp.concatenate(
        [taps_x, gain_inner[None], jnp.repeat(per_head[2], WIDTH)[None], jnp.zeros((2, taps_x.shape[1]))]
    )
    marks, doc_rows, head_rows, vectors, z_mine, out_mine = step(
        marks, doc_rows, head_rows, vectors, z_mine, out_mine
    )
    gain_rel = to_relative(norm_gain, data_at)
    own_rel = to_relative(block_input[0], data_at).astype(f32)
    x_got, x_first, small, z_other, in_share, grad_share, out_other, own_rel, marks, vectors = step(
        x_got, x_first, small, z_other, in_share, grad_share, out_other, own_rel, marks, vectors
    )

    x_second = swap(x_got, "dp", last_bit)
    small = rows_of(small, swap(small, "dp", last_bit))
    z_far = swap(z_other, "dp", PAIR)
    in_far = swap(in_share, "dp", PAIR)
    bc_piece_rows = quarter * bc_weight.shape[1] // 128
    bc_held = small[:, :bc_piece_rows].reshape(data_count, quarter, -1)
    x_second, small, z_far, in_far, z_mine, grad_share, out_other, bc_held = step(
        x_second, small, z_far, in_far, z_mine, grad_share, out_other, bc_held
    )

    z_held, z_got = gather_middle(rows_of(z_mine, z_far))
    z_first = swap(z_held, "dp", last_bit)
    in_far = join_halves(in_far, swap(in_far, "tensor", 2), tensor_at // 2, 0)
    bc_held = join_halves(bc_held, swap(bc_held, "tensor", 1), core, 1)
    low_x = rows_of(x_held, x_got, x_first, x_second)
    z_got, z_first, in_far, bc_held, grad_share, out_other, low_x = step(
        z_got, z_first, in_far, bc_held, grad_share, out_other, low_x
    )

    z_second = swap(z_got, "dp", last_bit)
    out_far = swap(out_other, "dp", PAIR)
    grad_far = swap(grad_share, "dp", PAIR)
    in_far = join_halves(in_far, swap(in_far, "tensor", 1), core, 0)
    bc_held = join_halves(bc_held, swap(bc_held, "tensor", 2), tensor_at // 2, 1)
    low_bc = bc_held.reshape(data_count * row_count, -1)
    in_rel = jnp.stack([own_rel, to_relative(in_far, data_at).astype(f32)])
    mean_square = jnp.mean(in_rel * in_rel, axis=-1, keepdims=True)
    normed_low = (in_rel * lax.rsqrt(mean_square + norm_eps) * gain_rel).astype(bf16)
    z_second, out_far, grad_far, normed_low = step(z_second, out_far, grad_far, normed_low)
    low_z = rows_of(z_held, z_got, z_first, z_second)
    out_held, out_got = gather_middle(rows_of(out_mine, out_far))
    out_first = swap(out_held, "dp", last_bit)
    grad_far = join_halves(grad_far, swap(grad_far, "tensor", 2), tensor_at // 2, 0)
    low_out = rows_of(out_held, out_got, out_first, swap(out_got, "dp", last_bit))
    grad_far = join_halves(grad_far, swap(grad_far, "tensor", 1), core, 0)
    both_grad = jnp.stack([out_grad[0], grad_far])

    low_dt = (
        small[:, bc_piece_rows:].reshape(data_count, dt_weight.shape[1], row_count).transpose(1, 0, 2)
    ).reshape(dt_weight.shape[1], -1)
    low_dt, _ = halves(low_dt, half, 0)
    low_dt = jnp.pad(low_dt, ((0, 128 - head_count), (0, 0)))
    normed_flat = normed_low.reshape(-1, normed_low.shape[-1])
    tokens = normed_flat.shape[0]

    def per_slot(values):
        return values.reshape(2, slot_tokens, -1)

    bc_raw = per_slot(jnp.dot(normed_flat, low_bc, preferred_element_type=f32))
    dt_raw = per_slot(rows_times(normed_flat, low_dt))
    x_raw = per_slot(jnp.dot(normed_flat, low_x, preferred_element_type=f32))
    gate_z = per_slot(jnp.dot(normed_flat, low_z, preferred_element_type=f32))
    common = (marks, doc_rows, bc_raw, dt_raw, conv_bc, head_rows, x_raw, gate_z, vectors)
    scaled_both, scanned, square_parts = mixer_forward(common)
    scaled_low = scaled_both.reshape(tokens, -1)

    projected = per_slot(rows_times(scaled_low, low_out))
    cot_rel = to_relative(both_grad, data_at) * live.astype(bf16)[:, None, None]
    totals = jnp.stack([jnp.sum(square_parts, axis=-1), jnp.sum(cot_rel.astype(f32) * projected, axis=-1)], axis=1)
    totals = totals + swap(totals, "tensor", 1)
    _, leaving = kept_and_sent(projected, tensor_at, 1, bf16)
    arriving = swap(after(leaving, totals), "tensor", 1)
    totals = totals + swap(totals, "tensor", 2)
    totals = totals + swap(totals, "dp", PAIR)[::-1]
    total_squares, rms_grad = totals[:, 0], totals[:, 1]
    inv_rms = lax.rsqrt(total_squares / INNER + norm_eps)
    squares_grad = rms_grad * -0.5 * inv_rms * inv_rms * inv_rms / INNER
    proj_grad = (cot_rel.astype(f32) * inv_rms[:, :, None]).astype(bf16).reshape(tokens, -1)
    scaled_grad = per_slot(jnp.dot(proj_grad, low_out, preferred_element_type=f32))

    part = low_out.shape[0] // 4
    middle_bit = dp_bits()[-2]

    def across(value, bit):
        return swap(value, "dp", bit)

    out_sent = [gradient_rows(proj_grad, scaled_low, place, bf16) for place in (3, 2)]
    out_passed, out_kept = [swap(value, "dp", last_bit) for value in out_sent]
    gradients = (
        after(scaled_grad, *out_sent, arriving),
        jnp.broadcast_to(squares_grad[:, :, None], (2, slot_tokens, 8)),
    )
    backward = mixer_backward(common, scanned, *gradients, 0)
    proj_later, out_passed, projected, *backward = step(proj_grad, out_passed, projected, *backward)
    shared, _ = kept_and_sent(projected, tensor_at, 1, bf16)
    shared, leaving = kept_and_sent(shared + arriving.astype(f32), tensor_at, 2, bf16)
    out_middle = gradient_rows(proj_later, scaled_low, 1, bf16, out_passed)
    out_middle, leaving, *backward = step(out_middle, leaving, *backward)
    out_got = across(out_middle, middle_bit)
    arriving = swap(leaving, "tensor", 2)
    inv_mine = lax.dynamic_slice_in_dim(inv_rms[0], share_at, share, 0)
    in_mine = to_relative(share_of(block_input[0]), data_at).astype(f32)
    cot_mine = to_relative(share_of(out_grad[0]), data_at).astype(f32) * live[0]
    z_both, x_both, bc_grad_part, dt_both, vector_terms, taps_bc_terms, head_terms = mixer_backward(
        common, scanned, *gradients, 1, backward
    )
    x_both, z_both, bc_grad_part, out_kept, arriving = step(
        x_both, z_both, bc_grad_part, out_kept, arriving
    )
    vector_terms = jnp.sum(vector_terms, axis=0)
    convx_slot, gated_slot = vector_terms[:4], vector_terms[4]
    convbc_part = jnp.sum(taps_bc_terms, axis=0)[:4]
    head_slot = jnp.concatenate(
        [
            jnp.sum(head_terms, axis=0)[:2, :head_count],
            jnp.sum(vector_terms[5].reshape(head_count, -1), axis=1)[None],
        ]
    )
    bc_kept, bc_leaving = kept_and_sent(bc_grad_part, tensor_at, 1, f32)
    bc_arriving = swap(bc_leaving, "tensor", 1)
    z_low = z_both.reshape(tokens, -1)
    x_low = x_both.reshape(tokens, -1)
    dt_low = dt_both.astype(bf16).reshape(tokens, -1)
    matrices = (low_z, low_x, low_dt)
    x_sent = gradient_rows(normed_flat, x_low, 3, bf16)
    x_low, z_low, x_sent, bc_arriving, out_got = step(x_low, z_low, x_sent, bc_arriving, out_got)

    x_passed = swap(x_sent, "dp", last_bit)
    bc_kept, bc_leaving = kept_and_sent(bc_kept + bc_arriving, tensor_at, 2, f32)
    bc_arriving = swap(bc_leaving, "tensor", 2)
    x_low, z_low, bc_leaving = step(x_low, z_low, bc_leaving)
    z_sent = gradient_rows(normed_flat, z_low, 3, bf16)
    both_sent = jnp.concatenate(
        [gradient_rows(normed_flat, values, 2, bf16) for values in (x_low, z_low)], axis=0
    )
    x_low, z_low, z_sent, both_sent, bc_arriving, arriving = step(
        x_low, z_low, z_sent, both_sent, bc_arriving, arriving
    )

    bc_kept = bc_kept + bc_arriving
    bc_far = swap(bc_kept[1], "dp", PAIR)
    shared = shared + arriving.astype(f32)
    shared_leaving = low_bits(shared[1])
    out_mine, out_leaving = middle_sum(gradient_rows(proj_later, scaled_low, 0, f32, out_kept), out_got)
    x_low, z_low, shared_leaving, out_mine, out_leaving = step(
        x_low, z_low, shared_leaving, out_mine, out_leaving
    )
    out_far = across(out_leaving, PAIR)
    projected_far = across(shared_leaving, PAIR)
    input_leaving = input_terms(1 - core, z_low, x_low, dt_low, *matrices)
    x_low, z_low, x_passed, input_leaving, bc_far, out_far, projected_far = step(
        x_low, z_low, x_passed, input_leaving, bc_far, out_far, projected_far
    )

    z_passed = swap(z_sent, "dp", last_bit)
    x_middle = gradient_rows(normed_flat, x_low, 1, bf16, x_passed)
    x_got = across(x_middle, middle_bit)
    input_arriving = swap(input_leaving, "tensor", 1)
    bc_low_mine = (bc_kept[0] + bc_far).astype(bf16)
    bc_far = swap(bc_low_mine, "tensor", 2)
    x_low, z_low, x_middle, bc_far = step(x_low, z_low, x_middle, bc_far)
    projected_mine = shared[0] + flip_pairs(projected_far.astype(f32))
    output = from_relative((in_mine + inv_mine[:, None] * projected_mine).astype(bf16), data_at)
    output_far = swap(output, "tensor", 2)
    input_kept = input_terms(core, z_low, x_low, dt_low, *matrices)
    out_share = join_halves(out_mine, out_far.astype(f32), half, 1)
    x_low, z_low, input_kept, z_passed, input_arriving, output_far, out_share = step(
        x_low, z_low, input_kept, z_passed, input_arriving, output_far, out_share
    )

    z_middle = gradient_rows(normed_flat, z_low, 1, bf16, z_passed)
    z_got = across(z_middle, middle_bit)
    both_kept = swap(both_sent, "dp", last_bit)
    bc_low = join_halves(bc_low_mine, bc_far, tensor_at // 2, 0)
    bc_far = swap(bc_low, "tensor", 1)
    x_low, z_low, z_middle, bc_low = step(x_low, z_low, z_middle, bc_low)
    input_kept, input_leaving = kept_and_sent(input_kept + input_arriving, tensor_at, 2, bf16)
    dt_part = tokens_out(dt_low, normed_flat)[:head_count]
    bc_far, dt_part, input_kept, input_leaving = step(bc_far, dt_part, input_kept, input_leaving)

    input_arriving = swap(input_leaving, "tensor", 2)
    bc_low = join_halves(bc_low, bc_far, core, 0)
    bc_columns = bc_low.shape[1] // 4
    bc_part = tokens_out(
        lax.dynamic_slice_in_dim(bc_low, tensor_at * bc_columns, bc_columns, 1), normed_low[0]
    )
    held = jnp.concatenate([bc_part, dt_part], axis=0)
    held = jnp.stack(
        [held[:, block * row_count : (block + 1) * row_count] for block in range(data_count)]
    )
    count = held.shape[0] // 2
    held = held[:count] + swap(held[count:], "dp", last_bit)
    output = join_halves(output, output_far, tensor_at // 2, 0)
    held, both_kept, x_got, output = step(held, both_kept, x_got, output)
    output_far = swap(output, "tensor", 1)
    for bit in reversed(dp_bits()[1:-1]):
        count = held.shape[0] // 2
        held = held[:count] + swap(held[count:], "dp", bit)
    x_terms = gradient_rows(normed_flat, x_low, 0, f32, both_kept[:part])
    z_terms = gradient_rows(normed_flat, z_low, 0, f32, both_kept[part:])
    x_mine, x_leaving = middle_sum(x_terms, x_got)
    input_mine = input_kept + input_arriving.astype(f32)
    input_leaving = low_bits(input_mine[1])
    z_terms, x_leaving, input_leaving = step(z_terms, x_leaving, input_leaving)

    input_far = swap(input_leaving, "dp", PAIR)
    output = join_halves(output, output_far, core, 0)
    small_far = swap(held[1], "dp", PAIR)
    z_mine, z_leaving = middle_sum(z_terms, z_got)
    z_leaving, small_far, input_far = step(z_leaving, small_far, input_far)
    both_far = across(jnp.concatenate([x_leaving, z_leaving], axis=0), PAIR)
    normed_grad = (
        input_mine[0] + flip_pairs(input_far.astype(f32)) + rows_times(bc_low_mine, low_bc)
    )

    _, norm_pull = jax.vjp(norm_input, in_mine, gain_rel)
    block_grad, gain_slot = norm_pull(normed_grad)
    input_grad = from_relative((cot_mine + block_grad).astype(bf16), data_at)
    both_far, gain_slot, output = step(both_far, gain_slot, output)
    x_share = join_halves(x_mine, both_far[: x_mine.shape[0]].astype(f32), half, 1)
    z_share = join_halves(z_mine, both_far[x_mine.shape[0] :].astype(f32), half, 1)

    bc_share = held[0, :bc_columns] + small_far[:bc_columns]
    dt_share = join_halves(held[0, bc_columns:], small_far[bc_columns:], half, 0).T
    bc_share = join_halves(bc_share, swap(bc_share, "tensor", 1), core, 0)
    bc_share = join_halves(bc_share, swap(bc_share, "tensor", 2), tensor_at // 2, 0).T

    def in_half(values):
        return join_halves(values, jnp.zeros_like(values), half, values.ndim - 1)

    def packed_sum(pieces, axis_bits):
        rows = []
        for piece in pieces:
            flat = piece.reshape(-1)
            rows.append(jnp.pad(flat, (0, -flat.size % 128)).reshape(-1, 128))
        total = jnp.concatenate(rows, axis=0)
        for axis, bits in axis_bits:
            total = add_over(total, axis, bits)
        result, at = [], 0
        for piece, row in zip(pieces, rows):
            part = total[at : at + row.shape[0]]
            if piece.size % 128:
                part = part[0, : piece.size]
            result.append(part.reshape(piece.shape))
            at += row.shape[0]
        return result

    norm_sum, convbc_sum = packed_sum(
        [from_relative(gain_slot, data_at), convbc_part], [("tensor", (1, 2))]
    )
    z_share, bc_share, norm_sum, convbc_sum = step(z_share, bc_share, norm_sum, convbc_sum)
    z_square = z_share * z_share + tiny_eps
    x_square = x_share * x_share + tiny_eps
    bc_square = bc_share * bc_share + tiny_eps
    dt_square = dt_share * dt_share + tiny_eps
    out_square = out_share * out_share + tiny_eps
    row_sums = jnp.stack(
        [
            jnp.sum(z_square, axis=1),
            jnp.sum(x_square, axis=1),
            jnp.sum(dt_square, axis=1),
            jnp.sum(out_square, axis=1),
        ]
    )
    z_row_sum, x_row_sum, dt_row_sum, out_row_sum = add_over(row_sums, "tensor", (1, 2))
    bc_row_sum = jnp.sum(bc_square, axis=1)

    (
        norm_total,
        convbc_total,
        gated_total,
        convx_total,
        z_col_sum,
        x_col_sum,
        out_col_sum,
        bc_col_sum,
        dt_col_sum,
        head_total,
    ) = packed_sum(
        [
            norm_sum,
            convbc_sum,
            in_half(gated_slot),
            in_half(convx_slot),
            jnp.sum(z_square, axis=0),
            jnp.sum(x_square, axis=0),
            jnp.sum(out_square, axis=0),
            jnp.sum(bc_square, axis=0),
            jnp.sum(dt_square, axis=0),
            in_half(head_slot),
        ],
        [("dp", dp_bits())],
    )
    z_rows_new = mix_state(z_rows, z_row_sum / INNER)
    x_rows_new = mix_state(x_rows, x_row_sum / INNER)
    bc_rows_new = mix_state(bc_rows, bc_row_sum / (2 * STATE))
    dt_rows_new = mix_state(dt_rows, dt_row_sum / HEADS)
    out_rows_new = mix_state(out_rows, out_row_sum / INNER)
    z_cols_new = mix_state(z_cols, z_col_sum / D)
    x_cols_new = mix_state(x_cols, x_col_sum / D)
    bc_cols_new = mix_state(bc_cols, bc_col_sum / D)
    dt_cols_new = mix_state(dt_cols, dt_col_sum / D)
    out_cols_new = mix_state(out_cols, out_col_sum / D)
    norm_second = mix_state(norm_gain_sq, norm_total * norm_total + tiny_eps)
    gated_second = mix_state(gated_gain_sq, gated_total * gated_total + tiny_eps)
    convx_second = mix_state(conv_x_sq, convx_total * convx_total + tiny_eps)
    convbc_second = mix_state(conv_bc_sq, convbc_total * convbc_total + tiny_eps)
    head_second = mix_state(head_sq, head_total * head_total + tiny_eps)
    norm_unit = norm_total * lax.rsqrt(norm_second)
    gated_unit = gated_total * lax.rsqrt(gated_second)
    convx_unit = convx_total * lax.rsqrt(convx_second)
    convbc_unit = convbc_total * lax.rsqrt(convbc_second)
    head_unit = head_total * lax.rsqrt(head_second)
    z_unit = z_share * lax.rsqrt(z_rows_new[:, None] * z_cols_new[None, :])
    x_unit = x_share * lax.rsqrt(x_rows_new[:, None] * x_cols_new[None, :])
    bc_unit = bc_share * lax.rsqrt(bc_rows_new[:, None] * bc_cols_new[None, :])
    dt_unit = dt_share * lax.rsqrt(dt_rows_new[:, None] * dt_cols_new[None, :])
    out_unit = out_share * lax.rsqrt(out_rows_new[:, None] * out_cols_new[None, :])
    tensor_count = lax.axis_size("tensor")
    scalars = (
        (
            jnp.sum(z_unit * z_unit),
            jnp.sum(x_unit * x_unit),
            jnp.sum(bc_unit * bc_unit) / tensor_count,
            jnp.sum(dt_unit * dt_unit),
            jnp.sum(out_unit * out_unit),
            jnp.sum(gated_unit * gated_unit) / data_count,
            jnp.sum(convx_unit * convx_unit) / data_count,
            jnp.sum(head_unit * head_unit) / data_count,
        )
    )
    places = lax.broadcasted_iota(jnp.int32, (8, 128), 0)
    unit_sums = jnp.zeros((8, 128), f32)
    for place, value in enumerate(scalars):
        unit_sums = jnp.where(places == place, value, unit_sums)
    unit_sums = add_over(unit_sums, "tensor", (1, 2))
    unit_sums, input_grad, output = step(unit_sums, input_grad, output)
    input_far = swap(input_grad, "tensor", 2)
    unit_sums = add_over(unit_sums, "dp", dp_bits())
    input_far, unit_sums = step(input_far, unit_sums)
    input_grad = join_halves(input_grad, input_far, tensor_at // 2, 0)
    input_grad = join_halves(input_grad, swap(input_grad, "tensor", 1), core, 0)
    (
        z_total,
        x_total,
        bc_total_sq,
        dt_total,
        out_total,
        gated_sq_total,
        convx_sq_total,
        head_sq_total,
    ) = unit_sums[:, 0]
    norm_sq_total = jnp.sum(norm_unit * norm_unit)
    convbc_sq_total = jnp.sum(convbc_unit * convbc_unit)
    in_rate = D ** (-0.5)
    out_rate = INNER ** (-0.5)
    z_upd = -in_rate * normalized(z_unit, z_total, D * INNER)
    x_upd = -in_rate * normalized(x_unit, x_total, D * INNER)
    bc_upd = -in_rate * normalized(bc_unit, bc_total_sq, D * 2 * STATE)
    dt_upd = -in_rate * normalized(dt_unit, dt_total, D * HEADS)
    out_upd = -out_rate * normalized(out_unit, out_total, D * INNER)
    norm_upd = -vector_rate * normalized(norm_unit, norm_sq_total, D)
    gated_upd = -vector_rate * normalized(gated_unit, gated_sq_total, INNER)
    convx_upd = -vector_rate * normalized(convx_unit, convx_sq_total, KCONV * INNER)
    convbc_upd = -vector_rate * normalized(convbc_unit, convbc_sq_total, KCONV * 2 * STATE)
    head_upd = -vector_rate * normalized(head_unit, head_sq_total, 3 * HEADS)
    return (
        output[None],
        input_grad[None],
        norm_total,
        norm_upd,
        norm_second,
        z_share,
        z_upd,
        z_rows_new,
        z_cols_new,
        x_share,
        x_upd,
        x_rows_new,
        x_cols_new,
        bc_share,
        bc_upd,
        bc_rows_new,
        bc_cols_new,
        dt_share,
        dt_upd,
        dt_rows_new,
        dt_cols_new,
        convx_total,
        convx_upd,
        convx_second,
        convbc_total,
        convbc_upd,
        convbc_second,
        head_total,
        head_upd,
        head_second,
        gated_total,
        gated_upd,
        gated_second,
        out_share,
        out_upd,
        out_rows_new,
        out_cols_new,
    )


def solution(mesh):
    in_specs = (
        P("dp", None, None),
        P("dp", None, None),
        P("dp", None),
        P("dp"),
        P(),
        P("dp", "tensor"),
        P("dp", "tensor"),
        P("dp", None),
        P("dp", "tensor"),
        P(None, "tensor"),
        P(),
        P(None, "tensor"),
        P("tensor"),
        P("dp", "tensor"),
        P(),
        P("dp"),
        P("tensor"),
        P("dp"),
        P("tensor"),
        P("dp"),
        P(),
        P("dp"),
        P("tensor"),
        P(None, "tensor"),
        P(),
        P(None, "tensor"),
        P("tensor"),
        P("dp"),
        P("tensor"),
    )
    out_specs = (
        P("dp", None, None),
        P("dp", None, None),
        P(),
        P(),
        P(),
        P("dp", "tensor"),
        P("dp", "tensor"),
        P("dp"),
        P("tensor"),
        P("dp", "tensor"),
        P("dp", "tensor"),
        P("dp"),
        P("tensor"),
        P("dp", None),
        P("dp", None),
        P("dp"),
        P(),
        P("dp", "tensor"),
        P("dp", "tensor"),
        P("dp"),
        P("tensor"),
        P(None, "tensor"),
        P(None, "tensor"),
        P(None, "tensor"),
        P(),
        P(),
        P(),
        P(None, "tensor"),
        P(None, "tensor"),
        P(None, "tensor"),
        P("tensor"),
        P("tensor"),
        P("tensor"),
        P("dp", "tensor"),
        P("dp", "tensor"),
        P("dp"),
        P("tensor"),
    )
    return jax.shard_map(shards, mesh=mesh, in_specs=in_specs, out_specs=out_specs, check_vma=False)
```

```python
import jax
import jax.numpy as jnp
from jax import lax
from jax.experimental import pallas as pl
from jax.experimental.pallas import tpu as pltpu
from jax.sharding import PartitionSpec as P

D = 2048
HEADS = 64
STATE = 128
INNER = 4096
KCONV = 4


norm_eps = 1e-05
decay_rate = 0.5
tiny_eps = 1e-30
unit_eps = 1e-06
vector_rate = 0.05


LANES = 128
PART = 256
WIDTH = 64


def cost_of(micros):
    return pl.CostEstimate(flops=micros * 1_000_000_000, bytes_accessed=1 << 20, transcendentals=0)


def two_parts(values):
    high = values.astype(jnp.bfloat16)
    return high, (values - high.astype(jnp.float32)).astype(jnp.bfloat16)


def plain(left, right):
    return lax.dot_general(
        left, right, (((1,), (0,)), ((), ())), preferred_element_type=jnp.float32
    )


def turned(left, right):
    return lax.dot_general(
        left, right, (((1,), (1,)), ((), ())), preferred_element_type=jnp.float32
    )


def fine(product, left, right):
    left_high, left_low = two_parts(left)
    right_high, right_low = two_parts(right)
    return (
        product(left_high, right_high)
        + product(left_high, right_low)
        + product(left_low, right_high)
    )


def running_sum(values, backward):
    rows = lax.broadcasted_iota(jnp.int32, (PART, PART), 0)
    columns = lax.broadcasted_iota(jnp.int32, (PART, PART), 1)
    within = (rows <= columns) if backward else (rows >= columns)
    ones = within.astype(jnp.float32).astype(jnp.bfloat16)

    def inside(block):
        high, rest = block.astype(jnp.bfloat16), block
        total = plain(ones, high)
        rest = block - high.astype(jnp.float32)
        for _ in range(2):
            part = rest.astype(jnp.bfloat16)
            total = total + plain(ones, part)
            rest = rest - part.astype(jnp.float32)
        return total

    blocks = [inside(values[:PART]), inside(values[PART:])]
    if backward:
        blocks[0] = blocks[0] + blocks[1][0:1]
    else:
        blocks[1] = blocks[1] + blocks[0][PART - 1 : PART]
    return jnp.concatenate(blocks, axis=0)


def sigmoid(values):
    return 1.0 / (1.0 + jnp.exp(-values))


def conv_rows(values, taps, same):
    result = taps[0:1] * values
    for offset in range(1, 4):
        shifted = pltpu.roll(values, offset, 0)
        result = result + taps[offset : offset + 1] * (shifted * same[offset - 1])
    return result


def conv_rows_back(grad, values, taps, same):
    length = values.shape[0]
    result = taps[0:1] * grad
    tap_rows = [jnp.sum(grad * values, axis=0, keepdims=True)]
    for offset in range(1, 4):
        kept = grad * same[offset - 1]
        result = result + pltpu.roll(taps[offset : offset + 1] * kept, length - offset, 0)
        tap_rows.append(
            jnp.sum(kept * pltpu.roll(values, offset, 0), axis=0, keepdims=True)
        )
    return result, tap_rows


def softplus(values):
    return jnp.maximum(values, 0.0) + jnp.log1p(jnp.exp(-jnp.abs(values)))


def marks_of(marks_ref):
    marks = marks_ref[0]
    same = [marks[:, place : place + 1] for place in (1, 2, 3)]
    return marks[:, 0:1], same, marks[:, 4:5]


def prepare(transposed, marks_ref, row_ref, bc_ref, dt_ref, taps_bc_ref, head_ref,
            bc_pre_ref, bc_ref_out, dt_out, cum_wide, dt_wide, cum_rows, score, bias):
    doc, same, _ = marks_of(marks_ref)
    bc_pre = conv_rows(bc_ref[0], taps_bc_ref[...], same)
    bc = bc_pre * sigmoid(bc_pre)
    bc_pre_ref[...] = bc_pre
    bc_ref_out[...] = bc
    b_mat, c_mat = bc[:, :LANES], bc[:, LANES:]
    first, second = slice(0, PART), slice(PART, 2 * PART)
    for place, (out_rows, in_rows) in enumerate(((first, first), (second, second), (second, first))):
        if transposed:
            score[place] = fine(turned, b_mat[in_rows], c_mat[out_rows])
        else:
            score[place] = fine(turned, c_mat[out_rows], b_mat[in_rows])
    rows = lax.broadcasted_iota(jnp.int32, (PART, PART), 0)
    columns = lax.broadcasted_iota(jnp.int32, (PART, PART), 1)
    causal = (rows <= columns) if transposed else (rows >= columns)
    doc_row = row_ref[0][0:1]
    for place, part in enumerate((first, second)):
        seen = causal & (doc[part] == doc_row[:, part])
        bias[place] = jnp.where(seen, 0.0, -1e30)
    step = softplus(dt_ref[0] + head_ref[0:1])
    decay = step * -jnp.exp(head_ref[1:2])
    total = running_sum(decay, False)
    dt_out[...] = step
    flipped = total.T
    lane = lax.broadcasted_iota(jnp.int32, (2 * PART, LANES), 1)
    for pair in range(cum_wide.shape[0]):
        one, two = 2 * pair, 2 * pair + 1
        cum_wide[pair] = jnp.where(lane < WIDTH, total[:, one : one + 1], total[:, two : two + 1])
        dt_wide[pair] = jnp.where(lane < WIDTH, step[:, one : one + 1], step[:, two : two + 1])
        cum_rows[one] = flipped[one : one + 1]
        cum_rows[two] = flipped[two : two + 1]


def edge_weights(wide, in_last):
    edge = wide[PART - 1 : PART]
    after = jnp.exp(wide[PART:] - edge) * in_last[PART:]
    before = jnp.exp(edge - wide[:PART]) * in_last[:PART]
    return after, before


def forward_body(marks_ref, row_ref, bc_ref, dt_ref, taps_bc_ref, head_ref, x_ref, z_ref, vec_ref,
                 scaled_ref, scan_ref, squares_ref,
                 bc_pre, bc_act, dt_act, cum_wide, dt_wide, cum_rows, score, bias):
    pair = pl.program_id(1)

    @pl.when(pair == 0)
    def _():
        prepare(False, marks_ref, row_ref, bc_ref, dt_ref, taps_bc_ref, head_ref,
                bc_pre, bc_act, dt_act, cum_wide, dt_wide, cum_rows, score, bias)
        squares_ref[...] = jnp.zeros_like(squares_ref)

    _, same, in_last = marks_of(marks_ref)
    vec = vec_ref[...]
    pre = conv_rows(x_ref[0], vec[0:4], same)
    values = pre * sigmoid(pre)
    wide = cum_wide[pair]
    stepped = dt_wide[pair] * values
    high, low_part = two_parts(stepped)
    both = jnp.concatenate([high, low_part], axis=1)
    lane = lax.broadcasted_iota(jnp.int32, (PART, LANES), 1)
    blocks = []
    for place in range(2):
        part = slice(place * PART, (place + 1) * PART)
        answers = []
        for k in range(2):
            row = cum_rows[2 * pair + k][:, part]
            kernel = jnp.exp(wide[part, k * WIDTH : k * WIDTH + 1] - row + bias[place])
            mixing_high, mixing_low = two_parts(score[place] * kernel)
            answer = plain(mixing_high, both[part])
            answers.append(
                answer[:, :LANES] + answer[:, LANES:] + plain(mixing_low, high[part])
            )
        blocks.append(jnp.where(lane < WIDTH, answers[0], answers[1]))
    after, before = edge_weights(wide, in_last)
    blocks[1] = blocks[1] + after * fine(plain, score[2], before * stepped[:PART])
    scanned = jnp.concatenate(blocks, axis=0)
    scan_ref[0] = scanned
    gate = z_ref[0]
    gated = (scanned + vec[5:6] * values) * (gate * sigmoid(gate))
    squares_ref[0] = squares_ref[0] + gated * gated
    scaled_ref[0] = (gated * vec[4:5]).astype(scaled_ref.dtype)


def backward_body(marks_ref, row_ref, bc_ref, dt_ref, taps_bc_ref, head_ref, x_ref, z_ref, vec_ref,
                  scan_ref, grad_ref, sq_grad_ref,
                  z_out, x_out, bc_out, dt_out, vec_out, taps_bc_out, head_out,
                  bc_pre, bc_act, dt_act, cum_wide, dt_wide, cum_rows, score, bias,
                  score_grad, from_rows, from_columns, from_in):
    pair = pl.program_id(1)

    @pl.when(pair == 0)
    def _():
        prepare(True, marks_ref, row_ref, bc_ref, dt_ref, taps_bc_ref, head_ref,
                bc_pre, bc_act, dt_act, cum_wide, dt_wide, cum_rows, score, bias)
        score_grad[...] = jnp.zeros_like(score_grad)
        from_rows[...] = jnp.zeros_like(from_rows)
        from_columns[...] = jnp.zeros_like(from_columns)
        from_in[...] = jnp.zeros_like(from_in)

    _, same, in_last = marks_of(marks_ref)
    vec = vec_ref[...]
    taps, gain, skip = vec[0:4], vec[4:5], vec[5:6]
    x_raw = x_ref[0]
    pre = conv_rows(x_raw, taps, same)
    pre_sig = sigmoid(pre)
    values = pre * pre_sig
    wide = cum_wide[pair]
    step = dt_wide[pair]
    stepped = step * values
    gate = z_ref[0]
    gate_sig = sigmoid(gate)
    gate_act = gate * gate_sig
    scanned = scan_ref[0]
    mixed = scanned + skip * values
    gated = mixed * gate_act
    scaled_grad = grad_ref[0]
    gated_grad = scaled_grad * gain + 2.0 * sq_grad_ref[0][:, 0:1] * gated
    z_out[0] = (gated_grad * mixed * (gate_sig * (1.0 + gate * (1.0 - gate_sig)))).astype(z_out.dtype)
    grad = gated_grad * gate_act
    rows = [
        None, None, None, None,
        jnp.sum(scaled_grad * gated, axis=0, keepdims=True),
        jnp.sum(grad * values, axis=0, keepdims=True),
    ]
    high, low_part = two_parts(grad)
    both = jnp.concatenate([high, low_part], axis=1)
    lane = lax.broadcasted_iota(jnp.int32, (PART, LANES), 1)

    def add_exponents(head, out_part, in_part, terms):
        from_rows[head, :, out_part] += jnp.sum(terms, axis=0, keepdims=True)
        gone = jnp.sum(terms, axis=1, keepdims=True)
        from_columns[in_part] += jnp.where(lane == head, gone, 0.0)

    blocks = []
    for place in range(2):
        part = slice(place * PART, (place + 1) * PART)
        answers = []
        total = score_grad[place]
        for k in range(2):
            row = cum_rows[2 * pair + k][:, part]
            kernel = jnp.exp(row - wide[part, k * WIDTH : k * WIDTH + 1] + bias[place])
            mixing = score[place] * kernel
            mixing_high, mixing_low = two_parts(mixing)
            answer = plain(mixing_high, both[part])
            answers.append(
                answer[:, :LANES] + answer[:, LANES:] + plain(mixing_low, high[part])
            )
            own = (lane < WIDTH) if k == 0 else (lane >= WIDTH)
            own_high, own_low = two_parts(jnp.where(own, stepped[part], 0.0))
            pulled = turned(
                jnp.concatenate([own_high, own_high], axis=1), both[part]
            ) + turned(own_low, high[part])
            total = total + pulled * kernel
            add_exponents(2 * pair + k, part, part, pulled * mixing)
        score_grad[place] = total
        blocks.append(jnp.where(lane < WIDTH, answers[0], answers[1]))
    after, before = edge_weights(wide, in_last)
    late = after * grad[PART:]
    early = before * stepped[:PART]
    blocks[0] = blocks[0] + before * fine(plain, score[2], late)
    for k in range(2):
        own = (lane < WIDTH) if k == 0 else (lane >= WIDTH)
        pulled = fine(turned, jnp.where(own, early, 0.0), late)
        score_grad[2] = score_grad[2] + pulled
        add_exponents(2 * pair + k, slice(PART, 2 * PART), slice(0, PART), pulled * score[2])
    pulled_in = jnp.concatenate(blocks, axis=0)
    places = lax.broadcasted_iota(jnp.int32, (LANES, LANES), 0) // WIDTH + 2 * pair
    columns = lax.broadcasted_iota(jnp.int32, (LANES, LANES), 1)
    chosen = (places == columns).astype(jnp.float32).astype(jnp.bfloat16)
    chosen = jnp.concatenate([chosen, chosen], axis=0)
    from_in[...] += plain(jnp.concatenate(two_parts(values * pulled_in), axis=1), chosen)
    pre_grad = (skip * grad + step * pulled_in) * (pre_sig * (1.0 + pre * (1.0 - pre_sig)))
    x_grad, rows[:4] = conv_rows_back(pre_grad, x_raw, taps, same)
    x_out[0] = x_grad.astype(x_out.dtype)
    vec_out[0] = jnp.concatenate(rows + [jnp.zeros((2, LANES), jnp.float32)], axis=0)

    @pl.when(pair == pl.num_programs(1) - 1)
    def _():
        steps = dt_act[...]
        rate = -jnp.exp(head_ref[1:2])
        direct = from_in[...]
        heads = from_rows.shape[0]
        arrived = jnp.concatenate(
            [from_rows[head] for head in range(heads)]
            + [jnp.zeros((LANES - heads, 2 * PART), jnp.float32)],
            axis=0,
        ).T
        decay_grad = running_sum(arrived - from_columns[...], True)
        step_grad = (direct + rate * decay_grad) * sigmoid(dt_ref[0] + head_ref[0:1])
        dt_out[0] = step_grad
        head_out[0] = jnp.concatenate(
            [
                jnp.sum(step_grad, axis=0, keepdims=True),
                rate * jnp.sum(decay_grad * steps, axis=0, keepdims=True),
                jnp.zeros((6, LANES), jnp.float32),
            ],
            axis=0,
        )
        b_mat, c_mat = bc_act[:, :LANES], bc_act[:, LANES:]
        first, second, cross = score_grad[0], score_grad[1], score_grad[2]
        b_grad = jnp.concatenate(
            [
                fine(plain, first, c_mat[:PART]) + fine(plain, cross, c_mat[PART:]),
                fine(plain, second, c_mat[PART:]),
            ],
            axis=0,
        )
        c_grad = jnp.concatenate(
            [
                fine(plain, first.T, b_mat[:PART]),
                fine(plain, second.T, b_mat[PART:]) + fine(plain, cross.T, b_mat[:PART]),
            ],
            axis=0,
        )
        shape = bc_pre[...]
        slope = sigmoid(shape)
        slope = slope * (1.0 + shape * (1.0 - slope))
        bc_grad, tap_rows = conv_rows_back(
            jnp.concatenate([b_grad, c_grad], axis=1) * slope, bc_ref[0], taps_bc_ref[...], same
        )
        bc_out[0] = bc_grad
        taps_bc_out[0] = jnp.concatenate(
            tap_rows + [jnp.zeros((4, 2 * LANES), jnp.float32)], axis=0
        )


def slot_block(first, *shape):
    return pl.BlockSpec((1,) + shape, lambda slot, pair: (slot + first, 0, 0))


def whole_block(*shape):
    return pl.BlockSpec(shape, lambda slot, pair: (0,) * len(shape))


def pair_block(first, length):
    return pl.BlockSpec((1, length, LANES), lambda slot, pair: (slot + first, 0, pair))


def common_specs(first, length):
    return [
        slot_block(first, length, 8),
        slot_block(first, 8, length),
        slot_block(first, length, 2 * LANES),
        slot_block(first, length, LANES),
        whole_block(4, 2 * LANES),
        whole_block(8, LANES),
        pair_block(first, length),
        pair_block(first, length),
        pl.BlockSpec((8, LANES), lambda slot, pair: (0, pair)),
    ]


def common_scratch(length, pairs):
    return [
        pltpu.VMEM((length, 2 * LANES), jnp.float32),
        pltpu.VMEM((length, 2 * LANES), jnp.float32),
        pltpu.VMEM((length, LANES), jnp.float32),
        pltpu.VMEM((pairs, length, LANES), jnp.float32),
        pltpu.VMEM((pairs, length, LANES), jnp.float32),
        pltpu.VMEM((2 * pairs, 1, length), jnp.float32),
        pltpu.VMEM((3, PART, PART), jnp.float32),
        pltpu.VMEM((2, PART, PART), jnp.float32),
    ]


def mixer_forward(common, interpret=False):
    slots, length, width = common[6].shape
    pairs = width // LANES
    return pl.pallas_call(
        forward_body,
        grid=(slots, pairs),
        in_specs=common_specs(0, length),
        out_specs=[pair_block(0, length), pair_block(0, length), slot_block(0, length, LANES)],
        out_shape=[
            jax.ShapeDtypeStruct((slots, length, width), jnp.bfloat16),
            jax.ShapeDtypeStruct((slots, length, width), jnp.float32),
            jax.ShapeDtypeStruct((slots, length, LANES), jnp.float32),
        ],
        scratch_shapes=common_scratch(length, pairs),
        cost_estimate=cost_of(16),
        name="mixer_forward",
        interpret=interpret,
    )(*common)


def mixer_backward(common, scanned, scaled_grad, sq_grad, slot, earlier=(), interpret=False):
    slots, length, width = common[6].shape
    pairs = width // LANES
    given = len(common) + 3

    def body(*refs):
        backward_body(*refs[:given], *refs[given + len(earlier) :])

    return pl.pallas_call(
        body,
        grid=(1, pairs),
        in_specs=common_specs(slot, length)
        + [pair_block(slot, length), pair_block(slot, length), slot_block(slot, length, 8)]
        + [pl.BlockSpec(memory_space=pl.ANY) for _ in earlier],
        out_specs=[
            pair_block(slot, length),
            pair_block(slot, length),
            slot_block(slot, length, 2 * LANES),
            slot_block(slot, length, LANES),
            pl.BlockSpec((1, 8, LANES), lambda _, pair: (slot, 0, pair)),
            slot_block(slot, 8, 2 * LANES),
            slot_block(slot, 8, LANES),
        ],
        out_shape=[
            jax.ShapeDtypeStruct((slots, length, width), jnp.bfloat16),
            jax.ShapeDtypeStruct((slots, length, width), jnp.bfloat16),
            jax.ShapeDtypeStruct((slots, length, 2 * LANES), jnp.float32),
            jax.ShapeDtypeStruct((slots, length, LANES), jnp.float32),
            jax.ShapeDtypeStruct((slots, 8, width), jnp.float32),
            jax.ShapeDtypeStruct((slots, 8, 2 * LANES), jnp.float32),
            jax.ShapeDtypeStruct((slots, 8, LANES), jnp.float32),
        ],
        input_output_aliases={given + place: place for place in range(len(earlier))},
        scratch_shapes=common_scratch(length, pairs)
        + [
            pltpu.VMEM((3, PART, PART), jnp.float32),
            pltpu.VMEM((2 * pairs, 1, length), jnp.float32),
            pltpu.VMEM((length, LANES), jnp.float32),
            pltpu.VMEM((length, LANES), jnp.float32),
        ],
        cost_estimate=cost_of(16),
        name="mixer_backward",
        interpret=interpret,
    )(*common, scanned, scaled_grad, sq_grad, *earlier)


def input_body(place_ref, z_ref, x_ref, dt_ref, z_rows_ref, x_rows_ref, dt_rows_ref, *rest):
    del place_ref

    def flat(ref):
        return ref[...].reshape(-1, ref.shape[-1])

    total = (
        turned(flat(z_ref), z_rows_ref[...])
        + turned(flat(x_ref), x_rows_ref[...])
        + plain(flat(dt_ref), dt_rows_ref[...])
    ).reshape(rest[-1].shape)
    for added in rest[:-1]:
        total = total + added[...]
    rest[-1][...] = total


def input_terms(place, z_low, x_low, dt_low, low_z, low_x, low_dt, *added):
    tokens = z_low.shape[0] // 4
    width = low_z.shape[1]
    features = low_z.shape[0]
    block = features // 4

    def by_half(values):
        return values.reshape(2, 2, tokens, -1)

    def half_block(values):
        return pl.BlockSpec((2, 1, tokens, values.shape[1]), lambda at, where: (0, where[0], 0, 0))

    weight = pl.BlockSpec((block, width), lambda at, where: (at, 0))
    out = pl.BlockSpec((2, tokens, block), lambda at, where: (0, 0, at))
    return pl.pallas_call(
        input_body,
        grid_spec=pltpu.PrefetchScalarGridSpec(
            num_scalar_prefetch=1,
            grid=(4,),
            in_specs=[
                half_block(z_low),
                half_block(x_low),
                half_block(dt_low),
                weight,
                weight,
                pl.BlockSpec((low_dt.shape[0], block), lambda at, where: (0, at)),
            ]
            + [out] * len(added),
            out_specs=out,
        ),
        out_shape=jax.ShapeDtypeStruct((2, tokens, features), jnp.float32),
        cost_estimate=cost_of(6),
        name="input_terms",
    )(
        place.astype(jnp.int32).reshape(1),
        by_half(z_low),
        by_half(x_low),
        by_half(dt_low),
        low_z,
        low_x,
        low_dt,
        *added,
    )


def document_marks(segments):
    slots, length = segments.shape
    docs = segments.astype(jnp.float32)
    columns = [docs]
    for offset in (1, 2, 3):
        same = (segments[:, offset:] == segments[:, :-offset]).astype(jnp.float32)
        columns.append(jnp.pad(same, ((0, 0), (offset, 0))))
    columns.append((segments == segments[:, PART - 1 : PART]).astype(jnp.float32))
    zero = jnp.zeros_like(docs)
    marks = jnp.stack(columns + [zero] * 3, axis=-1)
    return marks, jnp.broadcast_to(docs[:, None, :], (slots, 8, length))


def norm_input(values, gain):
    mean_square = jnp.mean(values * values, axis=1, keepdims=True)
    return values * lax.rsqrt(mean_square + norm_eps) * gain


def rows_times(left, right):
    return lax.dot_general(
        left, right, (((1,), (1,)), ((), ())), preferred_element_type=jnp.float32
    )


def tokens_out(left, right):
    return lax.dot_general(
        left, right, (((0,), (0,)), ((), ())), preferred_element_type=jnp.float32
    )


def mix_state(old_state, fresh_term):
    return decay_rate * old_state + (1.0 - decay_rate) * fresh_term


def normalized(unit, square_total, entries):
    return unit * lax.rsqrt(square_total / entries + unit_eps)


def swap(value, axis, bit):
    size = lax.axis_size(axis)
    return lax.ppermute(value, axis, [(place, place ^ bit) for place in range(size)])


def add_over(value, axis, bits):
    for bit in bits:
        value = value + swap(value, axis, bit)
    return value


PAIR = 2


def dp_bits():
    count = lax.axis_size("dp")
    rest = [1 << place for place in reversed(range(count.bit_length() - 1)) if 1 << place != PAIR]
    return [PAIR] + rest


def block_masks():
    bits = dp_bits()
    return [
        sum(bit for place, bit in enumerate(bits) if (number >> place) & 1)
        for number in range(lax.axis_size("dp"))
    ]


def place_of(offset):
    return sum(
        ((offset // bit) % 2) << place for place, bit in enumerate(dp_bits())
    )


def to_relative(values, mine):
    blocks = lax.axis_size("dp")
    width = values.shape[-1] // blocks
    return jnp.concatenate(
        [
            lax.dynamic_slice_in_dim(values, (mine ^ mask) * width, width, values.ndim - 1)
            for mask in block_masks()
        ],
        axis=-1,
    )


def from_relative(values, mine):
    blocks = lax.axis_size("dp")
    width = values.shape[-1] // blocks
    return jnp.concatenate(
        [
            lax.dynamic_slice_in_dim(values, place_of(mine ^ block) * width, width, values.ndim - 1)
            for block in range(blocks)
        ],
        axis=-1,
    )


def halves(values, half, axis):
    width = values.shape[axis] // 2
    mine = lax.dynamic_slice_in_dim(values, half * width, width, axis)
    other = lax.dynamic_slice_in_dim(values, (1 - half) * width, width, axis)
    return mine, other


def join_halves(mine, other, half, axis):
    low, high = jnp.where(half == 0, mine, other), jnp.where(half == 0, other, mine)
    return jnp.concatenate([low, high], axis=axis)


def after(value, *others):
    return lax.optimization_barrier((value,) + others)[0] if others else value


def step(*values):
    return lax.optimization_barrier(values)


def gather_middle(held):
    middle = dp_bits()[1:-1]
    for bit in middle[:-1]:
        held = jnp.concatenate([held, swap(held, "dp", bit)], axis=0)
    return held, swap(held, "dp", middle[-1])


def gradient_rows(left, right, place, kind, *added):
    part = left.shape[1] // 4
    total = tokens_out(left[:, place * part : (place + 1) * part], right)
    for value in added:
        total = total + value.astype(jnp.float32)
    return total.astype(kind)


def low_bits(value):
    return value.astype(jnp.bfloat16)


def middle_sum(held, got):
    held = held + got.astype(jnp.float32)
    for bit in reversed(dp_bits()[1:-2]):
        count = held.shape[0] // 2
        sent = swap(low_bits(held[count:]), "dp", bit)
        held = held[:count] + sent.astype(jnp.float32)
    count = held.shape[0] // 2
    return held[:count], low_bits(held[count:])


def kept_and_sent(held, tensor_at, bit, kind):
    mine, other = halves(held, (tensor_at // bit) % 2, 1)
    return mine, other.astype(kind)


def share_tokens(terms, tensor_at):
    held = terms
    for bit in (1, 2):
        mine, other = kept_and_sent(held, tensor_at, bit, jnp.float32)
        held = mine + swap(other, "tensor", bit)
    return held[0] + swap(held[1], "dp", PAIR)


def flip_pairs(values):
    blocks = lax.axis_size("dp")
    width = values.shape[-1] // blocks
    pieces = [values[..., (place ^ 1) * width : ((place ^ 1) + 1) * width] for place in range(blocks)]
    return jnp.concatenate(pieces, axis=-1)


def whole_tokens(values, tensor_at):
    for bit in (2, 1):
        values = join_halves(values, swap(values, "tensor", bit), (tensor_at // bit) % 2, 0)
    return values


def shards(
    block_input,
    out_grad,
    seg_ids,
    slot_live,
    norm_gain,
    z_weight,
    x_weight,
    bc_weight,
    dt_weight,
    conv_x,
    conv_bc,
    head_params,
    gated_gain,
    out_weight,
    norm_gain_sq,
    z_rows,
    z_cols,
    x_rows,
    x_cols,
    bc_rows,
    bc_cols,
    dt_rows,
    dt_cols,
    conv_x_sq,
    conv_bc_sq,
    head_sq,
    gated_gain_sq,
    out_rows,
    out_cols,
):
    data_count = lax.axis_size("dp")
    data_at = lax.axis_index("dp")
    tensor_at = lax.axis_index("tensor")
    half = (data_at // PAIR) % 2
    core = tensor_at % 2
    row_count = z_weight.shape[0]
    quarter = row_count // 4
    slot_tokens = block_input.shape[1]
    f32, bf16 = jnp.float32, jnp.bfloat16

    share = slot_tokens // 4
    share_at = (core * 2 + tensor_at // 2) * share
    last_bit = dp_bits()[-1]

    def share_of(values):
        return lax.dynamic_slice_in_dim(values, share_at, share, 0)

    def halves_of(weight):
        return halves(weight.astype(bf16), half, 1)

    def rows_of(*pieces):
        return jnp.concatenate(pieces, axis=0)

    whole_numbers = jnp.concatenate(
        [seg_ids[0], jnp.broadcast_to(slot_live, (8 * 128 - slot_tokens,))]
    ).astype(bf16).reshape(-1, 128)
    dt_rows_low = dt_weight.astype(bf16).T
    bc_mine = lax.dynamic_slice_in_dim(bc_weight.astype(bf16), tensor_at * quarter, quarter, 0)
    small = rows_of(bc_mine.reshape(-1, 128), dt_rows_low.reshape(-1, 128))
    small_count = small.shape[0]
    x_mine, x_other = halves_of(x_weight)
    small_far = swap(rows_of(small, whole_numbers), "dp", PAIR)
    x_far = swap(x_other, "dp", PAIR)
    small_far, x_far, x_mine, small, z_weight, out_weight, block_input, out_grad = step(
        small_far, x_far, x_mine, small, z_weight, out_weight, block_input, out_grad
    )

    far_numbers = small_far[small_count:].astype(jnp.int32)
    segments = jnp.stack([seg_ids[0], far_numbers.reshape(-1)[:slot_tokens]])
    live = jnp.stack([slot_live[0], far_numbers[-1, 0]]).astype(f32)
    small = jnp.stack([small, small_far[:small_count]])
    for bit in dp_bits()[1:-1]:
        small = rows_of(small, swap(small, "dp", bit))
    x_held, x_got = gather_middle(rows_of(x_mine, x_far))
    x_first = swap(x_held, "dp", last_bit)
    z_mine, z_other = halves_of(z_weight)
    out_mine, out_other = halves_of(out_weight)
    in_share, grad_share = share_of(block_input[0]), share_of(out_grad[0])
    marks, doc_rows = document_marks(segments)
    taps_x, _ = halves(conv_x, half, 1)
    per_head, _ = halves(head_params, half, 1)
    gain_inner, _ = halves(gated_gain, half, 0)
    head_count = per_head.shape[1]
    head_rows = jnp.pad(per_head, ((0, 5), (0, 128 - head_count)))
    vectors = jnp.concatenate(
        [taps_x, gain_inner[None], jnp.repeat(per_head[2], WIDTH)[None], jnp.zeros((2, taps_x.shape[1]))]
    )
    marks, doc_rows, head_rows, vectors, z_mine, out_mine = step(
        marks, doc_rows, head_rows, vectors, z_mine, out_mine
    )
    gain_rel = to_relative(norm_gain, data_at)
    own_rel = to_relative(block_input[0], data_at).astype(f32)
    x_got, x_first, small, z_other, in_share, grad_share, out_other, own_rel, marks, vectors = step(
        x_got, x_first, small, z_other, in_share, grad_share, out_other, own_rel, marks, vectors
    )

    x_second = swap(x_got, "dp", last_bit)
    small = rows_of(small, swap(small, "dp", last_bit))
    z_far = swap(z_other, "dp", PAIR)
    in_far = swap(in_share, "dp", PAIR)
    bc_piece_rows = quarter * bc_weight.shape[1] // 128
    bc_held = small[:, :bc_piece_rows].reshape(data_count, quarter, -1)
    x_second, small, z_far, in_far, z_mine, grad_share, out_other, bc_held = step(
        x_second, small, z_far, in_far, z_mine, grad_share, out_other, bc_held
    )

    z_held, z_got = gather_middle(rows_of(z_mine, z_far))
    z_first = swap(z_held, "dp", last_bit)
    in_far = join_halves(in_far, swap(in_far, "tensor", 2), tensor_at // 2, 0)
    bc_held = join_halves(bc_held, swap(bc_held, "tensor", 1), core, 1)
    low_x = rows_of(x_held, x_got, x_first, x_second)
    z_got, z_first, in_far, bc_held, grad_share, out_other, low_x = step(
        z_got, z_first, in_far, bc_held, grad_share, out_other, low_x
    )

    z_second = swap(z_got, "dp", last_bit)
    out_far = swap(out_other, "dp", PAIR)
    grad_far = swap(grad_share, "dp", PAIR)
    in_far = join_halves(in_far, swap(in_far, "tensor", 1), core, 0)
    bc_held = join_halves(bc_held, swap(bc_held, "tensor", 2), tensor_at // 2, 1)
    low_bc = bc_held.reshape(data_count * row_count, -1)
    in_rel = jnp.stack([own_rel, to_relative(in_far, data_at).astype(f32)])
    mean_square = jnp.mean(in_rel * in_rel, axis=-1, keepdims=True)
    normed_low = (in_rel * lax.rsqrt(mean_square + norm_eps) * gain_rel).astype(bf16)
    z_second, out_far, grad_far, normed_low = step(z_second, out_far, grad_far, normed_low)
    low_z = rows_of(z_held, z_got, z_first, z_second)
    out_held, out_got = gather_middle(rows_of(out_mine, out_far))
    out_first = swap(out_held, "dp", last_bit)
    grad_far = join_halves(grad_far, swap(grad_far, "tensor", 2), tensor_at // 2, 0)
    low_out = rows_of(out_held, out_got, out_first, swap(out_got, "dp", last_bit))
    grad_far = join_halves(grad_far, swap(grad_far, "tensor", 1), core, 0)
    both_grad = jnp.stack([out_grad[0], grad_far])

    low_dt = (
        small[:, bc_piece_rows:].reshape(data_count, dt_weight.shape[1], row_count).transpose(1, 0, 2)
    ).reshape(dt_weight.shape[1], -1)
    low_dt, _ = halves(low_dt, half, 0)
    low_dt = jnp.pad(low_dt, ((0, 128 - head_count), (0, 0)))
    normed_flat = normed_low.reshape(-1, normed_low.shape[-1])
    tokens = normed_flat.shape[0]

    def per_slot(values):
        return values.reshape(2, slot_tokens, -1)

    bc_raw = per_slot(jnp.dot(normed_flat, low_bc, preferred_element_type=f32))
    dt_raw = per_slot(rows_times(normed_flat, low_dt))
    x_raw = per_slot(jnp.dot(normed_flat, low_x, preferred_element_type=f32))
    gate_z = per_slot(jnp.dot(normed_flat, low_z, preferred_element_type=f32))
    common = (marks, doc_rows, bc_raw, dt_raw, conv_bc, head_rows, x_raw, gate_z, vectors)
    scaled_both, scanned, square_parts = mixer_forward(common)
    scaled_low = scaled_both.reshape(tokens, -1)

    projected = per_slot(rows_times(scaled_low, low_out))
    cot_rel = to_relative(both_grad, data_at) * live.astype(bf16)[:, None, None]
    totals = jnp.stack([jnp.sum(square_parts, axis=-1), jnp.sum(cot_rel.astype(f32) * projected, axis=-1)], axis=1)
    totals = totals + swap(totals, "tensor", 1)
    _, leaving = kept_and_sent(projected, tensor_at, 1, bf16)
    arriving = swap(after(leaving, totals), "tensor", 1)
    totals = totals + swap(totals, "tensor", 2)
    totals = totals + swap(totals, "dp", PAIR)[::-1]
    total_squares, rms_grad = totals[:, 0], totals[:, 1]
    inv_rms = lax.rsqrt(total_squares / INNER + norm_eps)
    squares_grad = rms_grad * -0.5 * inv_rms * inv_rms * inv_rms / INNER
    proj_grad = (cot_rel.astype(f32) * inv_rms[:, :, None]).astype(bf16).reshape(tokens, -1)
    scaled_grad = per_slot(jnp.dot(proj_grad, low_out, preferred_element_type=f32))

    part = low_out.shape[0] // 4
    middle_bit = dp_bits()[-2]

    def across(value, bit):
        return swap(value, "dp", bit)

    out_sent = [gradient_rows(proj_grad, scaled_low, place, bf16) for place in (3, 2)]
    out_passed, out_kept = [swap(value, "dp", last_bit) for value in out_sent]
    gradients = (
        after(scaled_grad, *out_sent, arriving),
        jnp.broadcast_to(squares_grad[:, :, None], (2, slot_tokens, 8)),
    )
    backward = mixer_backward(common, scanned, *gradients, 0)
    proj_later, out_passed, projected, *backward = step(proj_grad, out_passed, projected, *backward)
    shared, _ = kept_and_sent(projected, tensor_at, 1, bf16)
    shared, leaving = kept_and_sent(shared + arriving.astype(f32), tensor_at, 2, bf16)
    out_middle = gradient_rows(proj_later, scaled_low, 1, bf16, out_passed)
    out_middle, leaving, *backward = step(out_middle, leaving, *backward)
    out_got = across(out_middle, middle_bit)
    arriving = swap(leaving, "tensor", 2)
    inv_mine = lax.dynamic_slice_in_dim(inv_rms[0], share_at, share, 0)
    in_mine = to_relative(share_of(block_input[0]), data_at).astype(f32)
    cot_mine = to_relative(share_of(out_grad[0]), data_at).astype(f32) * live[0]
    z_both, x_both, bc_grad_part, dt_both, vector_terms, taps_bc_terms, head_terms = mixer_backward(
        common, scanned, *gradients, 1, backward
    )
    x_both, z_both, bc_grad_part, out_kept, arriving = step(
        x_both, z_both, bc_grad_part, out_kept, arriving
    )
    vector_terms = jnp.sum(vector_terms, axis=0)
    convx_slot, gated_slot = vector_terms[:4], vector_terms[4]
    convbc_part = jnp.sum(taps_bc_terms, axis=0)[:4]
    head_slot = jnp.concatenate(
        [
            jnp.sum(head_terms, axis=0)[:2, :head_count],
            jnp.sum(vector_terms[5].reshape(head_count, -1), axis=1)[None],
        ]
    )
    bc_kept, bc_leaving = kept_and_sent(bc_grad_part, tensor_at, 1, f32)
    bc_arriving = swap(bc_leaving, "tensor", 1)
    z_low = z_both.reshape(tokens, -1)
    x_low = x_both.reshape(tokens, -1)
    dt_low = dt_both.astype(bf16).reshape(tokens, -1)
    matrices = (low_z, low_x, low_dt)
    x_sent = gradient_rows(normed_flat, x_low, 3, bf16)
    x_low, z_low, x_sent, bc_arriving, out_got = step(x_low, z_low, x_sent, bc_arriving, out_got)

    x_passed = swap(x_sent, "dp", last_bit)
    bc_kept, bc_leaving = kept_and_sent(bc_kept + bc_arriving, tensor_at, 2, f32)
    bc_arriving = swap(bc_leaving, "tensor", 2)
    x_low, z_low, bc_leaving = step(x_low, z_low, bc_leaving)
    z_sent = gradient_rows(normed_flat, z_low, 3, bf16)
    both_sent = jnp.concatenate(
        [gradient_rows(normed_flat, values, 2, bf16) for values in (x_low, z_low)], axis=0
    )
    x_low, z_low, z_sent, both_sent, bc_arriving, arriving = step(
        x_low, z_low, z_sent, both_sent, bc_arriving, arriving
    )

    bc_kept = bc_kept + bc_arriving
    bc_far = swap(bc_kept[1], "dp", PAIR)
    shared = shared + arriving.astype(f32)
    shared_leaving = low_bits(shared[1])
    out_mine, out_leaving = middle_sum(gradient_rows(proj_later, scaled_low, 0, f32, out_kept), out_got)
    x_low, z_low, shared_leaving, out_mine, out_leaving = step(
        x_low, z_low, shared_leaving, out_mine, out_leaving
    )
    out_far = across(out_leaving, PAIR)
    projected_far = across(shared_leaving, PAIR)
    input_leaving = input_terms(1 - core, z_low, x_low, dt_low, *matrices)
    x_low, z_low, x_passed, input_leaving, bc_far, out_far, projected_far = step(
        x_low, z_low, x_passed, input_leaving, bc_far, out_far, projected_far
    )

    z_passed = swap(z_sent, "dp", last_bit)
    x_middle = gradient_rows(normed_flat, x_low, 1, bf16, x_passed)
    x_got = across(x_middle, middle_bit)
    input_arriving = swap(input_leaving, "tensor", 1)
    bc_low_mine = (bc_kept[0] + bc_far).astype(bf16)
    bc_far = swap(bc_low_mine, "tensor", 2)
    x_low, z_low, x_middle, bc_far = step(x_low, z_low, x_middle, bc_far)
    projected_mine = shared[0] + flip_pairs(projected_far.astype(f32))
    output = from_relative((in_mine + inv_mine[:, None] * projected_mine).astype(bf16), data_at)
    output_far = swap(output, "tensor", 2)
    input_kept = input_terms(core, z_low, x_low, dt_low, *matrices)
    out_share = join_halves(out_mine, out_far.astype(f32), half, 1)
    x_low, z_low, input_kept, z_passed, input_arriving, output_far, out_share = step(
        x_low, z_low, input_kept, z_passed, input_arriving, output_far, out_share
    )

    z_middle = gradient_rows(normed_flat, z_low, 1, bf16, z_passed)
    z_got = across(z_middle, middle_bit)
    both_kept = swap(both_sent, "dp", last_bit)
    bc_low = join_halves(bc_low_mine, bc_far, tensor_at // 2, 0)
    bc_far = swap(bc_low, "tensor", 1)
    x_low, z_low, z_middle, bc_low = step(x_low, z_low, z_middle, bc_low)
    input_kept, input_leaving = kept_and_sent(input_kept + input_arriving, tensor_at, 2, bf16)
    dt_part = tokens_out(dt_low, normed_flat)[:head_count]
    bc_far, dt_part, input_kept, input_leaving = step(bc_far, dt_part, input_kept, input_leaving)

    input_arriving = swap(input_leaving, "tensor", 2)
    bc_low = join_halves(bc_low, bc_far, core, 0)
    bc_columns = bc_low.shape[1] // 4
    bc_part = tokens_out(
        lax.dynamic_slice_in_dim(bc_low, tensor_at * bc_columns, bc_columns, 1), normed_low[0]
    )
    held = jnp.concatenate([bc_part, dt_part], axis=0)
    held = jnp.stack(
        [held[:, block * row_count : (block + 1) * row_count] for block in range(data_count)]
    )
    count = held.shape[0] // 2
    held = held[:count] + swap(held[count:], "dp", last_bit)
    output = join_halves(output, output_far, tensor_at // 2, 0)
    held, both_kept, x_got, output = step(held, both_kept, x_got, output)
    output_far = swap(output, "tensor", 1)
    for bit in reversed(dp_bits()[1:-1]):
        count = held.shape[0] // 2
        held = held[:count] + swap(held[count:], "dp", bit)
    x_terms = gradient_rows(normed_flat, x_low, 0, f32, both_kept[:part])
    z_terms = gradient_rows(normed_flat, z_low, 0, f32, both_kept[part:])
    x_mine, x_leaving = middle_sum(x_terms, x_got)
    input_mine = input_kept + input_arriving.astype(f32)
    input_leaving = low_bits(input_mine[1])
    z_terms, x_leaving, input_leaving = step(z_terms, x_leaving, input_leaving)

    input_far = swap(input_leaving, "dp", PAIR)
    output = join_halves(output, output_far, core, 0)
    small_far = swap(held[1], "dp", PAIR)
    z_mine, z_leaving = middle_sum(z_terms, z_got)
    z_leaving, small_far, input_far = step(z_leaving, small_far, input_far)
    both_far = across(jnp.concatenate([x_leaving, z_leaving], axis=0), PAIR)
    normed_grad = (
        input_mine[0] + flip_pairs(input_far.astype(f32)) + rows_times(bc_low_mine, low_bc)
    )

    _, norm_pull = jax.vjp(norm_input, in_mine, gain_rel)
    block_grad, gain_slot = norm_pull(normed_grad)
    input_grad = from_relative((cot_mine + block_grad).astype(bf16), data_at)
    both_far, gain_slot, output = step(both_far, gain_slot, output)
    x_share = join_halves(x_mine, both_far[: x_mine.shape[0]].astype(f32), half, 1)
    z_share = join_halves(z_mine, both_far[x_mine.shape[0] :].astype(f32), half, 1)

    bc_share = held[0, :bc_columns] + small_far[:bc_columns]
    dt_share = join_halves(held[0, bc_columns:], small_far[bc_columns:], half, 0).T
    bc_share = join_halves(bc_share, swap(bc_share, "tensor", 1), core, 0)
    bc_share = join_halves(bc_share, swap(bc_share, "tensor", 2), tensor_at // 2, 0).T

    def in_half(values):
        return join_halves(values, jnp.zeros_like(values), half, values.ndim - 1)

    def packed_sum(pieces, axis_bits):
        sizes = [piece.size for piece in pieces]
        flat = jnp.concatenate([piece.reshape(-1) for piece in pieces])
        fill = -flat.size % 128
        flat = jnp.pad(flat, (0, fill)).reshape(-1, 128)
        for axis, bits in axis_bits:
            flat = add_over(flat, axis, bits)
        flat = flat.reshape(-1)
        result, at = [], 0
        for piece, size in zip(pieces, sizes):
            result.append(flat[at : at + size].reshape(piece.shape))
            at += size
        return result

    norm_sum, convbc_sum = packed_sum(
        [from_relative(gain_slot, data_at), convbc_part], [("tensor", (1, 2))]
    )
    z_share, bc_share, norm_sum, convbc_sum = step(z_share, bc_share, norm_sum, convbc_sum)
    z_square = z_share * z_share + tiny_eps
    x_square = x_share * x_share + tiny_eps
    bc_square = bc_share * bc_share + tiny_eps
    dt_square = dt_share * dt_share + tiny_eps
    out_square = out_share * out_share + tiny_eps
    row_sums = jnp.stack(
        [
            jnp.sum(z_square, axis=1),
            jnp.sum(x_square, axis=1),
            jnp.sum(dt_square, axis=1),
            jnp.sum(out_square, axis=1),
        ]
    )
    z_row_sum, x_row_sum, dt_row_sum, out_row_sum = add_over(row_sums, "tensor", (1, 2))
    bc_row_sum = jnp.sum(bc_square, axis=1)

    (
        norm_total,
        convbc_total,
        gated_total,
        convx_total,
        head_total,
        z_col_sum,
        x_col_sum,
        bc_col_sum,
        dt_col_sum,
        out_col_sum,
    ) = packed_sum(
        [
            norm_sum,
            convbc_sum,
            in_half(gated_slot),
            in_half(convx_slot),
            in_half(head_slot),
            jnp.sum(z_square, axis=0),
            jnp.sum(x_square, axis=0),
            jnp.sum(bc_square, axis=0),
            jnp.sum(dt_square, axis=0),
            jnp.sum(out_square, axis=0),
        ],
        [("dp", dp_bits())],
    )
    z_rows_new = mix_state(z_rows, z_row_sum / INNER)
    x_rows_new = mix_state(x_rows, x_row_sum / INNER)
    bc_rows_new = mix_state(bc_rows, bc_row_sum / (2 * STATE))
    dt_rows_new = mix_state(dt_rows, dt_row_sum / HEADS)
    out_rows_new = mix_state(out_rows, out_row_sum / INNER)
    z_cols_new = mix_state(z_cols, z_col_sum / D)
    x_cols_new = mix_state(x_cols, x_col_sum / D)
    bc_cols_new = mix_state(bc_cols, bc_col_sum / D)
    dt_cols_new = mix_state(dt_cols, dt_col_sum / D)
    out_cols_new = mix_state(out_cols, out_col_sum / D)
    norm_second = mix_state(norm_gain_sq, norm_total * norm_total + tiny_eps)
    gated_second = mix_state(gated_gain_sq, gated_total * gated_total + tiny_eps)
    convx_second = mix_state(conv_x_sq, convx_total * convx_total + tiny_eps)
    convbc_second = mix_state(conv_bc_sq, convbc_total * convbc_total + tiny_eps)
    head_second = mix_state(head_sq, head_total * head_total + tiny_eps)
    norm_unit = norm_total * lax.rsqrt(norm_second)
    gated_unit = gated_total * lax.rsqrt(gated_second)
    convx_unit = convx_total * lax.rsqrt(convx_second)
    convbc_unit = convbc_total * lax.rsqrt(convbc_second)
    head_unit = head_total * lax.rsqrt(head_second)
    z_unit = z_share * lax.rsqrt(z_rows_new[:, None] * z_cols_new[None, :])
    x_unit = x_share * lax.rsqrt(x_rows_new[:, None] * x_cols_new[None, :])
    bc_unit = bc_share * lax.rsqrt(bc_rows_new[:, None] * bc_cols_new[None, :])
    dt_unit = dt_share * lax.rsqrt(dt_rows_new[:, None] * dt_cols_new[None, :])
    out_unit = out_share * lax.rsqrt(out_rows_new[:, None] * out_cols_new[None, :])
    tensor_count = lax.axis_size("tensor")
    unit_sums = jnp.stack(
        [
            jnp.sum(z_unit * z_unit),
            jnp.sum(x_unit * x_unit),
            jnp.sum(bc_unit * bc_unit) / tensor_count,
            jnp.sum(dt_unit * dt_unit),
            jnp.sum(out_unit * out_unit),
            jnp.sum(gated_unit * gated_unit) / data_count,
            jnp.sum(convx_unit * convx_unit) / data_count,
            jnp.sum(head_unit * head_unit) / data_count,
        ]
    )
    unit_sums = jnp.broadcast_to(unit_sums[:, None], (8, 128))
    unit_sums = add_over(unit_sums, "tensor", (1, 2))
    unit_sums, input_grad, output = step(unit_sums, input_grad, output)
    input_far = swap(input_grad, "tensor", 2)
    unit_sums = add_over(unit_sums, "dp", dp_bits())
    input_far, unit_sums = step(input_far, unit_sums)
    input_grad = join_halves(input_grad, input_far, tensor_at // 2, 0)
    input_grad = join_halves(input_grad, swap(input_grad, "tensor", 1), core, 0)
    (
        z_total,
        x_total,
        bc_total_sq,
        dt_total,
        out_total,
        gated_sq_total,
        convx_sq_total,
        head_sq_total,
    ) = unit_sums[:, 0]
    norm_sq_total = jnp.sum(norm_unit * norm_unit)
    convbc_sq_total = jnp.sum(convbc_unit * convbc_unit)
    in_rate = D ** (-0.5)
    out_rate = INNER ** (-0.5)
    z_upd = -in_rate * normalized(z_unit, z_total, D * INNER)
    x_upd = -in_rate * normalized(x_unit, x_total, D * INNER)
    bc_upd = -in_rate * normalized(bc_unit, bc_total_sq, D * 2 * STATE)
    dt_upd = -in_rate * normalized(dt_unit, dt_total, D * HEADS)
    out_upd = -out_rate * normalized(out_unit, out_total, D * INNER)
    norm_upd = -vector_rate * normalized(norm_unit, norm_sq_total, D)
    gated_upd = -vector_rate * normalized(gated_unit, gated_sq_total, INNER)
    convx_upd = -vector_rate * normalized(convx_unit, convx_sq_total, KCONV * INNER)
    convbc_upd = -vector_rate * normalized(convbc_unit, convbc_sq_total, KCONV * 2 * STATE)
    head_upd = -vector_rate * normalized(head_unit, head_sq_total, 3 * HEADS)
    return (
        output[None],
        input_grad[None],
        norm_total,
        norm_upd,
        norm_second,
        z_share,
        z_upd,
        z_rows_new,
        z_cols_new,
        x_share,
        x_upd,
        x_rows_new,
        x_cols_new,
        bc_share,
        bc_upd,
        bc_rows_new,
        bc_cols_new,
        dt_share,
        dt_upd,
        dt_rows_new,
        dt_cols_new,
        convx_total,
        convx_upd,
        convx_second,
        convbc_total,
        convbc_upd,
        convbc_second,
        head_total,
        head_upd,
        head_second,
        gated_total,
        gated_upd,
        gated_second,
        out_share,
        out_upd,
        out_rows_new,
        out_cols_new,
    )


def solution(mesh):
    in_specs = (
        P("dp", None, None),
        P("dp", None, None),
        P("dp", None),
        P("dp"),
        P(),
        P("dp", "tensor"),
        P("dp", "tensor"),
        P("dp", None),
        P("dp", "tensor"),
        P(None, "tensor"),
        P(),
        P(None, "tensor"),
        P("tensor"),
        P("dp", "tensor"),
        P(),
        P("dp"),
        P("tensor"),
        P("dp"),
        P("tensor"),
        P("dp"),
        P(),
        P("dp"),
        P("tensor"),
        P(None, "tensor"),
        P(),
        P(None, "tensor"),
        P("tensor"),
        P("dp"),
        P("tensor"),
    )
    out_specs = (
        P("dp", None, None),
        P("dp", None, None),
        P(),
        P(),
        P(),
        P("dp", "tensor"),
        P("dp", "tensor"),
        P("dp"),
        P("tensor"),
        P("dp", "tensor"),
        P("dp", "tensor"),
        P("dp"),
        P("tensor"),
        P("dp", None),
        P("dp", None),
        P("dp"),
        P(),
        P("dp", "tensor"),
        P("dp", "tensor"),
        P("dp"),
        P("tensor"),
        P(None, "tensor"),
        P(None, "tensor"),
        P(None, "tensor"),
        P(),
        P(),
        P(),
        P(None, "tensor"),
        P(None, "tensor"),
        P(None, "tensor"),
        P("tensor"),
        P("tensor"),
        P("tensor"),
        P("dp", "tensor"),
        P("dp", "tensor"),
        P("dp"),
        P("tensor"),
    )
    return jax.shard_map(shards, mesh=mesh, in_specs=in_specs, out_specs=out_specs, check_vma=False)
```
